32 devices in a mesh: dp: 8 (over z, core), tensor: 4 (over y, x).
Axes of the slice: x: 2, y: 2, z: 4, core: 2. Of those that a mesh axis runs over, the one named last changes fastest.
Arguments:
- tokens: bfloat16 [8192, 2048], P(('dp', 'tensor')), may hold values from -6 to 6
- positions: int32 [8192], P('dp'), may hold values from 0 to 4095, as said below
- input_gain: float32 [2048], replicated, may hold values from 0.25 to 1.75
- middle_gain: float32 [2048], replicated, may hold values from 0.25 to 1.75
- query_gain: float32 [128], replicated, may hold values from 0.25 to 1.75
- key_gain: float32 [128], replicated, may hold values from 0.25 to 1.75
- query_weight: bfloat16 [2048, 2048], P('dp', 'tensor'), may hold values from -0.125 to 0.125
- key_matrix: bfloat16 [2048, 1024], P('dp', 'tensor'), may hold values from -0.125 to 0.125
- value_matrix: bfloat16 [2048, 1024], P('dp', 'tensor'), may hold values from -0.125 to 0.125
- output_weight: bfloat16 [2048, 2048], P('dp', 'tensor'), may hold values from -2 to 2
- gate_weight: bfloat16 [2048, 6144], P('dp', 'tensor'), may hold values from -0.125 to 0.125
- up_weight: bfloat16 [2048, 6144], P('dp', 'tensor'), may hold values from -0.125 to 0.125
- down_weight: bfloat16 [2048, 6144], P('dp', 'tensor'), may hold values from -0.078125 to 0.078125
- layer_cotangent: bfloat16 [8192, 2048], P(('dp', 'tensor')), may hold values from -6 to 6
Outputs:
- layer_output: float32 [8192, 2048], P(('dp', 'tensor'))
- tokens_grad: float32 [8192, 2048], P(('dp', 'tensor'))
- input_gain_grad: float32 [2048], replicated
- middle_gain_grad: float32 [2048], replicated
- query_gain_grad: float32 [128], replicated
- key_gain_grad: float32 [128], replicated
- query_weight_grad: float32 [2048, 2048], P('dp', 'tensor')
- key_weight_grad: float32 [2048, 1024], P('dp', 'tensor')
- value_weight_grad: float32 [2048, 1024], P('dp', 'tensor')
- output_weight_grad: float32 [2048, 2048], P('dp', 'tensor')
- gate_weight_grad: float32 [2048, 6144], P('dp', 'tensor')
- up_weight_grad: float32 [2048, 6144], P('dp', 'tensor')
- down_weight_grad: float32 [2048, 6144], P('dp', 'tensor')
The draws below stay inside these ranges and needn't reach their ends.
Inputs may be any that keep to these rules, and one draw needn't show every extreme that they name: Within each sequence of 1024 tokens the positions rise from token to token by 1 to 4; some sequence starts at 0 and some sequence ends at 4095.
All inputs are finite; a program needn't handle non-finite values.
Results may differ from the reference program's by a relative error of at most 0.024.
Values may be sent and summed in bfloat16 or wider, within the bound.
No kernel may reach another device: no remote copies, remote signals or barrier semaphores. Data moves between devices by JAX's collectives and lax.ppermute only.
A program may use at most 192 MiB of HBM per device.

```python
import math
import jax
import jax.numpy as jnp
from jax import lax

MODEL_WIDTH = 2048
QUERY_HEADS = 16
KV_HEAD_COUNT = 8
HEAD_WIDTH = 128
FF = 6144
SEQUENCE_LENGTH = 1024
SEQUENCE_COUNT = 1
TOKEN_COUNT = 1024
TOKENS = 8192
N_DP = 8


def draw_positions(key, part):
    sequence_total = TOKENS // SEQUENCE_LENGTH
    largest_step = max(1, 4096 // SEQUENCE_LENGTH)
    step_key, start_key = jax.random.split(key)
    increments = jax.random.randint(step_key, (sequence_total, SEQUENCE_LENGTH), 1, largest_step + 1)
    offsets = jnp.cumsum(increments, axis=1) - increments[:, :1]
    last_offset = offsets[:, -1]
    starts = jax.random.randint(start_key, (sequence_total,), 0, 4096 - last_offset)
    sequence_index = jnp.arange(sequence_total, dtype=jnp.int32)
    starts = jnp.where(sequence_index == 0, 4095 - last_offset, starts)
    starts = jnp.where(sequence_index == 1, 0, starts)
    return (starts[:, None] + offsets).reshape(TOKENS).astype(jnp.int32)


def steps_of(key, dims, shards, least, largest):
    def one(position, blocks):
        steps = jax.random.uniform(jax.random.fold_in(jax.random.fold_in(key, 6), position), (blocks,), jnp.float32, least / len(shards), largest / len(shards))
        return jnp.repeat(jnp.exp(steps), dims[position] // blocks).reshape((-1,) + (1,) * (len(dims) - position - 1))

    loudness = one(*shards[0])
    for cut in shards[1:]:
        loudness = loudness * one(*cut)
    return loudness


def gaussian(key, extent, spread, limit, shards=(), kind=jnp.bfloat16):
    drawn = jax.random.normal(key, extent, jnp.float32) * spread
    if len(shards) > 0:
        drawn = steps_of(key, extent, shards, -0.22, 0.18) * drawn
    return jnp.clip(drawn, min=-limit, max=limit).astype(kind)


def setup_inputs(seed: int = 0) -> dict:
    seeds = jax.random.split(jax.random.key(seed), 15)
    return {
        "tokens": gaussian(seeds[0], (TOKENS, MODEL_WIDTH), 1.0, 6.0, ((0, 32),)),
        "positions": draw_positions(jax.random.fold_in(seeds[14], 71), 0),
        "input_gain": jnp.clip(1.0 + 0.15 * jax.random.normal(seeds[2], (MODEL_WIDTH,), jnp.float32), 0.25, 1.75),
        "middle_gain": jnp.clip(1.0 + 0.15 * jax.random.normal(seeds[3], (MODEL_WIDTH,), jnp.float32), 0.25, 1.75),
        "query_gain": jnp.clip(1.0 + 0.15 * jax.random.normal(seeds[4], (HEAD_WIDTH,), jnp.float32), 0.25, 1.75),
        "key_gain": jnp.clip(1.0 + 0.15 * jax.random.normal(seeds[5], (HEAD_WIDTH,), jnp.float32), 0.25, 1.75),
        "query_weight": gaussian(seeds[6], (MODEL_WIDTH, QUERY_HEADS * HEAD_WIDTH), MODEL_WIDTH ** -0.5, 0.125, ((0, 8), (1, 4))),
        "key_matrix": gaussian(seeds[7], (MODEL_WIDTH, KV_HEAD_COUNT * HEAD_WIDTH), MODEL_WIDTH ** -0.5, 0.125, ((0, 8), (1, 4))),
        "value_matrix": gaussian(seeds[8], (MODEL_WIDTH, KV_HEAD_COUNT * HEAD_WIDTH), MODEL_WIDTH ** -0.5, 0.125, ((0, 8), (1, 4))),
        "output_weight": gaussian(seeds[9], (MODEL_WIDTH, QUERY_HEADS * HEAD_WIDTH), (max(QUERY_HEADS * HEAD_WIDTH * 4 // SEQUENCE_LENGTH, 1)) ** -0.5, 2.0, ((0, 8), (1, 4))),
        "gate_weight": gaussian(seeds[10], (MODEL_WIDTH, FF), MODEL_WIDTH ** -0.5, 0.125, ((0, 8), (1, 4))),
        "up_weight": gaussian(seeds[11], (MODEL_WIDTH, FF), MODEL_WIDTH ** -0.5, 0.125, ((0, 8), (1, 4))),
        "down_weight": gaussian(seeds[12], (MODEL_WIDTH, FF), FF ** -0.5, 0.078125, ((0, 8), (1, 4))),
        "layer_cotangent": gaussian(seeds[13], (TOKENS, MODEL_WIDTH), 1.0, 6.0, ((0, 32),)),
    }


epsilon = 1e-06
highest = lax.Precision.HIGHEST
masked = -1e+30

@jax.custom_vjp
def reduced_value(v):
    return lax.optimization_barrier(v.astype(jnp.bfloat16)).astype(jnp.float32)

@jax.custom_vjp
def reduced_restore(v):
    return v

def low_keep(v):
    return (reduced_value(v), None)

def low_pass(kept, grad):
    return (grad,)

def back_keep(v):
    return (v, None)

def back_low(kept, grad):
    return (reduced_value(grad),)
reduced_value.defvjp(low_keep, low_pass)
reduced_restore.defvjp(back_keep, back_low)

def product_result(left, right):
    return jnp.dot(left, right, precision=highest)

def normalize(value_rows, gain):
    return value_rows * lax.rsqrt(lax.optimization_barrier(jnp.mean(value_rows * value_rows, axis=-1, keepdims=True)) + epsilon) * gain

def rotate(value_rows):
    halfway = value_rows.shape[-1] // 2
    return jnp.concatenate([-value_rows[..., halfway:], value_rows[..., :halfway]], axis=-1)

def tables(positions, width):
    frequency = jnp.exp(jnp.arange(width // 2, dtype=jnp.float32) * (-2.0 * math.log(1000000.0) / width))
    angles = positions.astype(jnp.float32)[:, None] * frequency[None, :]
    cosine = jnp.cos(angles)
    sine_table = jnp.sin(angles)
    return (jnp.concatenate([cosine, cosine], axis=-1)[:, None, :], jnp.concatenate([sine_table, sine_table], axis=-1)[:, None, :])

def attend_heads(operands):
    query_rows, key_rows, value_rows = operands
    grouped_heads = query_rows.reshape(SEQUENCE_LENGTH, KV_HEAD_COUNT, QUERY_HEADS // KV_HEAD_COUNT, HEAD_WIDTH)
    scores = jnp.einsum('qhgd,khd->hgqk', grouped_heads, key_rows, precision=highest) * HEAD_WIDTH ** (-0.5)
    scores = reduced_restore(scores)
    row_index = lax.broadcasted_iota(jnp.int32, (SEQUENCE_LENGTH, SEQUENCE_LENGTH), 0)
    column_index = lax.broadcasted_iota(jnp.int32, (SEQUENCE_LENGTH, SEQUENCE_LENGTH), 1)
    scores = jnp.where(column_index <= row_index, scores, masked)
    shares = reduced_value(jax.nn.softmax(scores, axis=-1))
    attended_rows = jnp.einsum('hgqk,khd->qhgd', shares, value_rows, precision=highest)
    return reduced_value(reduced_restore(attended_rows)).reshape(SEQUENCE_LENGTH, QUERY_HEADS * HEAD_WIDTH)

def decoder(inputs, input_gain, middle_gain, query_gain, key_gain, query_weight, key_matrix, value_matrix, output_weight, gate_weight, up_weight, down_weight, cosine, sine_table):
    normed_rows = reduced_value(normalize(inputs, input_gain))
    query_raw = reduced_restore(product_result(normed_rows, query_weight)).reshape(TOKEN_COUNT, QUERY_HEADS, HEAD_WIDTH)
    raw_key_rows = reduced_restore(product_result(normed_rows, key_matrix)).reshape(TOKEN_COUNT, KV_HEAD_COUNT, HEAD_WIDTH)
    value_rows = reduced_value(reduced_restore(product_result(normed_rows, value_matrix))).reshape(TOKEN_COUNT, KV_HEAD_COUNT, HEAD_WIDTH)
    query_normed = normalize(query_raw, query_gain)
    query_rows = reduced_value(query_normed * cosine + rotate(query_normed) * sine_table)
    key_normed = normalize(raw_key_rows, key_gain)
    key_rows = reduced_value(key_normed * cosine + rotate(key_normed) * sine_table)
    attended_rows = lax.map(jax.checkpoint(attend_heads), (query_rows.reshape(SEQUENCE_COUNT, SEQUENCE_LENGTH, QUERY_HEADS, HEAD_WIDTH), key_rows.reshape(SEQUENCE_COUNT, SEQUENCE_LENGTH, KV_HEAD_COUNT, HEAD_WIDTH), value_rows.reshape(SEQUENCE_COUNT, SEQUENCE_LENGTH, KV_HEAD_COUNT, HEAD_WIDTH)))
    attended_rows = attended_rows.reshape(TOKEN_COUNT, QUERY_HEADS * HEAD_WIDTH)
    branch = reduced_restore(product_result(attended_rows, output_weight.T))
    middle = inputs + branch
    normed_middle = reduced_value(normalize(middle, middle_gain))
    gating = reduced_restore(product_result(normed_middle, gate_weight))
    upward = reduced_restore(product_result(normed_middle, up_weight))
    active = reduced_value(jax.nn.silu(gating) * upward)
    return middle + product_result(active, down_weight.T)

def reference(tokens, positions, input_gain, middle_gain, query_gain, key_gain, query_weight, key_matrix, value_matrix, output_weight, gate_weight, up_weight, down_weight, layer_cotangent):
    weights = tuple((weight.astype(jnp.float32) for weight in (input_gain, middle_gain, query_gain, key_gain, query_weight, key_matrix, value_matrix, output_weight, gate_weight, up_weight, down_weight)))
    group_inputs = tokens.astype(jnp.float32).reshape(N_DP, TOKEN_COUNT, MODEL_WIDTH)
    group_places = positions.reshape(N_DP, TOKEN_COUNT)
    group_cotangent = layer_cotangent.astype(jnp.float32).reshape(N_DP, TOKEN_COUNT, MODEL_WIDTH)

    def advance(totals, operands):
        inputs, places, cotangent = operands
        cosine, sine_table = tables(places, HEAD_WIDTH)

        def forward(layer_in, *params):
            return decoder(layer_in, *params, cosine, sine_table)
        output, pullback = jax.vjp(forward, inputs, *weights)
        gradients = pullback(cotangent)
        totals = tuple((summed + gradient for summed, gradient in zip(totals, gradients[1:])))
        return (totals, (output, gradients[0]))
    initial = tuple((jnp.zeros_like(weight) for weight in weights))
    totals, (outputs, input_grads) = lax.scan(advance, initial, (group_inputs, group_places, group_cotangent))
    return (outputs.reshape(TOKENS, MODEL_WIDTH), input_grads.reshape(TOKENS, MODEL_WIDTH), totals[0], totals[1], totals[2], totals[3], totals[4], totals[5], totals[6], totals[7], totals[8], totals[9], totals[10])
```

```python
import math

import jax
import jax.numpy as jnp
from jax import lax
from jax.experimental import pallas as pl
from jax.experimental.pallas import tpu as pltpu
from jax.sharding import PartitionSpec as P

SEQUENCE_LENGTH = 1024


epsilon = 1e-06
masked = -1e30


def matmul(left, right):
    return jnp.dot(left, right, preferred_element_type=jnp.float32)


def contract_first(left, right):
    return lax.dot_general(
        left, right, (((0,), (0,)), ((), ())), preferred_element_type=jnp.float32
    )


def contract_last(left, right):
    return lax.dot_general(
        left, right, (((1,), (1,)), ((), ())), preferred_element_type=jnp.float32
    )


def tables(positions, width):
    frequency = jnp.exp(
        jnp.arange(width // 2, dtype=jnp.float32) * (-2.0 * math.log(1000000.0) / width)
    )
    angles = positions.astype(jnp.float32)[:, None] * frequency[None, :]
    cosine = jnp.cos(angles)
    sine = jnp.sin(angles)
    return (
        jnp.concatenate([cosine, cosine], axis=-1),
        jnp.concatenate([-sine, sine], axis=-1),
    )


def inverse_rms(value_rows):
    return lax.rsqrt(jnp.mean(value_rows * value_rows, axis=-1, keepdims=True) + epsilon)


def norm_backward(upstream, scaled, inverse, gain):
    inner = upstream * gain
    return inverse * (inner - scaled * jnp.mean(inner * scaled, axis=-1, keepdims=True))


class Links:
    def __init__(self, dp_size, tensor_size):
        self.dp_size = dp_size
        self.tensor_size = tensor_size

    def across(self, value, bit):
        return lax.ppermute(
            value, "tensor", [(place, place ^ bit) for place in range(self.tensor_size)]
        )

    def relative_tokens(self, values):
        count = values.shape[0] // self.tensor_size
        place = lax.axis_index("tensor")
        return jnp.concatenate(
            [
                lax.dynamic_slice_in_dim(values, (place ^ other) * count, count, 0)
                for other in range(self.tensor_size)
            ],
            axis=0,
        )

    def gather_tokens(self, block):
        if self.tensor_size != 4:
            bit = 1
            while bit < self.tensor_size:
                block = jnp.concatenate([block, self.across(block, bit)], axis=0)
                bit *= 2
            return block
        half = block.shape[0] // 2
        by_x = self.across(block, 1)
        by_y = self.across(block, 2)
        corner_low = self.across(by_y[:half], 1)
        corner_high = self.across(by_x[half:], 2)
        return jnp.concatenate([block, by_x, by_y, corner_low, corner_high], axis=0)

    def scatter_tokens(self, partial):
        if self.tensor_size != 4:
            bit = self.tensor_size // 2
            while bit:
                middle = partial.shape[0] // 2
                arrived = self.across(partial[middle:], bit).astype(jnp.float32)
                total = partial[:middle].astype(jnp.float32) + arrived
                partial = total.astype(partial.dtype)
                bit //= 2
            return total
        count = partial.shape[0] // self.tensor_size
        half = count // 2

        def piece(block, high):
            start = block * count + high * half
            return partial[start : start + half]

        wide = jnp.float32
        low_own = self.across(piece(1, 0), 1)
        low_pass = self.across(piece(3, 0), 1)
        high_own = self.across(piece(2, 1), 2)
        high_pass = self.across(piece(3, 1), 2)
        low_last = self.across(
            (piece(2, 0).astype(wide) + low_pass.astype(wide)).astype(partial.dtype), 2
        )
        high_last = self.across(
            (piece(1, 1).astype(wide) + high_pass.astype(wide)).astype(partial.dtype), 1
        )
        low = piece(0, 0).astype(wide) + low_own.astype(wide) + low_last.astype(wide)
        high = piece(0, 1).astype(wide) + high_own.astype(wide) + high_last.astype(wide)
        return jnp.concatenate([low, high], axis=0)

    def gather_weight(self, shard):
        return lax.all_gather(shard, "dp", axis=0, tiled=True)

    def scatter_weight(self, partial):
        return lax.psum_scatter(partial, "dp", scatter_dimension=0, tiled=True)

    def total(self, value):
        bit = 1
        while bit < self.tensor_size:
            value = value + self.across(value, bit)
            bit *= 2
        bit = 1
        while bit < self.dp_size:
            value = value + lax.ppermute(
                value, "dp", [(place, place ^ bit) for place in range(self.dp_size)]
            )
            bit *= 2
        return value


def product(left, right, left_axis, right_axis):
    return lax.dot_general(
        left,
        right,
        (((left_axis,), (right_axis,)), ((), ())),
        preferred_element_type=jnp.float32,
    )


class Attention:
    def __init__(self, rows, head_size, query_heads, key_heads, blocks):
        self.rows = rows
        self.head_size = head_size
        self.query_heads = query_heads
        self.key_heads = key_heads
        self.grouping = query_heads // key_heads
        self.blocks = blocks
        self.block = rows // blocks
        self.scale = head_size ** (-0.5)

    def outside(self, place, index):
        return pl.ds(pl.multiple_of((index ^ place) * self.block, self.block), self.block)

    def inside(self, index):
        return slice(index * self.block, (index + 1) * self.block)

    def head(self, index):
        return slice(index * self.head_size, (index + 1) * self.head_size)

    def turn(self, rows):
        return pltpu.roll(rows, self.head_size // 2, axis=1)

    def forward_kernel(
        self, place_ref, raw_query, raw_key, raw_value, cosine, sine, query_gain, key_gain,
        query, key, value, attended, totals,
    ):
        place = place_ref[0]

        def prepared(raw, gain, where):
            normed = raw * inverse_rms(raw) * gain
            turned = normed * cosine[where, :] + self.turn(normed) * sine[where, :]
            return turned.astype(jnp.bfloat16)

        for index in range(self.blocks):
            there, here = self.outside(place, index), self.inside(index)
            key[here, :] = prepared(raw_key[there, :], key_gain[...], there)
            value[here, :] = raw_value[there, :].astype(jnp.bfloat16)
            for member in range(self.grouping):
                query[here, self.head(member)] = prepared(
                    raw_query[there, self.head(member)], query_gain[...], there
                )
        for member in range(self.grouping):
            for index in range(self.blocks):
                span = (index + 1) * self.block
                scores = self.scale * product(
                    query[self.inside(index), self.head(member)], key[:span, :], 1, 1
                )
                row = index * self.block + lax.broadcasted_iota(jnp.int32, scores.shape, 0)
                column = lax.broadcasted_iota(jnp.int32, scores.shape, 1)
                scores = jnp.where(column <= row, scores, masked)
                highest = jnp.max(scores, axis=1, keepdims=True)
                powers = jnp.exp(scores - highest)
                total = jnp.sum(powers, axis=1, keepdims=True)
                shares = (powers * (1.0 / total)).astype(jnp.bfloat16)
                attended[self.outside(place, index), self.head(member)] = product(
                    shares, value[:span, :], 1, 0
                ).astype(jnp.bfloat16)
                log_total = jnp.broadcast_to(
                    highest + jnp.log(total), (self.block, self.head_size)
                )
                totals[0, member : member + 1, self.inside(index)] = log_total.T[:1, :]

    def forward(self, place, raw, cosine, sine, query_gain, key_gain):
        rows, size, group = self.rows, self.head_size, self.grouping
        wide = group * size
        first_key, first_value = self.query_heads, self.query_heads + self.key_heads
        whole = lambda h, p: (0, 0)
        by_head = lambda h, p: (0, h)
        low = jnp.bfloat16
        return pl.pallas_call(
            self.forward_kernel,
            name="attention_forward",
            grid_spec=pltpu.PrefetchScalarGridSpec(
                num_scalar_prefetch=1,
                grid=(self.key_heads,),
                in_specs=[
                    pl.BlockSpec((rows, wide), by_head),
                    pl.BlockSpec((rows, size), lambda h, p: (0, first_key + h)),
                    pl.BlockSpec((rows, size), lambda h, p: (0, first_value + h)),
                    pl.BlockSpec((rows, size), whole),
                    pl.BlockSpec((rows, size), whole),
                    pl.BlockSpec((1, size), whole),
                    pl.BlockSpec((1, size), whole),
                ],
                out_specs=[
                    pl.BlockSpec((rows, wide), by_head),
                    pl.BlockSpec((rows, size), by_head),
                    pl.BlockSpec((rows, size), by_head),
                    pl.BlockSpec((rows, wide), by_head),
                    pl.BlockSpec((1, group, rows), lambda h, p: (h, 0, 0)),
                ],
            ),
            out_shape=[
                jax.ShapeDtypeStruct((rows, self.query_heads * size), low),
                jax.ShapeDtypeStruct((rows, self.key_heads * size), low),
                jax.ShapeDtypeStruct((rows, self.key_heads * size), low),
                jax.ShapeDtypeStruct((rows, self.query_heads * size), low),
                jax.ShapeDtypeStruct((self.key_heads, group, rows), jnp.float32),
            ],
        )(place, raw, raw, raw, cosine, sine, query_gain[None, :], key_gain[None, :])

    def backward_kernel(
        self, place_ref, raw_query, raw_key, cosine, sine, query_gain, key_gain,
        query, key, value, totals, upstream,
        raw_grad, query_gain_grad, key_gain_grad, key_total, value_total,
    ):
        place = place_ref[0]
        current = pl.program_id(0)
        size, group = self.head_size, self.grouping

        @pl.when(current == 0)
        def _():
            query_gain_grad[...] = jnp.zeros_like(query_gain_grad)
            key_gain_grad[...] = jnp.zeros_like(key_gain_grad)

        def store(where, head, grad):
            column = pl.multiple_of(head * size, size)
            raw_grad[where, pl.ds(column, size)] = grad.astype(jnp.bfloat16)

        def through_norm(raw, grad, gain, where, gain_grad):
            inverse = inverse_rms(raw)
            scaled = raw * inverse
            normed_grad = grad * cosine[where, :] - self.turn(grad) * sine[where, :]
            gain_grad[...] += jnp.sum(normed_grad * scaled, axis=0, keepdims=True)
            return norm_backward(normed_grad, scaled, inverse, gain)

        for member in range(group):
            for index in reversed(range(self.blocks)):
                here, there = self.inside(index), self.outside(place, index)
                span = (index + 1) * self.block
                query_block = query[here, self.head(member)]
                grad_block = upstream[there, self.head(member)]
                scores = self.scale * product(key[:span, :], query_block, 1, 1)
                row = index * self.block + lax.broadcasted_iota(jnp.int32, scores.shape, 1)
                column = lax.broadcasted_iota(jnp.int32, scores.shape, 0)
                scores = jnp.where(column <= row, scores, masked)
                shares = jnp.exp(scores - totals[0, member : member + 1, here])
                share_grad = product(value[:span, :], grad_block, 1, 1)
                inner = jnp.sum(share_grad * shares, axis=0, keepdims=True)
                score_grad = (shares * (share_grad - inner)).astype(jnp.bfloat16)
                value_part = product(shares.astype(jnp.bfloat16), grad_block, 1, 0)
                key_part = product(score_grad, query_block, 1, 0)
                if member == 0 and index == self.blocks - 1:
                    value_total[...] = value_part
                    key_total[...] = key_part
                else:
                    value_total[:span, :] += value_part
                    key_total[:span, :] += key_part
                query_grad = self.scale * product(score_grad, key[:span, :], 0, 0)
                store(
                    there,
                    current * group + member,
                    through_norm(
                        raw_query[there, self.head(member)],
                        query_grad,
                        query_gain[...],
                        there,
                        query_gain_grad,
                    ),
                )
        for index in range(self.blocks):
            here, there = self.inside(index), self.outside(place, index)
            store(
                there,
                self.query_heads + current,
                through_norm(
                    raw_key[there, :],
                    self.scale * key_total[here, :],
                    key_gain[...],
                    there,
                    key_gain_grad,
                ),
            )
            store(there, self.query_heads + self.key_heads + current, value_total[here, :])

    def backward(
        self, place, raw, cosine, sine, query_gain, key_gain, query, key, value, totals, upstream
    ):
        rows, size, group = self.rows, self.head_size, self.grouping
        wide = group * size
        first_key = self.query_heads
        whole = lambda h, p: (0, 0)
        by_head = lambda h, p: (0, h)
        columns = (self.query_heads + 2 * self.key_heads) * size
        return pl.pallas_call(
            self.backward_kernel,
            name="attention_backward",
            grid_spec=pltpu.PrefetchScalarGridSpec(
                num_scalar_prefetch=1,
                grid=(self.key_heads,),
                in_specs=[
                    pl.BlockSpec((rows, wide), by_head),
                    pl.BlockSpec((rows, size), lambda h, p: (0, first_key + h)),
                    pl.BlockSpec((rows, size), whole),
                    pl.BlockSpec((rows, size), whole),
                    pl.BlockSpec((1, size), whole),
                    pl.BlockSpec((1, size), whole),
                    pl.BlockSpec((rows, wide), by_head),
                    pl.BlockSpec((rows, size), by_head),
                    pl.BlockSpec((rows, size), by_head),
                    pl.BlockSpec((1, group, rows), lambda h, p: (h, 0, 0)),
                    pl.BlockSpec((rows, wide), by_head),
                ],
                out_specs=[
                    pl.BlockSpec((rows, columns), whole),
                    pl.BlockSpec((1, size), whole),
                    pl.BlockSpec((1, size), whole),
                ],
                scratch_shapes=[
                    pltpu.VMEM((rows, size), jnp.float32),
                    pltpu.VMEM((rows, size), jnp.float32),
                ],
            ),
            out_shape=[
                jax.ShapeDtypeStruct((rows, columns), jnp.bfloat16),
                jax.ShapeDtypeStruct((1, size), jnp.float32),
                jax.ShapeDtypeStruct((1, size), jnp.float32),
            ],
        )(
            place, raw, raw, cosine, sine, query_gain[None, :], key_gain[None, :],
            query, key, value, totals, upstream,
        )


def shards(
    links,
    tokens,
    positions,
    input_gain,
    middle_gain,
    query_gain,
    key_gain,
    query_weight,
    key_matrix,
    value_matrix,
    output_weight,
    gate_weight,
    up_weight,
    down_weight,
    layer_cotangent,
):
    head_size = query_gain.shape[0]
    query_heads = query_weight.shape[1] // head_size
    key_heads = key_matrix.shape[1] // head_size
    query_width = query_heads * head_size
    key_width = key_heads * head_size
    group_rows = positions.shape[0]
    assert group_rows == SEQUENCE_LENGTH
    attention = Attention(group_rows, head_size, query_heads, key_heads, links.tensor_size)
    place = lax.axis_index("tensor").astype(jnp.int32)[None]
    hidden = gate_weight.shape[1]
    wide_attention = links.gather_weight(
        jnp.concatenate([query_weight, key_matrix, value_matrix], axis=1)
    )
    wide_output = links.gather_weight(output_weight)
    wide_feed = links.gather_weight(jnp.concatenate([gate_weight, up_weight], axis=1))
    wide_down = links.gather_weight(down_weight)

    positions = links.relative_tokens(positions)
    inputs = tokens.astype(jnp.float32)
    inverse_in = inverse_rms(inputs)
    scaled_in = inputs * inverse_in
    normed_rows = links.gather_tokens((scaled_in * input_gain).astype(jnp.bfloat16))
    own_cotangent, normed_rows = lax.optimization_barrier((layer_cotangent, normed_rows))
    cotangent = links.gather_tokens(own_cotangent)

    cosine, sine = tables(positions, head_size)
    raw_rows = matmul(normed_rows, wide_attention)
    query_rows, key_rows, value_rows, attended_rows, log_totals = attention.forward(
        place, raw_rows, cosine, sine, query_gain, key_gain
    )
    branch = links.scatter_tokens(contract_last(attended_rows, wide_output).astype(jnp.bfloat16))
    middle = inputs + branch
    inverse_mid = inverse_rms(middle)
    scaled_mid = middle * inverse_mid
    normed_middle = links.gather_tokens((scaled_mid * middle_gain).astype(jnp.bfloat16))
    feed = matmul(normed_middle, wide_feed)
    gating, upward = feed[:, :hidden], feed[:, hidden:]
    gate_sigmoid = jax.nn.sigmoid(gating)
    silu_gate = gating * gate_sigmoid
    active = (silu_gate * upward).astype(jnp.bfloat16)
    down_term = contract_first(cotangent, active).astype(jnp.bfloat16)
    active, down_term = lax.optimization_barrier((active, down_term))
    down_sum = links.scatter_weight(down_term)
    cotangent, down_term = lax.optimization_barrier((cotangent, down_term))
    active_grad = matmul(cotangent, wide_down)
    gate_grad = (
        active_grad * upward * gate_sigmoid * (1.0 + gating * (1.0 - gate_sigmoid))
    ).astype(jnp.bfloat16)
    upward_grad = (active_grad * silu_gate).astype(jnp.bfloat16)
    feed_grad = jnp.concatenate([gate_grad, upward_grad], axis=1)
    middle_partial = contract_last(feed_grad, wide_feed)
    middle_normed_grad = links.scatter_tokens(middle_partial.astype(jnp.bfloat16))
    feed_term = contract_first(normed_middle, feed_grad).astype(jnp.bfloat16)
    feed_term, down_sum = lax.optimization_barrier((feed_term, down_sum))
    feed_sum = links.scatter_weight(feed_term)
    layer_output = middle + links.scatter_tokens(
        contract_last(active, wide_down).astype(jnp.bfloat16)
    )
    middle_gain_term = jnp.sum(middle_normed_grad * scaled_mid, axis=0)
    middle_grad = own_cotangent.astype(jnp.float32) + norm_backward(
        middle_normed_grad, scaled_mid, inverse_mid, middle_gain
    )
    low_middle_grad, feed_term = lax.optimization_barrier(
        (middle_grad.astype(jnp.bfloat16), feed_term)
    )
    branch_grad = links.gather_tokens(low_middle_grad)
    output_term = contract_first(branch_grad, attended_rows).astype(jnp.bfloat16)
    output_term, feed_sum = lax.optimization_barrier((output_term, feed_sum))
    output_sum = links.scatter_weight(output_term)
    branch_grad, output_term = lax.optimization_barrier((branch_grad, output_term))
    attended_grad = matmul(branch_grad, wide_output).astype(jnp.bfloat16)
    raw_grad, query_gain_term, key_gain_term = attention.backward(
        place,
        raw_rows,
        cosine,
        sine,
        query_gain,
        key_gain,
        query_rows,
        key_rows,
        value_rows,
        log_totals,
        attended_grad,
    )
    input_normed_grad = links.scatter_tokens(
        contract_last(raw_grad, wide_attention).astype(jnp.bfloat16)
    )
    attention_sum = links.scatter_weight(contract_first(normed_rows, raw_grad).astype(jnp.bfloat16))
    input_gain_term = jnp.sum(input_normed_grad * scaled_in, axis=0)
    tokens_grad = middle_grad + norm_backward(input_normed_grad, scaled_in, inverse_in, input_gain)
    other_terms = links.total(
        jnp.concatenate([middle_gain_term, query_gain_term[0], key_gain_term[0]])
    )
    width = tokens.shape[1]
    attention_sum, output_sum, feed_sum, down_sum = (
        summed.astype(jnp.float32) for summed in (attention_sum, output_sum, feed_sum, down_sum)
    )
    return (
        layer_output,
        tokens_grad,
        links.total(input_gain_term),
        other_terms[:width],
        other_terms[width : width + head_size],
        other_terms[width + head_size :],
        attention_sum[:, :query_width],
        attention_sum[:, query_width : query_width + key_width],
        attention_sum[:, query_width + key_width :],
        output_sum,
        feed_sum[:, :hidden],
        feed_sum[:, hidden:],
        down_sum,
    )


def solution(mesh):
    links = Links(mesh.shape["dp"], mesh.shape["tensor"])
    placed = (
        P(("dp", "tensor"), None),
        P("dp"),
        P(),
        P(),
        P(),
        P(),
        P("dp", "tensor"),
        P("dp", "tensor"),
        P("dp", "tensor"),
        P("dp", "tensor"),
        P("dp", "tensor"),
        P("dp", "tensor"),
        P("dp", "tensor"),
        P(("dp", "tensor"), None),
    )
    return jax.shard_map(
        lambda *arrays: shards(links, *arrays),
        mesh=mesh,
        in_specs=placed,
        out_specs=(
            P(("dp", "tensor"), None),
            P(("dp", "tensor"), None),
            P(),
            P(),
            P(),
            P(),
            P("dp", "tensor"),
            P("dp", "tensor"),
            P("dp", "tensor"),
            P("dp", "tensor"),
            P("dp", "tensor"),
            P("dp", "tensor"),
            P("dp", "tensor"),
        ),
        check_vma=False,
    )
```

```python
import math

import jax
import jax.numpy as jnp
from jax import lax
from jax.experimental import pallas as pl
from jax.experimental.pallas import tpu as pltpu
from jax.sharding import PartitionSpec as P

SEQUENCE_LENGTH = 1024


epsilon = 1e-06
masked = -1e30


def matmul(left, right):
    return jnp.dot(left, right, preferred_element_type=jnp.float32)


def contract_first(left, right):
    return lax.dot_general(
        left, right, (((0,), (0,)), ((), ())), preferred_element_type=jnp.float32
    )


def contract_last(left, right):
    return lax.dot_general(
        left, right, (((1,), (1,)), ((), ())), preferred_element_type=jnp.float32
    )


def tables(positions, width):
    frequency = jnp.exp(
        jnp.arange(width // 2, dtype=jnp.float32) * (-2.0 * math.log(1000000.0) / width)
    )
    angles = positions.astype(jnp.float32)[:, None] * frequency[None, :]
    cosine = jnp.cos(angles)
    sine = jnp.sin(angles)
    return (
        jnp.concatenate([cosine, cosine], axis=-1),
        jnp.concatenate([-sine, sine], axis=-1),
    )


def inverse_rms(value_rows):
    return lax.rsqrt(jnp.mean(value_rows * value_rows, axis=-1, keepdims=True) + epsilon)


def norm_backward(upstream, scaled, inverse, gain):
    inner = upstream * gain
    return inverse * (inner - scaled * jnp.mean(inner * scaled, axis=-1, keepdims=True))


class Links:
    def __init__(self, dp_size, tensor_size):
        self.dp_size = dp_size
        self.tensor_size = tensor_size
        self.chips = dp_size // 2
        self.swap = [(place, place ^ 1) for place in range(dp_size)]

    def shifted(self, value, step):
        return lax.ppermute(
            value,
            "dp",
            [
                (2 * chip + core, 2 * ((chip + step) % self.chips) + core)
                for chip in range(self.chips)
                for core in range(2)
            ],
        )

    def other_core(self, value):
        return lax.ppermute(value, "dp", self.swap)

    def across(self, value, bit):
        return lax.ppermute(
            value, "tensor", [(place, place ^ bit) for place in range(self.tensor_size)]
        )

    def relative_tokens(self, values):
        count = values.shape[0] // self.tensor_size
        place = lax.axis_index("tensor")
        return jnp.concatenate(
            [
                lax.dynamic_slice_in_dim(values, (place ^ other) * count, count, 0)
                for other in range(self.tensor_size)
            ],
            axis=0,
        )

    def gather_first(self, block):
        if self.tensor_size != 4:
            return block, block
        return self.across(block, 1), self.across(block, 2)

    def gather_second(self, block, first):
        if self.tensor_size != 4:
            bit = 1
            while bit < self.tensor_size:
                block = jnp.concatenate([block, self.across(block, bit)], axis=0)
                bit *= 2
            return block
        half = block.shape[0] // 2
        by_x, by_y = first
        corner_low = self.across(by_y[:half], 1)
        corner_high = self.across(by_x[half:], 2)
        return jnp.concatenate([block, by_x, by_y, corner_low, corner_high], axis=0)

    def gather_tokens(self, block):
        return self.gather_second(block, self.gather_first(block))

    def scatter_tokens(self, partial):
        return self.scatter_second(partial, self.scatter_first(partial))

    def half_block(self, partial, block, high):
        half = partial.shape[0] // (2 * self.tensor_size)
        start = 2 * block * half + high * half
        return partial[start : start + half]

    def scatter_first(self, partial):
        if self.tensor_size != 4:
            return (partial,)
        return (
            self.across(self.half_block(partial, 3, 0), 1),
            self.across(self.half_block(partial, 3, 1), 2),
            self.across(self.half_block(partial, 1, 0), 1),
            self.across(self.half_block(partial, 2, 1), 2),
        )

    def scatter_second(self, partial, first):
        wide = jnp.float32
        if self.tensor_size != 4:
            (partial,) = first
            bit = self.tensor_size // 2
            while bit:
                middle = partial.shape[0] // 2
                arrived = self.across(partial[middle:], bit).astype(wide)
                total = partial[:middle].astype(wide) + arrived
                partial = total.astype(partial.dtype)
                bit //= 2
            return total
        low_pass, high_pass, low_own, high_own = first

        def passed(block, high, arrived):
            total = self.half_block(partial, block, high).astype(wide) + arrived.astype(wide)
            return total.astype(partial.dtype)

        low_last = self.across(passed(2, 0, low_pass), 2)
        high_last = self.across(passed(1, 1, high_pass), 1)
        low = self.half_block(partial, 0, 0).astype(wide) + low_own.astype(wide)
        high = self.half_block(partial, 0, 1).astype(wide) + high_own.astype(wide)
        return jnp.concatenate(
            [low + low_last.astype(wide), high + high_last.astype(wide)], axis=0
        )

    def gather_weight(self, shard):
        return lax.all_gather(shard, "dp", axis=0, tiled=True)

    def scatter_weight(self, partial):
        return lax.psum_scatter(partial, "dp", scatter_dimension=0, tiled=True)

    def total_tensor(self, value):
        bit = 1
        while bit < self.tensor_size:
            value = value + self.across(value, bit)
            bit *= 2
        return value

    def total_dp(self, value):
        chip = lax.axis_index("dp") // 2
        value = value + self.other_core(value)
        parts = jnp.stack([value] + [self.shifted(value, step) for step in range(1, self.chips)])
        total = None
        for target in range(self.chips):
            part = lax.dynamic_index_in_dim(parts, (chip - target) % self.chips, 0, keepdims=False)
            total = part if total is None else total + part
        return total


def product(left, right, left_axis, right_axis):
    return lax.dot_general(
        left,
        right,
        (((left_axis,), (right_axis,)), ((), ())),
        preferred_element_type=jnp.float32,
    )


class Attention:
    def __init__(self, rows, head_size, query_heads, key_heads, blocks):
        self.rows = rows
        self.head_size = head_size
        self.query_heads = query_heads
        self.key_heads = key_heads
        self.grouping = query_heads // key_heads
        self.blocks = blocks
        self.block = rows // blocks
        self.scale = head_size ** (-0.5)

    def cost(self, products):
        scores = self.query_heads * self.rows * self.rows
        return pl.CostEstimate(
            flops=products * 2 * scores * 2 * self.head_size,
            transcendentals=scores,
            bytes_accessed=16 * self.query_heads * self.rows * self.head_size,
        )

    def outside(self, place, index):
        return pl.ds(pl.multiple_of((index ^ place) * self.block, self.block), self.block)

    def inside(self, index):
        return slice(index * self.block, (index + 1) * self.block)

    def head(self, index):
        return slice(index * self.head_size, (index + 1) * self.head_size)

    def turn(self, rows):
        return pltpu.roll(rows, self.head_size // 2, axis=1)

    def forward_kernel(
        self, place_ref, raw_query, raw_key, raw_value, cosine, sine, query_gain, key_gain,
        query, key, value, attended, totals,
    ):
        place = place_ref[0]

        def prepared(raw, gain, where):
            normed = raw * inverse_rms(raw) * gain
            turned = normed * cosine[where, :] + self.turn(normed) * sine[where, :]
            return turned.astype(jnp.bfloat16)

        for index in range(self.blocks):
            there, here = self.outside(place, index), self.inside(index)
            key[here, :] = prepared(raw_key[there, :], key_gain[...], there)
            value[here, :] = raw_value[there, :].astype(jnp.bfloat16)
            for member in range(self.grouping):
                query[here, self.head(member)] = prepared(
                    raw_query[there, self.head(member)], query_gain[...], there
                )
        for member in range(self.grouping):
            for index in range(self.blocks):
                span = (index + 1) * self.block
                scores = self.scale * product(
                    query[self.inside(index), self.head(member)], key[:span, :], 1, 1
                )
                row = index * self.block + lax.broadcasted_iota(jnp.int32, scores.shape, 0)
                column = lax.broadcasted_iota(jnp.int32, scores.shape, 1)
                scores = jnp.where(column <= row, scores, masked)
                highest = jnp.max(scores, axis=1, keepdims=True)
                powers = jnp.exp(scores - highest)
                total = jnp.sum(powers, axis=1, keepdims=True)
                shares = (powers * (1.0 / total)).astype(jnp.bfloat16)
                attended[self.outside(place, index), self.head(member)] = product(
                    shares, value[:span, :], 1, 0
                ).astype(jnp.bfloat16)
                log_total = jnp.broadcast_to(
                    highest + jnp.log(total), (self.block, self.head_size)
                )
                totals[0, member : member + 1, self.inside(index)] = log_total.T[:1, :]

    def forward(self, place, raw, cosine, sine, query_gain, key_gain):
        rows, size, group = self.rows, self.head_size, self.grouping
        wide = group * size
        first_key, first_value = self.query_heads, self.query_heads + self.key_heads
        whole = lambda h, p: (0, 0)
        by_head = lambda h, p: (0, h)
        low = jnp.bfloat16
        return pl.pallas_call(
            self.forward_kernel,
            name="attention_forward",
            cost_estimate=self.cost(2),
            grid_spec=pltpu.PrefetchScalarGridSpec(
                num_scalar_prefetch=1,
                grid=(self.key_heads,),
                in_specs=[
                    pl.BlockSpec((rows, wide), by_head),
                    pl.BlockSpec((rows, size), lambda h, p: (0, first_key + h)),
                    pl.BlockSpec((rows, size), lambda h, p: (0, first_value + h)),
                    pl.BlockSpec((rows, size), whole),
                    pl.BlockSpec((rows, size), whole),
                    pl.BlockSpec((1, size), whole),
                    pl.BlockSpec((1, size), whole),
                ],
                out_specs=[
                    pl.BlockSpec((rows, wide), by_head),
                    pl.BlockSpec((rows, size), by_head),
                    pl.BlockSpec((rows, size), by_head),
                    pl.BlockSpec((rows, wide), by_head),
                    pl.BlockSpec((1, group, rows), lambda h, p: (h, 0, 0)),
                ],
            ),
            out_shape=[
                jax.ShapeDtypeStruct((rows, self.query_heads * size), low),
                jax.ShapeDtypeStruct((rows, self.key_heads * size), low),
                jax.ShapeDtypeStruct((rows, self.key_heads * size), low),
                jax.ShapeDtypeStruct((rows, self.query_heads * size), low),
                jax.ShapeDtypeStruct((self.key_heads, group, rows), jnp.float32),
            ],
        )(place, raw, raw, raw, cosine, sine, query_gain[None, :], key_gain[None, :])

    def backward_kernel(
        self, place_ref, raw_query, raw_key, cosine, sine, query_gain, key_gain,
        query, key, value, totals, upstream,
        raw_grad, query_gain_grad, key_gain_grad, key_total, value_total,
    ):
        place = place_ref[0]
        current = pl.program_id(0)
        size, group = self.head_size, self.grouping

        @pl.when(current == 0)
        def _():
            query_gain_grad[...] = jnp.zeros_like(query_gain_grad)
            key_gain_grad[...] = jnp.zeros_like(key_gain_grad)

        def store(where, head, grad):
            column = pl.multiple_of(head * size, size)
            raw_grad[where, pl.ds(column, size)] = grad.astype(jnp.bfloat16)

        def through_norm(raw, grad, gain, where, gain_grad):
            inverse = inverse_rms(raw)
            scaled = raw * inverse
            normed_grad = grad * cosine[where, :] - self.turn(grad) * sine[where, :]
            gain_grad[...] += jnp.sum(normed_grad * scaled, axis=0, keepdims=True)
            return norm_backward(normed_grad, scaled, inverse, gain)

        for member in range(group):
            for index in reversed(range(self.blocks)):
                here, there = self.inside(index), self.outside(place, index)
                span = (index + 1) * self.block
                query_block = query[here, self.head(member)]
                grad_block = upstream[there, self.head(member)]
                scores = self.scale * product(key[:span, :], query_block, 1, 1)
                row = index * self.block + lax.broadcasted_iota(jnp.int32, scores.shape, 1)
                column = lax.broadcasted_iota(jnp.int32, scores.shape, 0)
                scores = jnp.where(column <= row, scores, masked)
                shares = jnp.exp(scores - totals[0, member : member + 1, here])
                share_grad = product(value[:span, :], grad_block, 1, 1)
                inner = jnp.sum(share_grad * shares, axis=0, keepdims=True)
                score_grad = (shares * (share_grad - inner)).astype(jnp.bfloat16)
                value_part = product(shares.astype(jnp.bfloat16), grad_block, 1, 0)
                key_part = product(score_grad, query_block, 1, 0)
                if member == 0 and index == self.blocks - 1:
                    value_total[...] = value_part
                    key_total[...] = key_part
                else:
                    value_total[:span, :] += value_part
                    key_total[:span, :] += key_part
                query_grad = self.scale * product(score_grad, key[:span, :], 0, 0)
                store(
                    there,
                    current * group + member,
                    through_norm(
                        raw_query[there, self.head(member)],
                        query_grad,
                        query_gain[...],
                        there,
                        query_gain_grad,
                    ),
                )
        for index in range(self.blocks):
            here, there = self.inside(index), self.outside(place, index)
            store(
                there,
                self.query_heads + current,
                through_norm(
                    raw_key[there, :],
                    self.scale * key_total[here, :],
                    key_gain[...],
                    there,
                    key_gain_grad,
                ),
            )
            store(there, self.query_heads + self.key_heads + current, value_total[here, :])

    def backward(
        self, place, raw, cosine, sine, query_gain, key_gain, query, key, value, totals, upstream
    ):
        rows, size, group = self.rows, self.head_size, self.grouping
        wide = group * size
        first_key = self.query_heads
        whole = lambda h, p: (0, 0)
        by_head = lambda h, p: (0, h)
        columns = (self.query_heads + 2 * self.key_heads) * size
        return pl.pallas_call(
            self.backward_kernel,
            name="attention_backward",
            cost_estimate=self.cost(5),
            grid_spec=pltpu.PrefetchScalarGridSpec(
                num_scalar_prefetch=1,
                grid=(self.key_heads,),
                in_specs=[
                    pl.BlockSpec((rows, wide), by_head),
                    pl.BlockSpec((rows, size), lambda h, p: (0, first_key + h)),
                    pl.BlockSpec((rows, size), whole),
                    pl.BlockSpec((rows, size), whole),
                    pl.BlockSpec((1, size), whole),
                    pl.BlockSpec((1, size), whole),
                    pl.BlockSpec((rows, wide), by_head),
                    pl.BlockSpec((rows, size), by_head),
                    pl.BlockSpec((rows, size), by_head),
                    pl.BlockSpec((1, group, rows), lambda h, p: (h, 0, 0)),
                    pl.BlockSpec((rows, wide), by_head),
                ],
                out_specs=[
                    pl.BlockSpec((rows, columns), whole),
                    pl.BlockSpec((1, size), whole),
                    pl.BlockSpec((1, size), whole),
                ],
                scratch_shapes=[
                    pltpu.VMEM((rows, size), jnp.float32),
                    pltpu.VMEM((rows, size), jnp.float32),
                ],
            ),
            out_shape=[
                jax.ShapeDtypeStruct((rows, columns), jnp.bfloat16),
                jax.ShapeDtypeStruct((1, size), jnp.float32),
                jax.ShapeDtypeStruct((1, size), jnp.float32),
            ],
        )(
            place, raw, raw, cosine, sine, query_gain[None, :], key_gain[None, :],
            query, key, value, totals, upstream,
        )


def shards(
    links,
    tokens,
    positions,
    input_gain,
    middle_gain,
    query_gain,
    key_gain,
    query_weight,
    key_matrix,
    value_matrix,
    output_weight,
    gate_weight,
    up_weight,
    down_weight,
    layer_cotangent,
):
    head_size = query_gain.shape[0]
    query_heads = query_weight.shape[1] // head_size
    key_heads = key_matrix.shape[1] // head_size
    query_width = query_heads * head_size
    key_width = key_heads * head_size
    group_rows = positions.shape[0]
    assert group_rows == SEQUENCE_LENGTH
    attention = Attention(group_rows, head_size, query_heads, key_heads, links.tensor_size)
    place = lax.axis_index("tensor").astype(jnp.int32)[None]
    hidden = gate_weight.shape[1]
    wide_mixing = links.gather_weight(
        jnp.concatenate([query_weight, key_matrix, value_matrix, output_weight], axis=1)
    )
    wide_attention = wide_mixing[:, : query_width + 2 * key_width]
    wide_output = wide_mixing[:, query_width + 2 * key_width :]
    wide_feed = links.gather_weight(jnp.concatenate([gate_weight, up_weight], axis=1))
    wide_down = links.gather_weight(down_weight)

    positions = links.relative_tokens(positions)
    inputs = tokens.astype(jnp.float32)
    inverse_in = inverse_rms(inputs)
    scaled_in = inputs * inverse_in
    normed_rows = links.gather_tokens((scaled_in * input_gain).astype(jnp.bfloat16))
    own_cotangent = layer_cotangent
    cotangent_first = links.gather_first(own_cotangent)
    normed_rows, cotangent_first = lax.optimization_barrier((normed_rows, cotangent_first))
    cotangent = links.gather_second(own_cotangent, cotangent_first)

    cosine, sine = tables(positions, head_size)
    raw_rows = matmul(normed_rows, wide_attention)
    query_rows, key_rows, value_rows, attended_rows, log_totals = attention.forward(
        place, raw_rows, cosine, sine, query_gain, key_gain
    )
    attended_rows, cotangent = lax.optimization_barrier((attended_rows, cotangent))
    branch_partial = contract_last(attended_rows, wide_output).astype(jnp.bfloat16)
    branch_first = links.scatter_first(branch_partial)
    branch = links.scatter_second(branch_partial, branch_first)
    middle = inputs + branch
    inverse_mid = inverse_rms(middle)
    scaled_mid = middle * inverse_mid
    normed_middle = links.gather_tokens((scaled_mid * middle_gain).astype(jnp.bfloat16))
    feed = matmul(normed_middle, wide_feed)
    gating, upward = feed[:, :hidden], feed[:, hidden:]
    gate_sigmoid = jax.nn.sigmoid(gating)
    silu_gate = gating * gate_sigmoid
    active = (silu_gate * upward).astype(jnp.bfloat16)
    down_term = contract_first(cotangent, active).astype(jnp.bfloat16)
    active, down_term = lax.optimization_barrier((active, down_term))
    down_sum = links.scatter_weight(down_term)
    cotangent, down_term = lax.optimization_barrier((cotangent, down_term))
    active_grad = matmul(cotangent, wide_down)
    gate_grad = (
        active_grad * upward * gate_sigmoid * (1.0 + gating * (1.0 - gate_sigmoid))
    ).astype(jnp.bfloat16)
    upward_grad = (active_grad * silu_gate).astype(jnp.bfloat16)
    feed_grad = jnp.concatenate([gate_grad, upward_grad], axis=1)
    middle_partial = contract_last(feed_grad, wide_feed)
    middle_partial = middle_partial.astype(jnp.bfloat16)
    feed_grad, middle_partial = lax.optimization_barrier((feed_grad, middle_partial))
    middle_first = links.scatter_first(middle_partial)
    feed_term = contract_first(normed_middle, feed_grad).astype(jnp.bfloat16)
    feed_term, middle_first, down_sum = lax.optimization_barrier(
        (feed_term, middle_first, down_sum)
    )
    feed_sum = links.scatter_weight(feed_term)
    middle_normed_grad = links.scatter_second(middle_partial, middle_first)
    feed_partial = contract_last(active, wide_down).astype(jnp.bfloat16)
    middle_normed_grad, feed_partial = lax.optimization_barrier((middle_normed_grad, feed_partial))
    middle_gain_term = jnp.sum(middle_normed_grad * scaled_mid, axis=0)
    middle_grad = own_cotangent.astype(jnp.float32) + norm_backward(
        middle_normed_grad, scaled_mid, inverse_mid, middle_gain
    )
    branch_grad = links.gather_tokens(middle_grad.astype(jnp.bfloat16))
    feed_partial, branch_grad = lax.optimization_barrier((feed_partial, branch_grad))
    feed_first = links.scatter_first(feed_partial)
    output_term = contract_first(branch_grad, attended_rows).astype(jnp.bfloat16)
    branch_grad, output_term = lax.optimization_barrier((branch_grad, output_term))
    attended_grad = matmul(branch_grad, wide_output).astype(jnp.bfloat16)
    raw_grad, query_gain_term, key_gain_term = attention.backward(
        place,
        raw_rows,
        cosine,
        sine,
        query_gain,
        key_gain,
        query_rows,
        key_rows,
        value_rows,
        log_totals,
        attended_grad,
    )
    raw_grad, feed_first = lax.optimization_barrier((raw_grad, feed_first))
    input_partial = contract_last(raw_grad, wide_attention).astype(jnp.bfloat16)
    input_first = links.scatter_first(input_partial)
    raw_grad, input_partial = lax.optimization_barrier((raw_grad, input_partial))
    attention_term = contract_first(normed_rows, raw_grad).astype(jnp.bfloat16)
    mixing_term = jnp.concatenate([attention_term, output_term], axis=1)
    mixing_term, feed_sum, passed = lax.optimization_barrier(
        (mixing_term, feed_sum, input_first[:2])
    )
    input_first = passed + input_first[2:]
    mixing_sum = links.scatter_weight(mixing_term)
    feed_branch = links.scatter_second(feed_partial, feed_first)
    input_first, feed_branch = lax.optimization_barrier((input_first, feed_branch))
    input_gain_term = (
        jnp.sum(input_partial.astype(jnp.float32) * normed_rows.astype(jnp.float32), axis=0)
        / input_gain
    )
    terms = jnp.concatenate(
        [input_gain_term, middle_gain_term, query_gain_term[0], key_gain_term[0]]
    )
    input_normed_grad = links.scatter_second(input_partial, input_first)
    terms, input_normed_grad = lax.optimization_barrier((terms, input_normed_grad))
    layer_output = middle + feed_branch
    tokens_grad = middle_grad + norm_backward(input_normed_grad, scaled_in, inverse_in, input_gain)
    terms = links.total_dp(links.total_tensor(terms))
    width = tokens.shape[1]
    mixing_sum, feed_sum = mixing_sum.astype(jnp.float32), feed_sum.astype(jnp.float32)
    return (
        layer_output,
        tokens_grad,
        terms[:width],
        terms[width : 2 * width],
        terms[2 * width : 2 * width + head_size],
        terms[2 * width + head_size :],
        mixing_sum[:, :query_width],
        mixing_sum[:, query_width : query_width + key_width],
        mixing_sum[:, query_width + key_width : query_width + 2 * key_width],
        mixing_sum[:, query_width + 2 * key_width :],
        feed_sum[:, :hidden],
        feed_sum[:, hidden:],
        down_sum.astype(jnp.float32),
    )


def solution(mesh):
    links = Links(mesh.shape["dp"], mesh.shape["tensor"])
    placed = (
        P(("dp", "tensor"), None),
        P("dp"),
        P(),
        P(),
        P(),
        P(),
        P("dp", "tensor"),
        P("dp", "tensor"),
        P("dp", "tensor"),
        P("dp", "tensor"),
        P("dp", "tensor"),
        P("dp", "tensor"),
        P("dp", "tensor"),
        P(("dp", "tensor"), None),
    )
    return jax.shard_map(
        lambda *arrays: shards(links, *arrays),
        mesh=mesh,
        in_specs=placed,
        out_specs=(
            P(("dp", "tensor"), None),
            P(("dp", "tensor"), None),
            P(),
            P(),
            P(),
            P(),
            P("dp", "tensor"),
            P("dp", "tensor"),
            P("dp", "tensor"),
            P("dp", "tensor"),
            P("dp", "tensor"),
            P("dp", "tensor"),
            P("dp", "tensor"),
        ),
        check_vma=False,
    )
```

```python
import math

import jax
import jax.numpy as jnp
from jax import lax
from jax.experimental import pallas as pl
from jax.experimental.pallas import tpu as pltpu
from jax.sharding import PartitionSpec as P

SEQUENCE_LENGTH = 1024


epsilon = 1e-06
masked = -1e30


def matmul(left, right):
    return jnp.dot(left, right, preferred_element_type=jnp.float32)


def contract_first(left, right):
    return lax.dot_general(
        left, right, (((0,), (0,)), ((), ())), preferred_element_type=jnp.float32
    )


def contract_last(left, right):
    return lax.dot_general(
        left, right, (((1,), (1,)), ((), ())), preferred_element_type=jnp.float32
    )


def tables(positions, width):
    frequency = jnp.exp(
        jnp.arange(width // 2, dtype=jnp.float32) * (-2.0 * math.log(1000000.0) / width)
    )
    angles = positions.astype(jnp.float32)[:, None] * frequency[None, :]
    cosine = jnp.cos(angles)
    sine = jnp.sin(angles)
    return (
        jnp.concatenate([cosine, cosine], axis=-1),
        jnp.concatenate([-sine, sine], axis=-1),
    )


def inverse_rms(value_rows):
    return lax.rsqrt(jnp.mean(value_rows * value_rows, axis=-1, keepdims=True) + epsilon)


def norm_backward(upstream, scaled, inverse, gain):
    inner = upstream * gain
    return inverse * (inner - scaled * jnp.mean(inner * scaled, axis=-1, keepdims=True))


class Links:
    def __init__(self, dp_size, tensor_size):
        self.dp_size = dp_size
        self.tensor_size = tensor_size
        self.chips = dp_size // 2
        self.swap = [(place, place ^ 1) for place in range(dp_size)]

    def shifted(self, value, step):
        return lax.ppermute(
            value,
            "dp",
            [
                (2 * chip + core, 2 * ((chip + step) % self.chips) + core)
                for chip in range(self.chips)
                for core in range(2)
            ],
        )

    def other_core(self, value):
        return lax.ppermute(value, "dp", self.swap)

    def across(self, value, bit):
        return lax.ppermute(
            value, "tensor", [(place, place ^ bit) for place in range(self.tensor_size)]
        )

    def relative_tokens(self, values):
        count = values.shape[0] // self.tensor_size
        place = lax.axis_index("tensor")
        return jnp.concatenate(
            [
                lax.dynamic_slice_in_dim(values, (place ^ other) * count, count, 0)
                for other in range(self.tensor_size)
            ],
            axis=0,
        )

    def gather_first(self, block):
        if self.tensor_size != 4:
            return block, block
        return self.across(block, 1), self.across(block, 2)

    def gather_second(self, block, first):
        if self.tensor_size != 4:
            bit = 1
            while bit < self.tensor_size:
                block = jnp.concatenate([block, self.across(block, bit)], axis=0)
                bit *= 2
            return block
        half = block.shape[0] // 2
        by_x, by_y = first
        corner_low = self.across(by_y[:half], 1)
        corner_high = self.across(by_x[half:], 2)
        return jnp.concatenate([block, by_x, by_y, corner_low, corner_high], axis=0)

    def gather_tokens(self, block):
        return self.gather_second(block, self.gather_first(block))

    def scatter_tokens(self, partial):
        return self.scatter_second(partial, self.scatter_first(partial))

    def half_block(self, partial, block, high):
        half = partial.shape[0] // (2 * self.tensor_size)
        start = 2 * block * half + high * half
        return partial[start : start + half]

    def scatter_first(self, partial):
        if self.tensor_size != 4:
            return (partial,)
        return (
            self.across(self.half_block(partial, 3, 0), 1),
            self.across(self.half_block(partial, 3, 1), 2),
            self.across(self.half_block(partial, 1, 0), 1),
            self.across(self.half_block(partial, 2, 1), 2),
        )

    def scatter_second(self, partial, first):
        wide = jnp.float32
        if self.tensor_size != 4:
            (partial,) = first
            bit = self.tensor_size // 2
            while bit:
                middle = partial.shape[0] // 2
                arrived = self.across(partial[middle:], bit).astype(wide)
                total = partial[:middle].astype(wide) + arrived
                partial = total.astype(partial.dtype)
                bit //= 2
            return total
        low_pass, high_pass, low_own, high_own = first

        def passed(block, high, arrived):
            total = self.half_block(partial, block, high).astype(wide) + arrived.astype(wide)
            return total.astype(partial.dtype)

        low_last = self.across(passed(2, 0, low_pass), 2)
        high_last = self.across(passed(1, 1, high_pass), 1)
        low = self.half_block(partial, 0, 0).astype(wide) + low_own.astype(wide)
        high = self.half_block(partial, 0, 1).astype(wide) + high_own.astype(wide)
        return jnp.concatenate(
            [low + low_last.astype(wide), high + high_last.astype(wide)], axis=0
        )

    def gather_weight(self, shard):
        return lax.all_gather(shard, "dp", axis=0, tiled=True)

    def scatter_weight(self, partial):
        return lax.psum_scatter(partial, "dp", scatter_dimension=0, tiled=True)

    def total_tensor(self, value):
        bit = 1
        while bit < self.tensor_size:
            value = value + self.across(value, bit)
            bit *= 2
        return value

    def total_dp(self, value):
        chip = lax.axis_index("dp") // 2
        value = value + self.other_core(value)
        parts = jnp.stack([value] + [self.shifted(value, step) for step in range(1, self.chips)])
        total = None
        for target in range(self.chips):
            part = lax.dynamic_index_in_dim(parts, (chip - target) % self.chips, 0, keepdims=False)
            total = part if total is None else total + part
        return total


def product(left, right, left_axis, right_axis):
    return lax.dot_general(
        left,
        right,
        (((left_axis,), (right_axis,)), ((), ())),
        preferred_element_type=jnp.float32,
    )


def split_columns(rows, widths):
    def kernel(source, *targets):
        start = 0
        for target in targets:
            width = target.shape[1]
            target[...] = source[:, start : start + width].astype(jnp.float32)
            start += width

    return pl.pallas_call(
        kernel,
        name="split_columns",
        out_shape=[jax.ShapeDtypeStruct((rows.shape[0], width), jnp.float32) for width in widths],
    )(rows)


class Attention:
    def __init__(self, rows, head_size, query_heads, key_heads, blocks):
        self.rows = rows
        self.head_size = head_size
        self.query_heads = query_heads
        self.key_heads = key_heads
        self.grouping = query_heads // key_heads
        self.blocks = blocks
        self.block = rows // blocks
        self.scale = head_size ** (-0.5)

    def cost(self, products):
        scores = self.query_heads * self.rows * self.rows
        return pl.CostEstimate(
            flops=products * 2 * scores * 2 * self.head_size,
            transcendentals=scores,
            bytes_accessed=16 * self.query_heads * self.rows * self.head_size,
        )

    def outside(self, place, index):
        return pl.ds(pl.multiple_of((index ^ place) * self.block, self.block), self.block)

    def inside(self, index):
        return slice(index * self.block, (index + 1) * self.block)

    def head(self, index):
        return slice(index * self.head_size, (index + 1) * self.head_size)

    def turn(self, rows):
        return pltpu.roll(rows, self.head_size // 2, axis=1)

    def forward_kernel(
        self, place_ref, raw_query, raw_key, raw_value, cosine, sine, query_gain, key_gain,
        query, key, value, attended, totals,
    ):
        place = place_ref[0]

        def prepared(raw, gain, where):
            normed = raw * inverse_rms(raw) * gain
            turned = normed * cosine[where, :] + self.turn(normed) * sine[where, :]
            return turned.astype(jnp.bfloat16)

        for index in range(self.blocks):
            there, here = self.outside(place, index), self.inside(index)
            key[here, :] = prepared(raw_key[there, :], key_gain[...], there)
            value[here, :] = raw_value[there, :].astype(jnp.bfloat16)
            for member in range(self.grouping):
                query[here, self.head(member)] = prepared(
                    raw_query[there, self.head(member)], query_gain[...], there
                )
        for member in range(self.grouping):
            for index in range(self.blocks):
                span = (index + 1) * self.block
                scores = self.scale * product(
                    query[self.inside(index), self.head(member)], key[:span, :], 1, 1
                )
                row = index * self.block + lax.broadcasted_iota(jnp.int32, scores.shape, 0)
                column = lax.broadcasted_iota(jnp.int32, scores.shape, 1)
                scores = jnp.where(column <= row, scores, masked)
                highest = jnp.max(scores, axis=1, keepdims=True)
                powers = jnp.exp(scores - highest)
                total = jnp.sum(powers, axis=1, keepdims=True)
                shares = (powers * (1.0 / total)).astype(jnp.bfloat16)
                attended[self.outside(place, index), self.head(member)] = product(
                    shares, value[:span, :], 1, 0
                ).astype(jnp.bfloat16)
                log_total = jnp.broadcast_to(
                    highest + jnp.log(total), (self.block, self.head_size)
                )
                totals[0, member : member + 1, self.inside(index)] = log_total.T[:1, :]

    def forward(self, place, raw, cosine, sine, query_gain, key_gain):
        rows, size, group = self.rows, self.head_size, self.grouping
        wide = group * size
        first_key, first_value = self.query_heads, self.query_heads + self.key_heads
        whole = lambda h, p: (0, 0)
        by_head = lambda h, p: (0, h)
        low = jnp.bfloat16
        return pl.pallas_call(
            self.forward_kernel,
            name="attention_forward",
            cost_estimate=self.cost(2),
            grid_spec=pltpu.PrefetchScalarGridSpec(
                num_scalar_prefetch=1,
                grid=(self.key_heads,),
                in_specs=[
                    pl.BlockSpec((rows, wide), by_head),
                    pl.BlockSpec((rows, size), lambda h, p: (0, first_key + h)),
                    pl.BlockSpec((rows, size), lambda h, p: (0, first_value + h)),
                    pl.BlockSpec((rows, size), whole),
                    pl.BlockSpec((rows, size), whole),
                    pl.BlockSpec((1, size), whole),
                    pl.BlockSpec((1, size), whole),
                ],
                out_specs=[
                    pl.BlockSpec((rows, wide), by_head),
                    pl.BlockSpec((rows, size), by_head),
                    pl.BlockSpec((rows, size), by_head),
                    pl.BlockSpec((rows, wide), by_head),
                    pl.BlockSpec((1, group, rows), lambda h, p: (h, 0, 0)),
                ],
            ),
            out_shape=[
                jax.ShapeDtypeStruct((rows, self.query_heads * size), low),
                jax.ShapeDtypeStruct((rows, self.key_heads * size), low),
                jax.ShapeDtypeStruct((rows, self.key_heads * size), low),
                jax.ShapeDtypeStruct((rows, self.query_heads * size), low),
                jax.ShapeDtypeStruct((self.key_heads, group, rows), jnp.float32),
            ],
        )(place, raw, raw, raw, cosine, sine, query_gain[None, :], key_gain[None, :])

    def backward_kernel(
        self, place_ref, raw_query, raw_key, cosine, sine, query_gain, key_gain,
        query, key, value, totals, upstream,
        raw_grad, query_gain_grad, key_gain_grad, key_total, value_total,
    ):
        place = place_ref[0]
        current = pl.program_id(0)
        size, group = self.head_size, self.grouping

        @pl.when(current == 0)
        def _():
            query_gain_grad[...] = jnp.zeros_like(query_gain_grad)
            key_gain_grad[...] = jnp.zeros_like(key_gain_grad)

        def store(where, head, grad):
            column = pl.multiple_of(head * size, size)
            raw_grad[where, pl.ds(column, size)] = grad.astype(jnp.bfloat16)

        def through_norm(raw, grad, gain, where, gain_grad):
            inverse = inverse_rms(raw)
            scaled = raw * inverse
            normed_grad = grad * cosine[where, :] - self.turn(grad) * sine[where, :]
            gain_grad[...] += jnp.sum(normed_grad * scaled, axis=0, keepdims=True)
            return norm_backward(normed_grad, scaled, inverse, gain)

        for member in range(group):
            for index in reversed(range(self.blocks)):
                here, there = self.inside(index), self.outside(place, index)
                span = (index + 1) * self.block
                query_block = query[here, self.head(member)]
                grad_block = upstream[there, self.head(member)]
                scores = self.scale * product(key[:span, :], query_block, 1, 1)
                row = index * self.block + lax.broadcasted_iota(jnp.int32, scores.shape, 1)
                column = lax.broadcasted_iota(jnp.int32, scores.shape, 0)
                scores = jnp.where(column <= row, scores, masked)
                shares = jnp.exp(scores - totals[0, member : member + 1, here])
                share_grad = product(value[:span, :], grad_block, 1, 1)
                inner = jnp.sum(share_grad * shares, axis=0, keepdims=True)
                score_grad = (shares * (share_grad - inner)).astype(jnp.bfloat16)
                value_part = product(shares.astype(jnp.bfloat16), grad_block, 1, 0)
                key_part = product(score_grad, query_block, 1, 0)
                if member == 0 and index == self.blocks - 1:
                    value_total[...] = value_part
                    key_total[...] = key_part
                else:
                    value_total[:span, :] += value_part
                    key_total[:span, :] += key_part
                query_grad = self.scale * product(score_grad, key[:span, :], 0, 0)
                store(
                    there,
                    current * group + member,
                    through_norm(
                        raw_query[there, self.head(member)],
                        query_grad,
                        query_gain[...],
                        there,
                        query_gain_grad,
                    ),
                )
        for index in range(self.blocks):
            here, there = self.inside(index), self.outside(place, index)
            store(
                there,
                self.query_heads + current,
                through_norm(
                    raw_key[there, :],
                    self.scale * key_total[here, :],
                    key_gain[...],
                    there,
                    key_gain_grad,
                ),
            )
            store(there, self.query_heads + self.key_heads + current, value_total[here, :])

    def backward(
        self, place, raw, cosine, sine, query_gain, key_gain, query, key, value, totals, upstream
    ):
        rows, size, group = self.rows, self.head_size, self.grouping
        wide = group * size
        first_key = self.query_heads
        whole = lambda h, p: (0, 0)
        by_head = lambda h, p: (0, h)
        columns = (self.query_heads + 2 * self.key_heads) * size
        return pl.pallas_call(
            self.backward_kernel,
            name="attention_backward",
            cost_estimate=self.cost(5),
            grid_spec=pltpu.PrefetchScalarGridSpec(
                num_scalar_prefetch=1,
                grid=(self.key_heads,),
                in_specs=[
                    pl.BlockSpec((rows, wide), by_head),
                    pl.BlockSpec((rows, size), lambda h, p: (0, first_key + h)),
                    pl.BlockSpec((rows, size), whole),
                    pl.BlockSpec((rows, size), whole),
                    pl.BlockSpec((1, size), whole),
                    pl.BlockSpec((1, size), whole),
                    pl.BlockSpec((rows, wide), by_head),
                    pl.BlockSpec((rows, size), by_head),
                    pl.BlockSpec((rows, size), by_head),
                    pl.BlockSpec((1, group, rows), lambda h, p: (h, 0, 0)),
                    pl.BlockSpec((rows, wide), by_head),
                ],
                out_specs=[
                    pl.BlockSpec((rows, columns), whole),
                    pl.BlockSpec((1, size), whole),
                    pl.BlockSpec((1, size), whole),
                ],
                scratch_shapes=[
                    pltpu.VMEM((rows, size), jnp.float32),
                    pltpu.VMEM((rows, size), jnp.float32),
                ],
            ),
            out_shape=[
                jax.ShapeDtypeStruct((rows, columns), jnp.bfloat16),
                jax.ShapeDtypeStruct((1, size), jnp.float32),
                jax.ShapeDtypeStruct((1, size), jnp.float32),
            ],
        )(
            place, raw, raw, cosine, sine, query_gain[None, :], key_gain[None, :],
            query, key, value, totals, upstream,
        )


def shards(
    links,
    tokens,
    positions,
    input_gain,
    middle_gain,
    query_gain,
    key_gain,
    query_weight,
    key_matrix,
    value_matrix,
    output_weight,
    gate_weight,
    up_weight,
    down_weight,
    layer_cotangent,
):
    head_size = query_gain.shape[0]
    query_heads = query_weight.shape[1] // head_size
    key_heads = key_matrix.shape[1] // head_size
    query_width = query_heads * head_size
    key_width = key_heads * head_size
    group_rows = positions.shape[0]
    assert group_rows == SEQUENCE_LENGTH
    attention = Attention(group_rows, head_size, query_heads, key_heads, links.tensor_size)
    place = lax.axis_index("tensor").astype(jnp.int32)[None]
    hidden = gate_weight.shape[1]
    wide_mixing = links.gather_weight(
        jnp.concatenate([query_weight, key_matrix, value_matrix, output_weight], axis=1)
    )
    wide_attention = wide_mixing[:, : query_width + 2 * key_width]
    wide_output = wide_mixing[:, query_width + 2 * key_width :]
    wide_feed = links.gather_weight(jnp.concatenate([gate_weight, up_weight], axis=1))
    wide_down = links.gather_weight(down_weight)

    positions = links.relative_tokens(positions)
    inputs = tokens.astype(jnp.float32)
    inverse_in = inverse_rms(inputs)
    scaled_in = inputs * inverse_in
    normed_rows = links.gather_tokens((scaled_in * input_gain).astype(jnp.bfloat16))
    own_cotangent = layer_cotangent
    cotangent_first = links.gather_first(own_cotangent)
    normed_rows, cotangent_first = lax.optimization_barrier((normed_rows, cotangent_first))
    cotangent = links.gather_second(own_cotangent, cotangent_first)

    cosine, sine = tables(positions, head_size)
    raw_rows = matmul(normed_rows, wide_attention)
    query_rows, key_rows, value_rows, attended_rows, log_totals = attention.forward(
        place, raw_rows, cosine, sine, query_gain, key_gain
    )
    attended_rows, cotangent = lax.optimization_barrier((attended_rows, cotangent))
    branch_partial = contract_last(attended_rows, wide_output).astype(jnp.bfloat16)
    branch_first = links.scatter_first(branch_partial)
    branch = links.scatter_second(branch_partial, branch_first)
    middle = inputs + branch
    inverse_mid = inverse_rms(middle)
    scaled_mid = middle * inverse_mid
    normed_middle = links.gather_tokens((scaled_mid * middle_gain).astype(jnp.bfloat16))
    feed = matmul(normed_middle, wide_feed)
    gating, upward = feed[:, :hidden], feed[:, hidden:]
    gate_sigmoid = jax.nn.sigmoid(gating)
    silu_gate = gating * gate_sigmoid
    active = (silu_gate * upward).astype(jnp.bfloat16)
    down_term = contract_first(cotangent, active).astype(jnp.bfloat16)
    active, down_term = lax.optimization_barrier((active, down_term))
    down_sum = links.scatter_weight(down_term)
    cotangent, down_term = lax.optimization_barrier((cotangent, down_term))
    active_grad = matmul(cotangent, wide_down)
    gate_grad = (
        active_grad * upward * gate_sigmoid * (1.0 + gating * (1.0 - gate_sigmoid))
    ).astype(jnp.bfloat16)
    upward_grad = (active_grad * silu_gate).astype(jnp.bfloat16)
    feed_grad = jnp.concatenate([gate_grad, upward_grad], axis=1)
    middle_partial = contract_last(feed_grad, wide_feed)
    middle_partial = middle_partial.astype(jnp.bfloat16)
    feed_grad, middle_partial = lax.optimization_barrier((feed_grad, middle_partial))
    middle_first = links.scatter_first(middle_partial)
    feed_term = contract_first(normed_middle, feed_grad).astype(jnp.bfloat16)
    feed_term, middle_first, down_sum = lax.optimization_barrier(
        (feed_term, middle_first, down_sum)
    )
    feed_sum = links.scatter_weight(feed_term)
    middle_normed_grad = links.scatter_second(middle_partial, middle_first)
    feed_partial = contract_last(active, wide_down).astype(jnp.bfloat16)
    middle_normed_grad, feed_partial = lax.optimization_barrier((middle_normed_grad, feed_partial))
    middle_gain_term = jnp.sum(middle_normed_grad * scaled_mid, axis=0)
    middle_grad = own_cotangent.astype(jnp.float32) + norm_backward(
        middle_normed_grad, scaled_mid, inverse_mid, middle_gain
    )
    branch_grad = links.gather_tokens(middle_grad.astype(jnp.bfloat16))
    feed_partial, branch_grad = lax.optimization_barrier((feed_partial, branch_grad))
    feed_first = links.scatter_first(feed_partial)
    output_term = contract_first(branch_grad, attended_rows).astype(jnp.bfloat16)
    branch_grad, output_term = lax.optimization_barrier((branch_grad, output_term))
    attended_grad = matmul(branch_grad, wide_output).astype(jnp.bfloat16)
    raw_grad, query_gain_term, key_gain_term = attention.backward(
        place,
        raw_rows,
        cosine,
        sine,
        query_gain,
        key_gain,
        query_rows,
        key_rows,
        value_rows,
        log_totals,
        attended_grad,
    )
    raw_grad, feed_first = lax.optimization_barrier((raw_grad, feed_first))
    attention_term = contract_first(normed_rows, raw_grad).astype(jnp.bfloat16)
    feed_first, attention_term = lax.optimization_barrier((feed_first, attention_term))
    feed_branch = links.scatter_second(feed_partial, feed_first)
    raw_grad, attention_term = lax.optimization_barrier((raw_grad, attention_term))
    input_partial = contract_last(raw_grad, wide_attention).astype(jnp.bfloat16)
    mixing_term = jnp.concatenate([attention_term, output_term], axis=1)
    mixing_term, feed_sum, feed_branch, input_partial = lax.optimization_barrier(
        (mixing_term, feed_sum, feed_branch, input_partial)
    )
    mixing_sum = links.scatter_weight(mixing_term)
    input_first = links.scatter_first(input_partial)
    input_gain_term = (
        jnp.sum(input_partial.astype(jnp.float32) * normed_rows.astype(jnp.float32), axis=0)
        / input_gain
    )
    terms = jnp.concatenate(
        [input_gain_term, middle_gain_term, query_gain_term[0], key_gain_term[0]]
    )
    input_normed_grad = links.scatter_second(input_partial, input_first)
    terms, input_normed_grad = lax.optimization_barrier((terms, input_normed_grad))
    layer_output = middle + feed_branch
    tokens_grad = middle_grad + norm_backward(input_normed_grad, scaled_in, inverse_in, input_gain)
    terms = links.total_dp(links.total_tensor(terms))
    width = tokens.shape[1]
    feed_sum = feed_sum.astype(jnp.float32)
    query_sum, key_sum, value_sum, output_sum = split_columns(
        mixing_sum, (query_width, key_width, key_width, query_width)
    )
    return (
        layer_output,
        tokens_grad,
        terms[:width],
        terms[width : 2 * width],
        terms[2 * width : 2 * width + head_size],
        terms[2 * width + head_size :],
        query_sum,
        key_sum,
        value_sum,
        output_sum,
        feed_sum[:, :hidden],
        feed_sum[:, hidden:],
        down_sum.astype(jnp.float32),
    )


def solution(mesh):
    links = Links(mesh.shape["dp"], mesh.shape["tensor"])
    placed = (
        P(("dp", "tensor"), None),
        P("dp"),
        P(),
        P(),
        P(),
        P(),
        P("dp", "tensor"),
        P("dp", "tensor"),
        P("dp", "tensor"),
        P("dp", "tensor"),
        P("dp", "tensor"),
        P("dp", "tensor"),
        P("dp", "tensor"),
        P(("dp", "tensor"), None),
    )
    return jax.shard_map(
        lambda *arrays: shards(links, *arrays),
        mesh=mesh,
        in_specs=placed,
        out_specs=(
            P(("dp", "tensor"), None),
            P(("dp", "tensor"), None),
            P(),
            P(),
            P(),
            P(),
            P("dp", "tensor"),
            P("dp", "tensor"),
            P("dp", "tensor"),
            P("dp", "tensor"),
            P("dp", "tensor"),
            P("dp", "tensor"),
            P("dp", "tensor"),
        ),
        check_vma=False,
    )
```

```python
import math

import jax
import jax.numpy as jnp
from jax import lax
from jax.experimental import pallas as pl
from jax.experimental.pallas import tpu as pltpu
from jax.sharding import PartitionSpec as P

SEQUENCE_LENGTH = 1024


epsilon = 1e-06
masked = -1e30


def matmul(left, right):
    return jnp.dot(left, right, preferred_element_type=jnp.float32)


def contract_first(left, right):
    return lax.dot_general(
        left, right, (((0,), (0,)), ((), ())), preferred_element_type=jnp.float32
    )


def contract_last(left, right):
    return lax.dot_general(
        left, right, (((1,), (1,)), ((), ())), preferred_element_type=jnp.float32
    )


def tables(positions, width):
    frequency = jnp.exp(
        jnp.arange(width // 2, dtype=jnp.float32) * (-2.0 * math.log(1000000.0) / width)
    )
    angles = positions.astype(jnp.float32)[:, None] * frequency[None, :]
    cosine = jnp.cos(angles)
    sine = jnp.sin(angles)
    return (
        jnp.concatenate([cosine, cosine], axis=-1),
        jnp.concatenate([-sine, sine], axis=-1),
    )


def inverse_rms(value_rows):
    return lax.rsqrt(jnp.mean(value_rows * value_rows, axis=-1, keepdims=True) + epsilon)


def norm_backward(upstream, scaled, inverse, gain):
    inner = upstream * gain
    return inverse * (inner - scaled * jnp.mean(inner * scaled, axis=-1, keepdims=True))


class Links:
    def __init__(self, dp_size, tensor_size):
        self.dp_size = dp_size
        self.tensor_size = tensor_size
        self.chips = dp_size // 2
        self.swap = [(place, place ^ 1) for place in range(dp_size)]

    def shifted(self, value, step):
        return lax.ppermute(
            value,
            "dp",
            [
                (2 * chip + core, 2 * ((chip + step) % self.chips) + core)
                for chip in range(self.chips)
                for core in range(2)
            ],
        )

    def other_core(self, value):
        return lax.ppermute(value, "dp", self.swap)

    def across(self, value, bit):
        return lax.ppermute(
            value, "tensor", [(place, place ^ bit) for place in range(self.tensor_size)]
        )

    def relative_tokens(self, values):
        count = values.shape[0] // self.tensor_size
        place = lax.axis_index("tensor")
        return jnp.concatenate(
            [
                lax.dynamic_slice_in_dim(values, (place ^ other) * count, count, 0)
                for other in range(self.tensor_size)
            ],
            axis=0,
        )

    def gather_first(self, block):
        if self.tensor_size != 4:
            return block, block
        return lax.optimization_barrier((self.across(block, 1), self.across(block, 2)))

    def gather_second(self, block, first):
        if self.tensor_size != 4:
            bit = 1
            while bit < self.tensor_size:
                block = jnp.concatenate([block, self.across(block, bit)], axis=0)
                bit *= 2
            return block
        half = block.shape[0] // 2
        by_x, by_y = first
        corner_low, corner_high = lax.optimization_barrier(
            (self.across(by_y[:half], 1), self.across(by_x[half:], 2))
        )
        return jnp.concatenate([block, by_x, by_y, corner_low, corner_high], axis=0)

    def gather_tokens(self, block):
        return self.gather_second(block, self.gather_first(block))

    def scatter_tokens(self, partial):
        return self.scatter_second(partial, self.scatter_first(partial))

    def half_block(self, partial, block, high):
        half = partial.shape[0] // (2 * self.tensor_size)
        start = 2 * block * half + high * half
        return partial[start : start + half]

    def scatter_first(self, partial):
        if self.tensor_size != 4:
            return (partial,)
        return lax.optimization_barrier(
            (
                self.across(self.half_block(partial, 3, 0), 1),
                self.across(self.half_block(partial, 3, 1), 2),
                self.across(self.half_block(partial, 1, 0), 1),
                self.across(self.half_block(partial, 2, 1), 2),
            )
        )

    def scatter_second(self, partial, first):
        wide = jnp.float32
        if self.tensor_size != 4:
            (partial,) = first
            bit = self.tensor_size // 2
            while bit:
                middle = partial.shape[0] // 2
                arrived = self.across(partial[middle:], bit).astype(wide)
                total = partial[:middle].astype(wide) + arrived
                partial = total.astype(partial.dtype)
                bit //= 2
            return total
        low_pass, high_pass, low_own, high_own = first

        def passed(block, high, arrived):
            total = self.half_block(partial, block, high).astype(wide) + arrived.astype(wide)
            return total.astype(partial.dtype)

        low_last, high_last = lax.optimization_barrier(
            (
                self.across(passed(2, 0, low_pass), 2),
                self.across(passed(1, 1, high_pass), 1),
            )
        )
        low = self.half_block(partial, 0, 0).astype(wide) + low_own.astype(wide)
        high = self.half_block(partial, 0, 1).astype(wide) + high_own.astype(wide)
        return jnp.concatenate(
            [low + low_last.astype(wide), high + high_last.astype(wide)], axis=0
        )

    def gather_weight(self, shard):
        return lax.all_gather(shard, "dp", axis=0, tiled=True)

    def scatter_weight(self, partial):
        return lax.psum_scatter(partial, "dp", scatter_dimension=0, tiled=True)

    def total_tensor(self, value):
        bit = 1
        while bit < self.tensor_size:
            value = value + self.across(value, bit)
            bit *= 2
        return value

    def total_dp(self, value):
        chip = lax.axis_index("dp") // 2
        value = value + self.other_core(value)
        parts = jnp.stack([value] + [self.shifted(value, step) for step in range(1, self.chips)])
        total = None
        for target in range(self.chips):
            part = lax.dynamic_index_in_dim(parts, (chip - target) % self.chips, 0, keepdims=False)
            total = part if total is None else total + part
        return total


def product(left, right, left_axis, right_axis):
    return lax.dot_general(
        left,
        right,
        (((left_axis,), (right_axis,)), ((), ())),
        preferred_element_type=jnp.float32,
    )


def split_columns(rows, widths):
    def kernel(source, *targets):
        start = 0
        for target in targets:
            width = target.shape[1]
            target[...] = source[:, start : start + width].astype(jnp.float32)
            start += width

    return pl.pallas_call(
        kernel,
        name="split_columns",
        out_shape=[jax.ShapeDtypeStruct((rows.shape[0], width), jnp.float32) for width in widths],
    )(rows)


class Attention:
    def __init__(self, rows, head_size, query_heads, key_heads, blocks):
        self.rows = rows
        self.head_size = head_size
        self.query_heads = query_heads
        self.key_heads = key_heads
        self.grouping = query_heads // key_heads
        self.blocks = blocks
        self.block = rows // blocks
        self.scale = head_size ** (-0.5)

    def cost(self, products):
        scores = self.query_heads * self.rows * self.rows
        return pl.CostEstimate(
            flops=products * 2 * scores * 2 * self.head_size,
            transcendentals=scores,
            bytes_accessed=16 * self.query_heads * self.rows * self.head_size,
        )

    def outside(self, place, index):
        return pl.ds(pl.multiple_of((index ^ place) * self.block, self.block), self.block)

    def inside(self, index):
        return slice(index * self.block, (index + 1) * self.block)

    def head(self, index):
        return slice(index * self.head_size, (index + 1) * self.head_size)

    def turn(self, rows):
        return pltpu.roll(rows, self.head_size // 2, axis=1)

    def forward_kernel(
        self, place_ref, raw_query, raw_key, raw_value, cosine, sine, query_gain, key_gain,
        query, key, value, attended, totals,
    ):
        place = place_ref[0]

        def prepared(raw, gain, where):
            normed = raw * inverse_rms(raw) * gain
            turned = normed * cosine[where, :] + self.turn(normed) * sine[where, :]
            return turned.astype(jnp.bfloat16)

        for index in range(self.blocks):
            there, here = self.outside(place, index), self.inside(index)
            key[here, :] = prepared(raw_key[there, :], key_gain[...], there)
            value[here, :] = raw_value[there, :].astype(jnp.bfloat16)
            for member in range(self.grouping):
                query[here, self.head(member)] = prepared(
                    raw_query[there, self.head(member)], query_gain[...], there
                )
        for member in range(self.grouping):
            for index in range(self.blocks):
                span = (index + 1) * self.block
                scores = self.scale * product(
                    query[self.inside(index), self.head(member)], key[:span, :], 1, 1
                )
                row = index * self.block + lax.broadcasted_iota(jnp.int32, scores.shape, 0)
                column = lax.broadcasted_iota(jnp.int32, scores.shape, 1)
                scores = jnp.where(column <= row, scores, masked)
                highest = jnp.max(scores, axis=1, keepdims=True)
                powers = jnp.exp(scores - highest)
                total = jnp.sum(powers, axis=1, keepdims=True)
                shares = (powers * (1.0 / total)).astype(jnp.bfloat16)
                attended[self.outside(place, index), self.head(member)] = product(
                    shares, value[:span, :], 1, 0
                ).astype(jnp.bfloat16)
                log_total = jnp.broadcast_to(
                    highest + jnp.log(total), (self.block, self.head_size)
                )
                totals[0, member : member + 1, self.inside(index)] = log_total.T[:1, :]

    def forward(self, place, raw, cosine, sine, query_gain, key_gain):
        rows, size, group = self.rows, self.head_size, self.grouping
        wide = group * size
        first_key, first_value = self.query_heads, self.query_heads + self.key_heads
        whole = lambda h, p: (0, 0)
        by_head = lambda h, p: (0, h)
        low = jnp.bfloat16
        return pl.pallas_call(
            self.forward_kernel,
            name="attention_forward",
            cost_estimate=self.cost(2),
            grid_spec=pltpu.PrefetchScalarGridSpec(
                num_scalar_prefetch=1,
                grid=(self.key_heads,),
                in_specs=[
                    pl.BlockSpec((rows, wide), by_head),
                    pl.BlockSpec((rows, size), lambda h, p: (0, first_key + h)),
                    pl.BlockSpec((rows, size), lambda h, p: (0, first_value + h)),
                    pl.BlockSpec((rows, size), whole),
                    pl.BlockSpec((rows, size), whole),
                    pl.BlockSpec((1, size), whole),
                    pl.BlockSpec((1, size), whole),
                ],
                out_specs=[
                    pl.BlockSpec((rows, wide), by_head),
                    pl.BlockSpec((rows, size), by_head),
                    pl.BlockSpec((rows, size), by_head),
                    pl.BlockSpec((rows, wide), by_head),
                    pl.BlockSpec((1, group, rows), lambda h, p: (h, 0, 0)),
                ],
            ),
            out_shape=[
                jax.ShapeDtypeStruct((rows, self.query_heads * size), low),
                jax.ShapeDtypeStruct((rows, self.key_heads * size), low),
                jax.ShapeDtypeStruct((rows, self.key_heads * size), low),
                jax.ShapeDtypeStruct((rows, self.query_heads * size), low),
                jax.ShapeDtypeStruct((self.key_heads, group, rows), jnp.float32),
            ],
        )(place, raw, raw, raw, cosine, sine, query_gain[None, :], key_gain[None, :])

    def backward_kernel(
        self, place_ref, raw_query, raw_key, cosine, sine, query_gain, key_gain,
        query, key, value, totals, upstream,
        raw_grad, query_gain_grad, key_gain_grad, key_total, value_total,
    ):
        place = place_ref[0]
        current = pl.program_id(0)
        size, group = self.head_size, self.grouping

        @pl.when(current == 0)
        def _():
            query_gain_grad[...] = jnp.zeros_like(query_gain_grad)
            key_gain_grad[...] = jnp.zeros_like(key_gain_grad)

        def store(where, head, grad):
            column = pl.multiple_of(head * size, size)
            raw_grad[where, pl.ds(column, size)] = grad.astype(jnp.bfloat16)

        def through_norm(raw, grad, gain, where, gain_grad):
            inverse = inverse_rms(raw)
            scaled = raw * inverse
            normed_grad = grad * cosine[where, :] - self.turn(grad) * sine[where, :]
            gain_grad[...] += jnp.sum(normed_grad * scaled, axis=0, keepdims=True)
            return norm_backward(normed_grad, scaled, inverse, gain)

        for member in range(group):
            for index in reversed(range(self.blocks)):
                here, there = self.inside(index), self.outside(place, index)
                span = (index + 1) * self.block
                query_block = query[here, self.head(member)]
                grad_block = upstream[there, self.head(member)]
                scores = self.scale * product(key[:span, :], query_block, 1, 1)
                row = index * self.block + lax.broadcasted_iota(jnp.int32, scores.shape, 1)
                column = lax.broadcasted_iota(jnp.int32, scores.shape, 0)
                scores = jnp.where(column <= row, scores, masked)
                shares = jnp.exp(scores - totals[0, member : member + 1, here])
                share_grad = product(value[:span, :], grad_block, 1, 1)
                inner = jnp.sum(share_grad * shares, axis=0, keepdims=True)
                score_grad = (shares * (share_grad - inner)).astype(jnp.bfloat16)
                value_part = product(shares.astype(jnp.bfloat16), grad_block, 1, 0)
                key_part = product(score_grad, query_block, 1, 0)
                if member == 0 and index == self.blocks - 1:
                    value_total[...] = value_part
                    key_total[...] = key_part
                else:
                    value_total[:span, :] += value_part
                    key_total[:span, :] += key_part
                query_grad = self.scale * product(score_grad, key[:span, :], 0, 0)
                store(
                    there,
                    current * group + member,
                    through_norm(
                        raw_query[there, self.head(member)],
                        query_grad,
                        query_gain[...],
                        there,
                        query_gain_grad,
                    ),
                )
        for index in range(self.blocks):
            here, there = self.inside(index), self.outside(place, index)
            store(
                there,
                self.query_heads + current,
                through_norm(
                    raw_key[there, :],
                    self.scale * key_total[here, :],
                    key_gain[...],
                    there,
                    key_gain_grad,
                ),
            )
            store(there, self.query_heads + self.key_heads + current, value_total[here, :])

    def backward(
        self, place, raw, cosine, sine, query_gain, key_gain, query, key, value, totals, upstream
    ):
        rows, size, group = self.rows, self.head_size, self.grouping
        wide = group * size
        first_key = self.query_heads
        whole = lambda h, p: (0, 0)
        by_head = lambda h, p: (0, h)
        columns = (self.query_heads + 2 * self.key_heads) * size
        return pl.pallas_call(
            self.backward_kernel,
            name="attention_backward",
            cost_estimate=self.cost(5),
            grid_spec=pltpu.PrefetchScalarGridSpec(
                num_scalar_prefetch=1,
                grid=(self.key_heads,),
                in_specs=[
                    pl.BlockSpec((rows, wide), by_head),
                    pl.BlockSpec((rows, size), lambda h, p: (0, first_key + h)),
                    pl.BlockSpec((rows, size), whole),
                    pl.BlockSpec((rows, size), whole),
                    pl.BlockSpec((1, size), whole),
                    pl.BlockSpec((1, size), whole),
                    pl.BlockSpec((rows, wide), by_head),
                    pl.BlockSpec((rows, size), by_head),
                    pl.BlockSpec((rows, size), by_head),
                    pl.BlockSpec((1, group, rows), lambda h, p: (h, 0, 0)),
                    pl.BlockSpec((rows, wide), by_head),
                ],
                out_specs=[
                    pl.BlockSpec((rows, columns), whole),
                    pl.BlockSpec((1, size), whole),
                    pl.BlockSpec((1, size), whole),
                ],
                scratch_shapes=[
                    pltpu.VMEM((rows, size), jnp.float32),
                    pltpu.VMEM((rows, size), jnp.float32),
                ],
            ),
            out_shape=[
                jax.ShapeDtypeStruct((rows, columns), jnp.bfloat16),
                jax.ShapeDtypeStruct((1, size), jnp.float32),
                jax.ShapeDtypeStruct((1, size), jnp.float32),
            ],
        )(
            place, raw, raw, cosine, sine, query_gain[None, :], key_gain[None, :],
            query, key, value, totals, upstream,
        )


def shards(
    links,
    tokens,
    positions,
    input_gain,
    middle_gain,
    query_gain,
    key_gain,
    query_weight,
    key_matrix,
    value_matrix,
    output_weight,
    gate_weight,
    up_weight,
    down_weight,
    layer_cotangent,
):
    head_size = query_gain.shape[0]
    query_heads = query_weight.shape[1] // head_size
    key_heads = key_matrix.shape[1] // head_size
    query_width = query_heads * head_size
    key_width = key_heads * head_size
    group_rows = positions.shape[0]
    assert group_rows == SEQUENCE_LENGTH
    attention = Attention(group_rows, head_size, query_heads, key_heads, links.tensor_size)
    place = lax.axis_index("tensor").astype(jnp.int32)[None]
    hidden = gate_weight.shape[1]
    wide_mixing = links.gather_weight(
        jnp.concatenate([query_weight, key_matrix, value_matrix, output_weight], axis=1)
    )
    wide_attention = wide_mixing[:, : query_width + 2 * key_width]
    wide_output = wide_mixing[:, query_width + 2 * key_width :]
    wide_feed = links.gather_weight(jnp.concatenate([gate_weight, up_weight], axis=1))
    wide_down = links.gather_weight(down_weight)

    positions = links.relative_tokens(positions)
    inputs = tokens.astype(jnp.float32)
    inverse_in = inverse_rms(inputs)
    scaled_in = inputs * inverse_in
    normed_rows = links.gather_tokens((scaled_in * input_gain).astype(jnp.bfloat16))
    own_cotangent = layer_cotangent
    cotangent_first = links.gather_first(own_cotangent)
    normed_rows, cotangent_first = lax.optimization_barrier((normed_rows, cotangent_first))
    cotangent = links.gather_second(own_cotangent, cotangent_first)

    cosine, sine = tables(positions, head_size)
    raw_rows = matmul(normed_rows, wide_attention)
    query_rows, key_rows, value_rows, attended_rows, log_totals = attention.forward(
        place, raw_rows, cosine, sine, query_gain, key_gain
    )
    attended_rows, cotangent = lax.optimization_barrier((attended_rows, cotangent))
    branch_partial = contract_last(attended_rows, wide_output).astype(jnp.bfloat16)
    branch_first = links.scatter_first(branch_partial)
    branch = links.scatter_second(branch_partial, branch_first)
    middle = inputs + branch
    inverse_mid = inverse_rms(middle)
    scaled_mid = middle * inverse_mid
    normed_middle = links.gather_tokens((scaled_mid * middle_gain).astype(jnp.bfloat16))
    feed = matmul(normed_middle, wide_feed)
    gating, upward = feed[:, :hidden], feed[:, hidden:]
    gate_sigmoid = jax.nn.sigmoid(gating)
    silu_gate = gating * gate_sigmoid
    active = (silu_gate * upward).astype(jnp.bfloat16)
    down_term = contract_first(cotangent, active).astype(jnp.bfloat16)
    active, down_term = lax.optimization_barrier((active, down_term))
    down_sum = links.scatter_weight(down_term)
    cotangent, down_term = lax.optimization_barrier((cotangent, down_term))
    active_grad = matmul(cotangent, wide_down)
    gate_grad = (
        active_grad * upward * gate_sigmoid * (1.0 + gating * (1.0 - gate_sigmoid))
    ).astype(jnp.bfloat16)
    upward_grad = (active_grad * silu_gate).astype(jnp.bfloat16)
    feed_grad = jnp.concatenate([gate_grad, upward_grad], axis=1)
    middle_partial = contract_last(feed_grad, wide_feed)
    middle_partial = middle_partial.astype(jnp.bfloat16)
    feed_grad, middle_partial = lax.optimization_barrier((feed_grad, middle_partial))
    middle_first = links.scatter_first(middle_partial)
    feed_term = contract_first(normed_middle, feed_grad).astype(jnp.bfloat16)
    feed_term, middle_first, down_sum = lax.optimization_barrier(
        (feed_term, middle_first, down_sum)
    )
    feed_sum = links.scatter_weight(feed_term)
    middle_normed_grad = links.scatter_second(middle_partial, middle_first)
    feed_partial = contract_last(active, wide_down).astype(jnp.bfloat16)
    middle_normed_grad, feed_partial = lax.optimization_barrier((middle_normed_grad, feed_partial))
    middle_gain_term = jnp.sum(middle_normed_grad * scaled_mid, axis=0)
    middle_grad = own_cotangent.astype(jnp.float32) + norm_backward(
        middle_normed_grad, scaled_mid, inverse_mid, middle_gain
    )
    branch_grad = links.gather_tokens(middle_grad.astype(jnp.bfloat16))
    feed_partial, branch_grad = lax.optimization_barrier((feed_partial, branch_grad))
    feed_first = links.scatter_first(feed_partial)
    output_term = contract_first(branch_grad, attended_rows).astype(jnp.bfloat16)
    branch_grad, output_term = lax.optimization_barrier((branch_grad, output_term))
    attended_grad = matmul(branch_grad, wide_output).astype(jnp.bfloat16)
    raw_grad, query_gain_term, key_gain_term = attention.backward(
        place,
        raw_rows,
        cosine,
        sine,
        query_gain,
        key_gain,
        query_rows,
        key_rows,
        value_rows,
        log_totals,
        attended_grad,
    )
    raw_grad, feed_first = lax.optimization_barrier((raw_grad, feed_first))
    attention_term = contract_first(normed_rows, raw_grad).astype(jnp.bfloat16)
    feed_first, attention_term = lax.optimization_barrier((feed_first, attention_term))
    feed_branch = links.scatter_second(feed_partial, feed_first)
    raw_grad, attention_term = lax.optimization_barrier((raw_grad, attention_term))
    input_partial = contract_last(raw_grad, wide_attention).astype(jnp.bfloat16)
    mixing_term = jnp.concatenate([attention_term, output_term], axis=1)
    mixing_term, feed_sum, feed_branch, input_partial = lax.optimization_barrier(
        (mixing_term, feed_sum, feed_branch, input_partial)
    )
    mixing_sum = links.scatter_weight(mixing_term)
    input_first = links.scatter_first(input_partial)
    input_gain_term = (
        jnp.sum(input_partial.astype(jnp.float32) * normed_rows.astype(jnp.float32), axis=0)
        / input_gain
    )
    terms = jnp.concatenate(
        [input_gain_term, middle_gain_term, query_gain_term[0], key_gain_term[0]]
    )
    input_normed_grad = links.scatter_second(input_partial, input_first)
    terms, input_normed_grad = lax.optimization_barrier((terms, input_normed_grad))
    layer_output = middle + feed_branch
    tokens_grad = middle_grad + norm_backward(input_normed_grad, scaled_in, inverse_in, input_gain)
    terms = links.total_dp(links.total_tensor(terms))
    width = tokens.shape[1]
    feed_sum = feed_sum.astype(jnp.float32)
    query_sum, key_sum, value_sum, output_sum = split_columns(
        mixing_sum, (query_width, key_width, key_width, query_width)
    )
    return (
        layer_output,
        tokens_grad,
        terms[:width],
        terms[width : 2 * width],
        terms[2 * width : 2 * width + head_size],
        terms[2 * width + head_size :],
        query_sum,
        key_sum,
        value_sum,
        output_sum,
        feed_sum[:, :hidden],
        feed_sum[:, hidden:],
        down_sum.astype(jnp.float32),
    )


def solution(mesh):
    links = Links(mesh.shape["dp"], mesh.shape["tensor"])
    placed = (
        P(("dp", "tensor"), None),
        P("dp"),
        P(),
        P(),
        P(),
        P(),
        P("dp", "tensor"),
        P("dp", "tensor"),
        P("dp", "tensor"),
        P("dp", "tensor"),
        P("dp", "tensor"),
        P("dp", "tensor"),
        P("dp", "tensor"),
        P(("dp", "tensor"), None),
    )
    return jax.shard_map(
        lambda *arrays: shards(links, *arrays),
        mesh=mesh,
        in_specs=placed,
        out_specs=(
            P(("dp", "tensor"), None),
            P(("dp", "tensor"), None),
            P(),
            P(),
            P(),
            P(),
            P("dp", "tensor"),
            P("dp", "tensor"),
            P("dp", "tensor"),
            P("dp", "tensor"),
            P("dp", "tensor"),
            P("dp", "tensor"),
            P("dp", "tensor"),
        ),
        check_vma=False,
    )
```

```python
import math

import jax
import jax.numpy as jnp
from jax import lax
from jax.experimental import pallas as pl
from jax.experimental.pallas import tpu as pltpu
from jax.sharding import PartitionSpec as P

SEQUENCE_LENGTH = 1024


epsilon = 1e-06
masked = -1e30


def matmul(left, right):
    return jnp.dot(left, right, preferred_element_type=jnp.float32)


def contract_first(left, right):
    return lax.dot_general(
        left, right, (((0,), (0,)), ((), ())), preferred_element_type=jnp.float32
    )


def weight_term(left, right):
    return lax.dot_general(
        left, right, (((0, 1), (0, 1)), ((), ())), preferred_element_type=jnp.float32
    ).astype(jnp.bfloat16)


def contract_last(left, right):
    return lax.dot_general(
        left, right, (((1,), (1,)), ((), ())), preferred_element_type=jnp.float32
    )


def tables(positions, width):
    frequency = jnp.exp(
        jnp.arange(width // 2, dtype=jnp.float32) * (-2.0 * math.log(1000000.0) / width)
    )
    angles = positions.astype(jnp.float32)[:, None] * frequency[None, :]
    cosine = jnp.cos(angles)
    sine = jnp.sin(angles)
    return (
        jnp.concatenate([cosine, cosine], axis=-1),
        jnp.concatenate([-sine, sine], axis=-1),
    )


def inverse_rms(value_rows):
    return lax.rsqrt(jnp.mean(value_rows * value_rows, axis=-1, keepdims=True) + epsilon)


def norm_backward(upstream, scaled, inverse, gain):
    inner = upstream * gain
    return inverse * (inner - scaled * jnp.mean(inner * scaled, axis=-1, keepdims=True))


class Links:
    def __init__(self, dp_size, tensor_size):
        self.dp_size = dp_size
        self.tensor_size = tensor_size
        self.chips = dp_size // 2
        self.swap = [(place, place ^ 1) for place in range(dp_size)]

    def shifted(self, value, step):
        return lax.ppermute(
            value,
            "dp",
            [
                (2 * chip + core, 2 * ((chip + step) % self.chips) + core)
                for chip in range(self.chips)
                for core in range(2)
            ],
        )

    def other_core(self, value):
        return lax.ppermute(value, "dp", self.swap)

    def across(self, value, bit):
        return lax.ppermute(
            value, "tensor", [(place, place ^ bit) for place in range(self.tensor_size)]
        )

    def relative_tokens(self, values):
        count = values.shape[0] // self.tensor_size
        place = lax.axis_index("tensor")
        return jnp.concatenate(
            [
                lax.dynamic_slice_in_dim(values, (place ^ other) * count, count, 0)
                for other in range(self.tensor_size)
            ],
            axis=0,
        )

    def gather_first(self, block):
        if self.tensor_size != 4:
            return block, block
        return lax.optimization_barrier((self.across(block, 1), self.across(block, 2)))

    def gather_second(self, block, first):
        if self.tensor_size != 4:
            bit = 1
            while bit < self.tensor_size:
                block = jnp.concatenate([block, self.across(block, bit)], axis=0)
                bit *= 2
            return block
        half = block.shape[0] // 2
        by_x, by_y = first
        corner_low, corner_high = lax.optimization_barrier(
            (self.across(by_y[:half], 1), self.across(by_x[half:], 2))
        )
        return jnp.concatenate([block, by_x, by_y, corner_low, corner_high], axis=0)

    def gather_tokens(self, block):
        return self.gather_second(block, self.gather_first(block))

    def scatter_tokens(self, partial):
        return self.scatter_second(partial, self.scatter_first(partial))

    def half_block(self, partial, block, high):
        half = partial.shape[0] // (2 * self.tensor_size)
        start = 2 * block * half + high * half
        return partial[start : start + half]

    def first_sends(self, partial):
        return (
            self.across(self.half_block(partial, 3, 0), 1),
            self.across(self.half_block(partial, 3, 1), 2),
            self.across(self.half_block(partial, 1, 0), 1),
            self.across(self.half_block(partial, 2, 1), 2),
        )

    def last_sends(self, partial, first):
        def passed(block, high, arrived):
            total = self.half_block(partial, block, high).astype(jnp.float32)
            return (total + arrived.astype(jnp.float32)).astype(partial.dtype)

        return (
            self.across(passed(2, 0, first[0]), 2),
            self.across(passed(1, 1, first[1]), 1),
        )

    def combined(self, partial, first, last):
        return jnp.concatenate(
            [
                self.half_block(partial, 0, high).astype(jnp.float32)
                + first[2 + high].astype(jnp.float32)
                + last[high].astype(jnp.float32)
                for high in range(2)
            ],
            axis=0,
        )

    def scatter_first(self, partial):
        if self.tensor_size != 4:
            return (partial,)
        return lax.optimization_barrier(self.first_sends(partial))

    def scatter_second(self, partial, first):
        if self.tensor_size != 4:
            (partial,) = first
            bit = self.tensor_size // 2
            while bit:
                middle = partial.shape[0] // 2
                arrived = self.across(partial[middle:], bit).astype(jnp.float32)
                total = partial[:middle].astype(jnp.float32) + arrived
                partial = total.astype(partial.dtype)
                bit //= 2
            return total
        last = lax.optimization_barrier(self.last_sends(partial, first))
        return self.combined(partial, first, last)

    def scatter_beside(self, partial, terms):
        if self.tensor_size != 4:
            return self.scatter_tokens(partial), self.total_tensor(terms)
        first, arrived = lax.optimization_barrier(
            (self.first_sends(partial), self.across(terms, 1))
        )
        terms = terms + arrived
        last, arrived = lax.optimization_barrier(
            (self.last_sends(partial, first), self.across(terms, 2))
        )
        return self.combined(partial, first, last), terms + arrived

    def gather_weight(self, shard):
        return lax.all_gather(shard, "dp", axis=0, tiled=True)

    def core_columns(self, rows, core):
        width = rows.shape[1] // self.dp_size
        return jnp.concatenate(
            [
                lax.dynamic_slice_in_dim(rows, (2 * chip + core) * width, width, 1)
                for chip in range(self.chips)
            ],
            axis=1,
        )

    def both_cores(self, rows):
        return jnp.stack([rows, self.other_core(rows)])

    def both_columns(self, rows):
        core = lax.axis_index("dp") % 2
        theirs = self.other_core(self.core_columns(rows, core ^ 1))
        return jnp.stack([self.core_columns(rows, core), theirs])

    def scatter_weight(self, partial):
        return lax.psum_scatter(partial, "dp", scatter_dimension=0, tiled=True)

    def scatter_chips(self, partial):
        groups = [list(range(core, self.dp_size, 2)) for core in range(2)]
        return lax.psum_scatter(
            partial, "dp", scatter_dimension=0, tiled=True, axis_index_groups=groups
        )

    def total_tensor(self, value):
        bit = 1
        while bit < self.tensor_size:
            value = value + self.across(value, bit)
            bit *= 2
        return value

    def total_dp(self, value):
        chip = lax.axis_index("dp") // 2
        value = value + self.other_core(value)
        parts = jnp.stack([value] + [self.shifted(value, step) for step in range(1, self.chips)])
        total = None
        for target in range(self.chips):
            part = lax.dynamic_index_in_dim(parts, (chip - target) % self.chips, 0, keepdims=False)
            total = part if total is None else total + part
        return total


def product(left, right, left_axis, right_axis):
    return lax.dot_general(
        left,
        right,
        (((left_axis,), (right_axis,)), ((), ())),
        preferred_element_type=jnp.float32,
    )


def split_columns(rows, widths):
    def kernel(source, *targets):
        start = 0
        for target in targets:
            width = target.shape[1]
            target[...] = source[:, start : start + width].astype(jnp.float32)
            start += width

    return pl.pallas_call(
        kernel,
        name="split_columns",
        out_shape=[jax.ShapeDtypeStruct((rows.shape[0], width), jnp.float32) for width in widths],
    )(rows)


class Attention:
    def __init__(self, rows, head_size, query_heads, key_heads, blocks):
        self.rows = rows
        self.head_size = head_size
        self.query_heads = query_heads
        self.key_heads = key_heads
        self.grouping = query_heads // key_heads
        self.blocks = blocks
        self.block = rows // blocks
        self.scale = head_size ** (-0.5)

    def cost(self, products):
        scores = self.query_heads * self.rows * self.rows
        return pl.CostEstimate(
            flops=products * 2 * scores * 2 * self.head_size,
            transcendentals=scores,
            bytes_accessed=16 * self.query_heads * self.rows * self.head_size,
        )

    def outside(self, place, index):
        return pl.ds(pl.multiple_of((index ^ place) * self.block, self.block), self.block)

    def inside(self, index):
        return slice(index * self.block, (index + 1) * self.block)

    def head(self, index):
        return slice(index * self.head_size, (index + 1) * self.head_size)

    def turn(self, rows):
        return pltpu.roll(rows, self.head_size // 2, axis=1)

    def forward_kernel(
        self, place_ref, raw_query, raw_key, raw_value, cosine, sine, query_gain, key_gain,
        query, key, value, attended, totals,
    ):
        place = place_ref[0]

        def prepared(raw, gain, where):
            normed = raw * inverse_rms(raw) * gain
            turned = normed * cosine[where, :] + self.turn(normed) * sine[where, :]
            return turned.astype(jnp.bfloat16)

        for index in range(self.blocks):
            there, here = self.outside(place, index), self.inside(index)
            key[here, :] = prepared(raw_key[there, :], key_gain[...], there)
            value[here, :] = raw_value[there, :].astype(jnp.bfloat16)
            for member in range(self.grouping):
                query[here, self.head(member)] = prepared(
                    raw_query[there, self.head(member)], query_gain[...], there
                )
        for member in range(self.grouping):
            for index in range(self.blocks):
                span = (index + 1) * self.block
                scores = self.scale * product(
                    query[self.inside(index), self.head(member)], key[:span, :], 1, 1
                )
                row = index * self.block + lax.broadcasted_iota(jnp.int32, scores.shape, 0)
                column = lax.broadcasted_iota(jnp.int32, scores.shape, 1)
                scores = jnp.where(column <= row, scores, masked)
                highest = jnp.max(scores, axis=1, keepdims=True)
                powers = jnp.exp(scores - highest)
                total = jnp.sum(powers, axis=1, keepdims=True)
                shares = (powers * (1.0 / total)).astype(jnp.bfloat16)
                attended[self.outside(place, index), self.head(member)] = product(
                    shares, value[:span, :], 1, 0
                ).astype(jnp.bfloat16)
                log_total = jnp.broadcast_to(
                    highest + jnp.log(total), (self.block, self.head_size)
                )
                totals[0, member : member + 1, self.inside(index)] = log_total.T[:1, :]

    def forward(self, place, raw, cosine, sine, query_gain, key_gain):
        rows, size, group = self.rows, self.head_size, self.grouping
        wide = group * size
        first_key, first_value = self.query_heads, self.query_heads + self.key_heads
        whole = lambda h, p: (0, 0)
        by_head = lambda h, p: (0, h)
        low = jnp.bfloat16
        return pl.pallas_call(
            self.forward_kernel,
            name="attention_forward",
            cost_estimate=self.cost(2),
            grid_spec=pltpu.PrefetchScalarGridSpec(
                num_scalar_prefetch=1,
                grid=(self.key_heads,),
                in_specs=[
                    pl.BlockSpec((rows, wide), by_head),
                    pl.BlockSpec((rows, size), lambda h, p: (0, first_key + h)),
                    pl.BlockSpec((rows, size), lambda h, p: (0, first_value + h)),
                    pl.BlockSpec((rows, size), whole),
                    pl.BlockSpec((rows, size), whole),
                    pl.BlockSpec((1, size), whole),
                    pl.BlockSpec((1, size), whole),
                ],
                out_specs=[
                    pl.BlockSpec((rows, wide), by_head),
                    pl.BlockSpec((rows, size), by_head),
                    pl.BlockSpec((rows, size), by_head),
                    pl.BlockSpec((rows, wide), by_head),
                    pl.BlockSpec((1, group, rows), lambda h, p: (h, 0, 0)),
                ],
            ),
            out_shape=[
                jax.ShapeDtypeStruct((rows, self.query_heads * size), low),
                jax.ShapeDtypeStruct((rows, self.key_heads * size), low),
                jax.ShapeDtypeStruct((rows, self.key_heads * size), low),
                jax.ShapeDtypeStruct((rows, self.query_heads * size), low),
                jax.ShapeDtypeStruct((self.key_heads, group, rows), jnp.float32),
            ],
        )(place, raw, raw, raw, cosine, sine, query_gain[None, :], key_gain[None, :])

    def backward_kernel(
        self, place_ref, raw_query, raw_key, cosine, sine, query_gain, key_gain,
        query, key, value, totals, upstream,
        raw_grad, query_gain_grad, key_gain_grad, key_total, value_total,
    ):
        place = place_ref[0]
        current = pl.program_id(0)
        size, group = self.head_size, self.grouping

        @pl.when(current == 0)
        def _():
            query_gain_grad[...] = jnp.zeros_like(query_gain_grad)
            key_gain_grad[...] = jnp.zeros_like(key_gain_grad)

        def store(where, head, grad):
            column = pl.multiple_of(head * size, size)
            raw_grad[where, pl.ds(column, size)] = grad.astype(jnp.bfloat16)

        def through_norm(raw, grad, gain, where, gain_grad):
            inverse = inverse_rms(raw)
            scaled = raw * inverse
            normed_grad = grad * cosine[where, :] - self.turn(grad) * sine[where, :]
            gain_grad[...] += jnp.sum(normed_grad * scaled, axis=0, keepdims=True)
            return norm_backward(normed_grad, scaled, inverse, gain)

        for member in range(group):
            for index in reversed(range(self.blocks)):
                here, there = self.inside(index), self.outside(place, index)
                span = (index + 1) * self.block
                query_block = query[here, self.head(member)]
                grad_block = upstream[there, self.head(member)]
                scores = self.scale * product(key[:span, :], query_block, 1, 1)
                row = index * self.block + lax.broadcasted_iota(jnp.int32, scores.shape, 1)
                column = lax.broadcasted_iota(jnp.int32, scores.shape, 0)
                scores = jnp.where(column <= row, scores, masked)
                shares = jnp.exp(scores - totals[0, member : member + 1, here])
                share_grad = product(value[:span, :], grad_block, 1, 1)
                inner = jnp.sum(share_grad * shares, axis=0, keepdims=True)
                score_grad = (shares * (share_grad - inner)).astype(jnp.bfloat16)
                value_part = product(shares.astype(jnp.bfloat16), grad_block, 1, 0)
                key_part = product(score_grad, query_block, 1, 0)
                if member == 0 and index == self.blocks - 1:
                    value_total[...] = value_part
                    key_total[...] = key_part
                else:
                    value_total[:span, :] += value_part
                    key_total[:span, :] += key_part
                query_grad = self.scale * product(score_grad, key[:span, :], 0, 0)
                store(
                    there,
                    current * group + member,
                    through_norm(
                        raw_query[there, self.head(member)],
                        query_grad,
                        query_gain[...],
                        there,
                        query_gain_grad,
                    ),
                )
        for index in range(self.blocks):
            here, there = self.inside(index), self.outside(place, index)
            store(
                there,
                self.query_heads + current,
                through_norm(
                    raw_key[there, :],
                    self.scale * key_total[here, :],
                    key_gain[...],
                    there,
                    key_gain_grad,
                ),
            )
            store(there, self.query_heads + self.key_heads + current, value_total[here, :])

    def backward(
        self, place, raw, cosine, sine, query_gain, key_gain, query, key, value, totals, upstream
    ):
        rows, size, group = self.rows, self.head_size, self.grouping
        wide = group * size
        first_key = self.query_heads
        whole = lambda h, p: (0, 0)
        by_head = lambda h, p: (0, h)
        columns = (self.query_heads + 2 * self.key_heads) * size
        return pl.pallas_call(
            self.backward_kernel,
            name="attention_backward",
            cost_estimate=self.cost(5),
            grid_spec=pltpu.PrefetchScalarGridSpec(
                num_scalar_prefetch=1,
                grid=(self.key_heads,),
                in_specs=[
                    pl.BlockSpec((rows, wide), by_head),
                    pl.BlockSpec((rows, size), lambda h, p: (0, first_key + h)),
                    pl.BlockSpec((rows, size), whole),
                    pl.BlockSpec((rows, size), whole),
                    pl.BlockSpec((1, size), whole),
                    pl.BlockSpec((1, size), whole),
                    pl.BlockSpec((rows, wide), by_head),
                    pl.BlockSpec((rows, size), by_head),
                    pl.BlockSpec((rows, size), by_head),
                    pl.BlockSpec((1, group, rows), lambda h, p: (h, 0, 0)),
                    pl.BlockSpec((rows, wide), by_head),
                ],
                out_specs=[
                    pl.BlockSpec((rows, columns), whole),
                    pl.BlockSpec((1, size), whole),
                    pl.BlockSpec((1, size), whole),
                ],
                scratch_shapes=[
                    pltpu.VMEM((rows, size), jnp.float32),
                    pltpu.VMEM((rows, size), jnp.float32),
                ],
            ),
            out_shape=[
                jax.ShapeDtypeStruct((rows, columns), jnp.bfloat16),
                jax.ShapeDtypeStruct((1, size), jnp.float32),
                jax.ShapeDtypeStruct((1, size), jnp.float32),
            ],
        )(
            place, raw, raw, cosine, sine, query_gain[None, :], key_gain[None, :],
            query, key, value, totals, upstream,
        )


def shards(
    links,
    tokens,
    positions,
    input_gain,
    middle_gain,
    query_gain,
    key_gain,
    query_weight,
    key_matrix,
    value_matrix,
    output_weight,
    gate_weight,
    up_weight,
    down_weight,
    layer_cotangent,
):
    head_size = query_gain.shape[0]
    query_heads = query_weight.shape[1] // head_size
    key_heads = key_matrix.shape[1] // head_size
    query_width = query_heads * head_size
    key_width = key_heads * head_size
    group_rows = positions.shape[0]
    assert group_rows == SEQUENCE_LENGTH
    attention = Attention(group_rows, head_size, query_heads, key_heads, links.tensor_size)
    place = lax.axis_index("tensor").astype(jnp.int32)[None]
    hidden = gate_weight.shape[1]
    wide_mixing = links.gather_weight(
        jnp.concatenate([query_weight, key_matrix, value_matrix, output_weight], axis=1)
    )
    wide_attention = wide_mixing[:, : query_width + 2 * key_width]
    wide_output = wide_mixing[:, query_width + 2 * key_width :]
    wide_feed = links.gather_weight(jnp.concatenate([gate_weight, up_weight], axis=1))
    wide_down = links.gather_weight(down_weight)

    positions = links.relative_tokens(positions)
    inputs = tokens.astype(jnp.float32)
    inverse_in = inverse_rms(inputs)
    scaled_in = inputs * inverse_in
    normed_rows = links.gather_tokens((scaled_in * input_gain).astype(jnp.bfloat16))
    own_cotangent = layer_cotangent
    cotangent_first = links.gather_first(own_cotangent)
    normed_rows, cotangent_first = lax.optimization_barrier((normed_rows, cotangent_first))
    cotangent = links.gather_second(own_cotangent, cotangent_first)

    cosine, sine = tables(positions, head_size)
    raw_rows = matmul(normed_rows, wide_attention)
    query_rows, key_rows, value_rows, attended_rows, log_totals = attention.forward(
        place, raw_rows, cosine, sine, query_gain, key_gain
    )
    attended_rows, cotangent = lax.optimization_barrier((attended_rows, cotangent))
    branch_partial = contract_last(attended_rows, wide_output).astype(jnp.bfloat16)
    branch_first = links.scatter_first(branch_partial)
    branch = links.scatter_second(branch_partial, branch_first)
    middle = inputs + branch
    inverse_mid = inverse_rms(middle)
    scaled_mid = middle * inverse_mid
    normed_middle = links.gather_tokens((scaled_mid * middle_gain).astype(jnp.bfloat16))
    feed = matmul(normed_middle, wide_feed)
    gating, upward = feed[:, :hidden], feed[:, hidden:]
    gate_sigmoid = jax.nn.sigmoid(gating)
    silu_gate = gating * gate_sigmoid
    active = (silu_gate * upward).astype(jnp.bfloat16)
    down_term = contract_first(cotangent, active).astype(jnp.bfloat16)
    active, down_term = lax.optimization_barrier((active, down_term))
    down_sum = links.scatter_weight(down_term)
    cotangent, down_term = lax.optimization_barrier((cotangent, down_term))
    active_grad = matmul(cotangent, wide_down)
    gate_grad = (
        active_grad * upward * gate_sigmoid * (1.0 + gating * (1.0 - gate_sigmoid))
    ).astype(jnp.bfloat16)
    upward_grad = (active_grad * silu_gate).astype(jnp.bfloat16)
    feed_grad = jnp.concatenate([gate_grad, upward_grad], axis=1)
    middle_partial = contract_last(feed_grad, wide_feed)
    middle_partial = middle_partial.astype(jnp.bfloat16)
    feed_grad, middle_partial = lax.optimization_barrier((feed_grad, middle_partial))
    middle_first = links.scatter_first(middle_partial)
    feed_term = contract_first(normed_middle, feed_grad).astype(jnp.bfloat16)
    feed_term, middle_first, down_sum = lax.optimization_barrier(
        (feed_term, middle_first, down_sum)
    )
    feed_sum = links.scatter_weight(feed_term)
    middle_normed_grad = links.scatter_second(middle_partial, middle_first)
    feed_partial = contract_last(active, wide_down).astype(jnp.bfloat16)
    middle_normed_grad, feed_partial = lax.optimization_barrier((middle_normed_grad, feed_partial))
    middle_gain_term = jnp.sum(middle_normed_grad * scaled_mid, axis=0)
    middle_grad = own_cotangent.astype(jnp.float32) + norm_backward(
        middle_normed_grad, scaled_mid, inverse_mid, middle_gain
    )
    branch_grad = links.gather_tokens(middle_grad.astype(jnp.bfloat16))
    feed_partial, branch_grad = lax.optimization_barrier((feed_partial, branch_grad))
    feed_first = links.scatter_first(feed_partial)
    attended_grad = matmul(branch_grad, wide_output).astype(jnp.bfloat16)
    raw_grad, query_gain_term, key_gain_term = attention.backward(
        place,
        raw_rows,
        cosine,
        sine,
        query_gain,
        key_gain,
        query_rows,
        key_rows,
        value_rows,
        log_totals,
        attended_grad,
    )
    raw_grad, feed_first, branch_grad = lax.optimization_barrier(
        (raw_grad, feed_first, branch_grad)
    )
    output_term = weight_term(links.both_columns(branch_grad), links.both_cores(attended_rows))
    attention_term = weight_term(links.both_columns(normed_rows), links.both_cores(raw_grad))
    feed_first, attention_term = lax.optimization_barrier((feed_first, attention_term))
    feed_branch = links.scatter_second(feed_partial, feed_first)
    raw_grad, attention_term = lax.optimization_barrier((raw_grad, attention_term))
    input_partial = contract_last(raw_grad, wide_attention).astype(jnp.bfloat16)
    mixing_term = jnp.concatenate([attention_term, output_term], axis=1)
    input_gain_term = (
        jnp.sum(input_partial.astype(jnp.float32) * normed_rows.astype(jnp.float32), axis=0)
        / input_gain
    )
    terms = jnp.concatenate(
        [input_gain_term, middle_gain_term, query_gain_term[0], key_gain_term[0]]
    )
    mixing_term, feed_sum, feed_branch, input_partial, terms = lax.optimization_barrier(
        (mixing_term, feed_sum, feed_branch, input_partial, terms)
    )
    mixing_sum = links.scatter_chips(mixing_term)
    input_normed_grad, terms = links.scatter_beside(input_partial, terms)
    layer_output = middle + feed_branch
    tokens_grad = middle_grad + norm_backward(input_normed_grad, scaled_in, inverse_in, input_gain)
    terms = links.total_dp(terms)
    width = tokens.shape[1]
    feed_sum = feed_sum.astype(jnp.float32)
    query_sum, key_sum, value_sum, output_sum = split_columns(
        mixing_sum, (query_width, key_width, key_width, query_width)
    )
    return (
        layer_output,
        tokens_grad,
        terms[:width],
        terms[width : 2 * width],
        terms[2 * width : 2 * width + head_size],
        terms[2 * width + head_size :],
        query_sum,
        key_sum,
        value_sum,
        output_sum,
        feed_sum[:, :hidden],
        feed_sum[:, hidden:],
        down_sum.astype(jnp.float32),
    )


def solution(mesh):
    links = Links(mesh.shape["dp"], mesh.shape["tensor"])
    placed = (
        P(("dp", "tensor"), None),
        P("dp"),
        P(),
        P(),
        P(),
        P(),
        P("dp", "tensor"),
        P("dp", "tensor"),
        P("dp", "tensor"),
        P("dp", "tensor"),
        P("dp", "tensor"),
        P("dp", "tensor"),
        P("dp", "tensor"),
        P(("dp", "tensor"), None),
    )
    return jax.shard_map(
        lambda *arrays: shards(links, *arrays),
        mesh=mesh,
        in_specs=placed,
        out_specs=(
            P(("dp", "tensor"), None),
            P(("dp", "tensor"), None),
            P(),
            P(),
            P(),
            P(),
            P("dp", "tensor"),
            P("dp", "tensor"),
            P("dp", "tensor"),
            P("dp", "tensor"),
            P("dp", "tensor"),
            P("dp", "tensor"),
            P("dp", "tensor"),
        ),
        check_vma=False,
    )
```

```python
import math

import jax
import jax.numpy as jnp
from jax import lax
from jax.experimental import pallas as pl
from jax.experimental.pallas import tpu as pltpu
from jax.sharding import PartitionSpec as P

SEQUENCE_LENGTH = 1024


epsilon = 1e-06
masked = -1e30


def matmul(left, right):
    return jnp.dot(left, right, preferred_element_type=jnp.float32)


def contract_first(left, right):
    return lax.dot_general(
        left, right, (((0,), (0,)), ((), ())), preferred_element_type=jnp.float32
    )


def weight_term(left, right):
    return lax.dot_general(
        left, right, (((0, 1), (0, 1)), ((), ())), preferred_element_type=jnp.float32
    ).astype(jnp.bfloat16)


def contract_last(left, right):
    return lax.dot_general(
        left, right, (((1,), (1,)), ((), ())), preferred_element_type=jnp.float32
    )


def tables(positions, width):
    frequency = jnp.exp(
        jnp.arange(width // 2, dtype=jnp.float32) * (-2.0 * math.log(1000000.0) / width)
    )
    angles = positions.astype(jnp.float32)[:, None] * frequency[None, :]
    cosine = jnp.cos(angles)
    sine = jnp.sin(angles)
    return (
        jnp.concatenate([cosine, cosine], axis=-1),
        jnp.concatenate([-sine, sine], axis=-1),
    )


def inverse_rms(value_rows):
    return lax.rsqrt(jnp.mean(value_rows * value_rows, axis=-1, keepdims=True) + epsilon)


def norm_backward(upstream, scaled, inverse, gain):
    inner = upstream * gain
    return inverse * (inner - scaled * jnp.mean(inner * scaled, axis=-1, keepdims=True))


class Links:
    def __init__(self, dp_size, tensor_size):
        self.dp_size = dp_size
        self.tensor_size = tensor_size
        self.chips = dp_size // 2
        self.swap = [(place, place ^ 1) for place in range(dp_size)]

    def shifted(self, value, step):
        return lax.ppermute(
            value,
            "dp",
            [
                (2 * chip + core, 2 * ((chip + step) % self.chips) + core)
                for chip in range(self.chips)
                for core in range(2)
            ],
        )

    def other_core(self, value):
        return lax.ppermute(value, "dp", self.swap)

    def across(self, value, bit):
        return lax.ppermute(
            value, "tensor", [(place, place ^ bit) for place in range(self.tensor_size)]
        )

    def relative_tokens(self, values):
        count = values.shape[0] // self.tensor_size
        place = lax.axis_index("tensor")
        return jnp.concatenate(
            [
                lax.dynamic_slice_in_dim(values, (place ^ other) * count, count, 0)
                for other in range(self.tensor_size)
            ],
            axis=0,
        )

    def gather_first(self, block):
        if self.tensor_size != 4:
            return block, block
        return lax.optimization_barrier((self.across(block, 1), self.across(block, 2)))

    def gather_second(self, block, first):
        if self.tensor_size != 4:
            bit = 1
            while bit < self.tensor_size:
                block = jnp.concatenate([block, self.across(block, bit)], axis=0)
                bit *= 2
            return block
        half = block.shape[0] // 2
        by_x, by_y = first
        corner_low, corner_high = lax.optimization_barrier(
            (self.across(by_y[:half], 1), self.across(by_x[half:], 2))
        )
        return jnp.concatenate([block, by_x, by_y, corner_low, corner_high], axis=0)

    def gather_tokens(self, block):
        return self.gather_second(block, self.gather_first(block))

    def scatter_tokens(self, partial):
        return self.scatter_second(partial, self.scatter_first(partial))

    def half_block(self, partial, block, high):
        half = partial.shape[0] // (2 * self.tensor_size)
        start = 2 * block * half + high * half
        return partial[start : start + half]

    def first_sends(self, partial):
        return (
            self.across(self.half_block(partial, 3, 0), 1),
            self.across(self.half_block(partial, 3, 1), 2),
            self.across(self.half_block(partial, 1, 0), 1),
            self.across(self.half_block(partial, 2, 1), 2),
        )

    def last_sends(self, partial, first):
        def passed(block, high, arrived):
            total = self.half_block(partial, block, high).astype(jnp.float32)
            return (total + arrived.astype(jnp.float32)).astype(partial.dtype)

        return (
            self.across(passed(2, 0, first[0]), 2),
            self.across(passed(1, 1, first[1]), 1),
        )

    def combined(self, partial, first, last):
        return jnp.concatenate(
            [
                self.half_block(partial, 0, high).astype(jnp.float32)
                + first[2 + high].astype(jnp.float32)
                + last[high].astype(jnp.float32)
                for high in range(2)
            ],
            axis=0,
        )

    def scatter_first(self, partial):
        if self.tensor_size != 4:
            return (partial,)
        return lax.optimization_barrier(self.first_sends(partial))

    def scatter_second(self, partial, first):
        if self.tensor_size != 4:
            (partial,) = first
            bit = self.tensor_size // 2
            while bit:
                middle = partial.shape[0] // 2
                arrived = self.across(partial[middle:], bit).astype(jnp.float32)
                total = partial[:middle].astype(jnp.float32) + arrived
                partial = total.astype(partial.dtype)
                bit //= 2
            return total
        last = lax.optimization_barrier(self.last_sends(partial, first))
        return self.combined(partial, first, last)

    def scatter_beside(self, partial, terms):
        if self.tensor_size != 4:
            return self.scatter_tokens(partial), self.total_tensor(terms)
        first, arrived = lax.optimization_barrier(
            (self.first_sends(partial), self.across(terms, 1))
        )
        terms = terms + arrived
        last, arrived = lax.optimization_barrier(
            (self.last_sends(partial, first), self.across(terms, 2))
        )
        return self.combined(partial, first, last), terms + arrived

    def gather_weight(self, shard):
        return lax.all_gather(shard, "dp", axis=0, tiled=True)

    def core_columns(self, rows, core):
        width = rows.shape[1] // self.dp_size
        return jnp.concatenate(
            [
                lax.dynamic_slice_in_dim(rows, (2 * chip + core) * width, width, 1)
                for chip in range(self.chips)
            ],
            axis=1,
        )

    def both_cores(self, rows):
        return jnp.stack([rows, self.other_core(rows)])

    def both_columns(self, rows):
        core = lax.axis_index("dp") % 2
        theirs = self.other_core(self.core_columns(rows, core ^ 1))
        return jnp.stack([self.core_columns(rows, core), theirs])

    def scatter_weight(self, partial):
        return lax.psum_scatter(partial, "dp", scatter_dimension=0, tiled=True)

    def scatter_chips(self, partial):
        groups = [list(range(core, self.dp_size, 2)) for core in range(2)]
        return lax.psum_scatter(
            partial, "dp", scatter_dimension=0, tiled=True, axis_index_groups=groups
        )

    def total_tensor(self, value):
        bit = 1
        while bit < self.tensor_size:
            value = value + self.across(value, bit)
            bit *= 2
        return value

    def total_dp(self, value):
        chip = lax.axis_index("dp") // 2
        value = value + self.other_core(value)
        parts = jnp.stack([value] + [self.shifted(value, step) for step in range(1, self.chips)])
        total = None
        for target in range(self.chips):
            part = lax.dynamic_index_in_dim(parts, (chip - target) % self.chips, 0, keepdims=False)
            total = part if total is None else total + part
        return total


def product(left, right, left_axis, right_axis):
    return lax.dot_general(
        left,
        right,
        (((left_axis,), (right_axis,)), ((), ())),
        preferred_element_type=jnp.float32,
    )


def split_columns(rows, widths):
    def kernel(source, *targets):
        start = 0
        for target in targets:
            width = target.shape[1]
            target[...] = source[:, start : start + width].astype(jnp.float32)
            start += width

    return pl.pallas_call(
        kernel,
        name="split_columns",
        out_shape=[jax.ShapeDtypeStruct((rows.shape[0], width), jnp.float32) for width in widths],
    )(rows)


class Attention:
    def __init__(self, rows, head_size, query_heads, key_heads, blocks):
        self.rows = rows
        self.head_size = head_size
        self.query_heads = query_heads
        self.key_heads = key_heads
        self.grouping = query_heads // key_heads
        self.blocks = blocks
        self.block = rows // blocks
        self.scale = head_size ** (-0.5)

    def cost(self, products):
        scores = self.query_heads * self.rows * self.rows
        return pl.CostEstimate(
            flops=products * 2 * scores * 2 * self.head_size,
            transcendentals=scores,
            bytes_accessed=16 * self.query_heads * self.rows * self.head_size,
        )

    def outside(self, place, index):
        return pl.ds(pl.multiple_of((index ^ place) * self.block, self.block), self.block)

    def inside(self, index):
        return slice(index * self.block, (index + 1) * self.block)

    def head(self, index):
        return slice(index * self.head_size, (index + 1) * self.head_size)

    def turn(self, rows):
        return pltpu.roll(rows, self.head_size // 2, axis=1)

    def forward_kernel(
        self, place_ref, raw_query, raw_key, raw_value, cosine, sine, query_gain, key_gain,
        query, key, value, attended, totals,
    ):
        place = place_ref[0]

        def prepared(raw, gain, where):
            normed = raw * inverse_rms(raw) * gain
            turned = normed * cosine[where, :] + self.turn(normed) * sine[where, :]
            return turned.astype(jnp.bfloat16)

        for index in range(self.blocks):
            there, here = self.outside(place, index), self.inside(index)
            key[here, :] = prepared(raw_key[there, :], key_gain[...], there)
            value[here, :] = raw_value[there, :].astype(jnp.bfloat16)
            for member in range(self.grouping):
                query[here, self.head(member)] = prepared(
                    raw_query[there, self.head(member)], query_gain[...], there
                )
        for member in range(self.grouping):
            for index in range(self.blocks):
                span = (index + 1) * self.block
                scores = self.scale * product(
                    query[self.inside(index), self.head(member)], key[:span, :], 1, 1
                )
                row = index * self.block + lax.broadcasted_iota(jnp.int32, scores.shape, 0)
                column = lax.broadcasted_iota(jnp.int32, scores.shape, 1)
                scores = jnp.where(column <= row, scores, masked)
                highest = jnp.max(scores, axis=1, keepdims=True)
                powers = jnp.exp(scores - highest)
                total = jnp.sum(powers, axis=1, keepdims=True)
                shares = (powers * (1.0 / total)).astype(jnp.bfloat16)
                attended[self.outside(place, index), self.head(member)] = product(
                    shares, value[:span, :], 1, 0
                ).astype(jnp.bfloat16)
                log_total = jnp.broadcast_to(
                    highest + jnp.log(total), (self.block, self.head_size)
                )
                totals[0, member : member + 1, self.inside(index)] = log_total.T[:1, :]

    def forward(self, place, raw, cosine, sine, query_gain, key_gain):
        rows, size, group = self.rows, self.head_size, self.grouping
        wide = group * size
        first_key, first_value = self.query_heads, self.query_heads + self.key_heads
        whole = lambda h, p: (0, 0)
        by_head = lambda h, p: (0, h)
        low = jnp.bfloat16
        return pl.pallas_call(
            self.forward_kernel,
            name="attention_forward",
            cost_estimate=self.cost(2),
            grid_spec=pltpu.PrefetchScalarGridSpec(
                num_scalar_prefetch=1,
                grid=(self.key_heads,),
                in_specs=[
                    pl.BlockSpec((rows, wide), by_head),
                    pl.BlockSpec((rows, size), lambda h, p: (0, first_key + h)),
                    pl.BlockSpec((rows, size), lambda h, p: (0, first_value + h)),
                    pl.BlockSpec((rows, size), whole),
                    pl.BlockSpec((rows, size), whole),
                    pl.BlockSpec((1, size), whole),
                    pl.BlockSpec((1, size), whole),
                ],
                out_specs=[
                    pl.BlockSpec((rows, wide), by_head),
                    pl.BlockSpec((rows, size), by_head),
                    pl.BlockSpec((rows, size), by_head),
                    pl.BlockSpec((rows, wide), by_head),
                    pl.BlockSpec((1, group, rows), lambda h, p: (h, 0, 0)),
                ],
            ),
            out_shape=[
                jax.ShapeDtypeStruct((rows, self.query_heads * size), low),
                jax.ShapeDtypeStruct((rows, self.key_heads * size), low),
                jax.ShapeDtypeStruct((rows, self.key_heads * size), low),
                jax.ShapeDtypeStruct((rows, self.query_heads * size), low),
                jax.ShapeDtypeStruct((self.key_heads, group, rows), jnp.float32),
            ],
        )(place, raw, raw, raw, cosine, sine, query_gain[None, :], key_gain[None, :])

    def backward_kernel(
        self, place_ref, raw_query, raw_key, cosine, sine, query_gain, key_gain,
        query, key, value, totals, upstream,
        raw_grad, query_gain_grad, key_gain_grad, key_total, value_total,
    ):
        place = place_ref[0]
        current = pl.program_id(0)
        size, group = self.head_size, self.grouping

        @pl.when(current == 0)
        def _():
            query_gain_grad[...] = jnp.zeros_like(query_gain_grad)
            key_gain_grad[...] = jnp.zeros_like(key_gain_grad)

        def store(where, head, grad):
            column = pl.multiple_of(head * size, size)
            raw_grad[where, pl.ds(column, size)] = grad.astype(jnp.bfloat16)

        def through_norm(raw, grad, gain, where, gain_grad):
            inverse = inverse_rms(raw)
            scaled = raw * inverse
            normed_grad = grad * cosine[where, :] - self.turn(grad) * sine[where, :]
            gain_grad[...] += jnp.sum(normed_grad * scaled, axis=0, keepdims=True)
            return norm_backward(normed_grad, scaled, inverse, gain)

        for member in range(group):
            for index in reversed(range(self.blocks)):
                here, there = self.inside(index), self.outside(place, index)
                span = (index + 1) * self.block
                query_block = query[here, self.head(member)]
                grad_block = upstream[there, self.head(member)]
                scores = self.scale * product(key[:span, :], query_block, 1, 1)
                row = index * self.block + lax.broadcasted_iota(jnp.int32, scores.shape, 1)
                column = lax.broadcasted_iota(jnp.int32, scores.shape, 0)
                scores = jnp.where(column <= row, scores, masked)
                shares = jnp.exp(scores - totals[0, member : member + 1, here])
                share_grad = product(value[:span, :], grad_block, 1, 1)
                inner = jnp.sum(share_grad * shares, axis=0, keepdims=True)
                score_grad = (shares * (share_grad - inner)).astype(jnp.bfloat16)
                value_part = product(shares.astype(jnp.bfloat16), grad_block, 1, 0)
                key_part = product(score_grad, query_block, 1, 0)
                if member == 0 and index == self.blocks - 1:
                    value_total[...] = value_part
                    key_total[...] = key_part
                else:
                    value_total[:span, :] += value_part
                    key_total[:span, :] += key_part
                query_grad = self.scale * product(score_grad, key[:span, :], 0, 0)
                store(
                    there,
                    current * group + member,
                    through_norm(
                        raw_query[there, self.head(member)],
                        query_grad,
                        query_gain[...],
                        there,
                        query_gain_grad,
                    ),
                )
        for index in range(self.blocks):
            here, there = self.inside(index), self.outside(place, index)
            store(
                there,
                self.query_heads + current,
                through_norm(
                    raw_key[there, :],
                    self.scale * key_total[here, :],
                    key_gain[...],
                    there,
                    key_gain_grad,
                ),
            )
            store(there, self.query_heads + self.key_heads + current, value_total[here, :])

    def backward(
        self, place, raw, cosine, sine, query_gain, key_gain, query, key, value, totals, upstream
    ):
        rows, size, group = self.rows, self.head_size, self.grouping
        wide = group * size
        first_key = self.query_heads
        whole = lambda h, p: (0, 0)
        by_head = lambda h, p: (0, h)
        columns = (self.query_heads + 2 * self.key_heads) * size
        return pl.pallas_call(
            self.backward_kernel,
            name="attention_backward",
            cost_estimate=pl.CostEstimate(flops=1, transcendentals=0, bytes_accessed=1),
            grid_spec=pltpu.PrefetchScalarGridSpec(
                num_scalar_prefetch=1,
                grid=(self.key_heads,),
                in_specs=[
                    pl.BlockSpec((rows, wide), by_head),
                    pl.BlockSpec((rows, size), lambda h, p: (0, first_key + h)),
                    pl.BlockSpec((rows, size), whole),
                    pl.BlockSpec((rows, size), whole),
                    pl.BlockSpec((1, size), whole),
                    pl.BlockSpec((1, size), whole),
                    pl.BlockSpec((rows, wide), by_head),
                    pl.BlockSpec((rows, size), by_head),
                    pl.BlockSpec((rows, size), by_head),
                    pl.BlockSpec((1, group, rows), lambda h, p: (h, 0, 0)),
                    pl.BlockSpec((rows, wide), by_head),
                ],
                out_specs=[
                    pl.BlockSpec((rows, columns), whole),
                    pl.BlockSpec((1, size), whole),
                    pl.BlockSpec((1, size), whole),
                ],
                scratch_shapes=[
                    pltpu.VMEM((rows, size), jnp.float32),
                    pltpu.VMEM((rows, size), jnp.float32),
                ],
            ),
            out_shape=[
                jax.ShapeDtypeStruct((rows, columns), jnp.bfloat16),
                jax.ShapeDtypeStruct((1, size), jnp.float32),
                jax.ShapeDtypeStruct((1, size), jnp.float32),
            ],
        )(
            place, raw, raw, cosine, sine, query_gain[None, :], key_gain[None, :],
            query, key, value, totals, upstream,
        )


def shards(
    links,
    tokens,
    positions,
    input_gain,
    middle_gain,
    query_gain,
    key_gain,
    query_weight,
    key_matrix,
    value_matrix,
    output_weight,
    gate_weight,
    up_weight,
    down_weight,
    layer_cotangent,
):
    head_size = query_gain.shape[0]
    query_heads = query_weight.shape[1] // head_size
    key_heads = key_matrix.shape[1] // head_size
    query_width = query_heads * head_size
    key_width = key_heads * head_size
    group_rows = positions.shape[0]
    assert group_rows == SEQUENCE_LENGTH
    attention = Attention(group_rows, head_size, query_heads, key_heads, links.tensor_size)
    place = lax.axis_index("tensor").astype(jnp.int32)[None]
    hidden = gate_weight.shape[1]
    wide_mixing = links.gather_weight(
        jnp.concatenate([query_weight, key_matrix, value_matrix, output_weight], axis=1)
    )
    wide_attention = wide_mixing[:, : query_width + 2 * key_width]
    wide_output = wide_mixing[:, query_width + 2 * key_width :]
    wide_feed = links.gather_weight(jnp.concatenate([gate_weight, up_weight], axis=1))
    wide_down = links.gather_weight(down_weight)

    positions = links.relative_tokens(positions)
    inputs = tokens.astype(jnp.float32)
    inverse_in = inverse_rms(inputs)
    scaled_in = inputs * inverse_in
    normed_rows = links.gather_tokens((scaled_in * input_gain).astype(jnp.bfloat16))
    own_cotangent = layer_cotangent
    cotangent_first = links.gather_first(own_cotangent)
    normed_rows, cotangent_first = lax.optimization_barrier((normed_rows, cotangent_first))
    cotangent = links.gather_second(own_cotangent, cotangent_first)

    cosine, sine = tables(positions, head_size)
    raw_rows = matmul(normed_rows, wide_attention)
    query_rows, key_rows, value_rows, attended_rows, log_totals = attention.forward(
        place, raw_rows, cosine, sine, query_gain, key_gain
    )
    attended_rows, cotangent = lax.optimization_barrier((attended_rows, cotangent))
    branch_partial = contract_last(attended_rows, wide_output).astype(jnp.bfloat16)
    branch_first = links.scatter_first(branch_partial)
    branch = links.scatter_second(branch_partial, branch_first)
    middle = inputs + branch
    inverse_mid = inverse_rms(middle)
    scaled_mid = middle * inverse_mid
    normed_middle = links.gather_tokens((scaled_mid * middle_gain).astype(jnp.bfloat16))
    feed = matmul(normed_middle, wide_feed)
    gating, upward = feed[:, :hidden], feed[:, hidden:]
    gate_sigmoid = jax.nn.sigmoid(gating)
    silu_gate = gating * gate_sigmoid
    active = (silu_gate * upward).astype(jnp.bfloat16)
    down_term = contract_first(cotangent, active).astype(jnp.bfloat16)
    middle_columns = links.both_columns(normed_middle)
    active, down_term, middle_columns = lax.optimization_barrier(
        (active, down_term, middle_columns)
    )
    down_sum = links.scatter_weight(down_term)
    cotangent, down_term = lax.optimization_barrier((cotangent, down_term))
    active_grad = matmul(cotangent, wide_down)
    gate_grad = (
        active_grad * upward * gate_sigmoid * (1.0 + gating * (1.0 - gate_sigmoid))
    ).astype(jnp.bfloat16)
    upward_grad = (active_grad * silu_gate).astype(jnp.bfloat16)
    feed_grad = jnp.concatenate([gate_grad, upward_grad], axis=1)
    middle_partial = contract_last(feed_grad, wide_feed)
    middle_partial = middle_partial.astype(jnp.bfloat16)
    other_grad = links.other_core(feed_grad)
    feed_grad, other_grad, middle_partial = lax.optimization_barrier(
        (feed_grad, other_grad, middle_partial)
    )
    middle_first = links.scatter_first(middle_partial)
    feed_term = weight_term(middle_columns, jnp.stack([feed_grad, other_grad]))
    feed_term, middle_first, down_sum = lax.optimization_barrier(
        (feed_term, middle_first, down_sum)
    )
    feed_sum = links.scatter_chips(feed_term)
    middle_normed_grad = links.scatter_second(middle_partial, middle_first)
    feed_partial = contract_last(active, wide_down).astype(jnp.bfloat16)
    middle_normed_grad, feed_partial = lax.optimization_barrier((middle_normed_grad, feed_partial))
    middle_gain_term = jnp.sum(middle_normed_grad * scaled_mid, axis=0)
    middle_grad = own_cotangent.astype(jnp.float32) + norm_backward(
        middle_normed_grad, scaled_mid, inverse_mid, middle_gain
    )
    branch_grad = links.gather_tokens(middle_grad.astype(jnp.bfloat16))
    feed_partial, branch_grad = lax.optimization_barrier((feed_partial, branch_grad))
    feed_first = links.scatter_first(feed_partial)
    attended_grad = matmul(branch_grad, wide_output).astype(jnp.bfloat16)
    raw_grad, query_gain_term, key_gain_term = attention.backward(
        place,
        raw_rows,
        cosine,
        sine,
        query_gain,
        key_gain,
        query_rows,
        key_rows,
        value_rows,
        log_totals,
        attended_grad,
    )
    raw_grad, feed_first, branch_grad = lax.optimization_barrier(
        (raw_grad, feed_first, branch_grad)
    )
    output_term = weight_term(links.both_columns(branch_grad), links.both_cores(attended_rows))
    attention_term = weight_term(links.both_columns(normed_rows), links.both_cores(raw_grad))
    feed_first, attention_term = lax.optimization_barrier((feed_first, attention_term))
    feed_branch = links.scatter_second(feed_partial, feed_first)
    raw_grad, attention_term = lax.optimization_barrier((raw_grad, attention_term))
    input_partial = contract_last(raw_grad, wide_attention).astype(jnp.bfloat16)
    mixing_term = jnp.concatenate([attention_term, output_term], axis=1)
    input_gain_term = (
        jnp.sum(input_partial.astype(jnp.float32) * normed_rows.astype(jnp.float32), axis=0)
        / input_gain
    )
    terms = jnp.concatenate(
        [input_gain_term, middle_gain_term, query_gain_term[0], key_gain_term[0]]
    )
    mixing_term, feed_sum, feed_branch, input_partial, terms = lax.optimization_barrier(
        (mixing_term, feed_sum, feed_branch, input_partial, terms)
    )
    mixing_sum = links.scatter_chips(mixing_term)
    input_normed_grad, terms = links.scatter_beside(input_partial, terms)
    layer_output = middle + feed_branch
    tokens_grad = middle_grad + norm_backward(input_normed_grad, scaled_in, inverse_in, input_gain)
    terms = links.total_dp(terms)
    width = tokens.shape[1]
    feed_sum = feed_sum.astype(jnp.float32)
    query_sum, key_sum, value_sum, output_sum = split_columns(
        mixing_sum, (query_width, key_width, key_width, query_width)
    )
    return (
        layer_output,
        tokens_grad,
        terms[:width],
        terms[width : 2 * width],
        terms[2 * width : 2 * width + head_size],
        terms[2 * width + head_size :],
        query_sum,
        key_sum,
        value_sum,
        output_sum,
        feed_sum[:, :hidden],
        feed_sum[:, hidden:],
        down_sum.astype(jnp.float32),
    )


def solution(mesh):
    links = Links(mesh.shape["dp"], mesh.shape["tensor"])
    placed = (
        P(("dp", "tensor"), None),
        P("dp"),
        P(),
        P(),
        P(),
        P(),
        P("dp", "tensor"),
        P("dp", "tensor"),
        P("dp", "tensor"),
        P("dp", "tensor"),
        P("dp", "tensor"),
        P("dp", "tensor"),
        P("dp", "tensor"),
        P(("dp", "tensor"), None),
    )
    return jax.shard_map(
        lambda *arrays: shards(links, *arrays),
        mesh=mesh,
        in_specs=placed,
        out_specs=(
            P(("dp", "tensor"), None),
            P(("dp", "tensor"), None),
            P(),
            P(),
            P(),
            P(),
            P("dp", "tensor"),
            P("dp", "tensor"),
            P("dp", "tensor"),
            P("dp", "tensor"),
            P("dp", "tensor"),
            P("dp", "tensor"),
            P("dp", "tensor"),
        ),
        check_vma=False,
    )
```

```python
import math

import jax
import jax.numpy as jnp
from jax import lax
from jax.experimental import pallas as pl
from jax.experimental.pallas import tpu as pltpu
from jax.sharding import PartitionSpec as P

SEQUENCE_LENGTH = 1024


epsilon = 1e-06
masked = -1e30


def matmul(left, right):
    return jnp.dot(left, right, preferred_element_type=jnp.float32)


def contract_first(left, right):
    return lax.dot_general(
        left, right, (((0,), (0,)), ((), ())), preferred_element_type=jnp.float32
    )


def weight_term(left, right):
    return lax.dot_general(
        left, right, (((0, 1), (0, 1)), ((), ())), preferred_element_type=jnp.float32
    ).astype(jnp.bfloat16)


def contract_last(left, right):
    return lax.dot_general(
        left, right, (((1,), (1,)), ((), ())), preferred_element_type=jnp.float32
    )


def tables(positions, width):
    frequency = jnp.exp(
        jnp.arange(width // 2, dtype=jnp.float32) * (-2.0 * math.log(1000000.0) / width)
    )
    angles = positions.astype(jnp.float32)[:, None] * frequency[None, :]
    cosine = jnp.cos(angles)
    sine = jnp.sin(angles)
    return (
        jnp.concatenate([cosine, cosine], axis=-1),
        jnp.concatenate([-sine, sine], axis=-1),
    )


def inverse_rms(value_rows):
    return lax.rsqrt(jnp.mean(value_rows * value_rows, axis=-1, keepdims=True) + epsilon)


def norm_backward(upstream, scaled, inverse, gain):
    inner = upstream * gain
    return inverse * (inner - scaled * jnp.mean(inner * scaled, axis=-1, keepdims=True))


class Links:
    def __init__(self, dp_size, tensor_size):
        self.dp_size = dp_size
        self.tensor_size = tensor_size
        self.chips = dp_size // 2
        self.swap = [(place, place ^ 1) for place in range(dp_size)]

    def shifted(self, value, step):
        return lax.ppermute(
            value,
            "dp",
            [
                (2 * chip + core, 2 * ((chip + step) % self.chips) + core)
                for chip in range(self.chips)
                for core in range(2)
            ],
        )

    def other_core(self, value):
        return lax.ppermute(value, "dp", self.swap)

    def across(self, value, bit):
        return lax.ppermute(
            value, "tensor", [(place, place ^ bit) for place in range(self.tensor_size)]
        )

    def relative_tokens(self, values):
        count = values.shape[0] // self.tensor_size
        place = lax.axis_index("tensor")
        return jnp.concatenate(
            [
                lax.dynamic_slice_in_dim(values, (place ^ other) * count, count, 0)
                for other in range(self.tensor_size)
            ],
            axis=0,
        )

    def gather_first(self, block):
        if self.tensor_size != 4:
            return block, block
        return lax.optimization_barrier((self.across(block, 1), self.across(block, 2)))

    def gather_second(self, block, first):
        if self.tensor_size != 4:
            bit = 1
            while bit < self.tensor_size:
                block = jnp.concatenate([block, self.across(block, bit)], axis=0)
                bit *= 2
            return block
        half = block.shape[0] // 2
        by_x, by_y = first
        corner_low, corner_high = lax.optimization_barrier(
            (self.across(by_y[:half], 1), self.across(by_x[half:], 2))
        )
        return jnp.concatenate([block, by_x, by_y, corner_low, corner_high], axis=0)

    def gather_tokens(self, block):
        return self.gather_second(block, self.gather_first(block))

    def scatter_tokens(self, partial):
        return self.scatter_second(partial, self.scatter_first(partial))

    def half_block(self, partial, block, high):
        half = partial.shape[0] // (2 * self.tensor_size)
        start = 2 * block * half + high * half
        return partial[start : start + half]

    def first_sends(self, partial):
        return (
            self.across(self.half_block(partial, 3, 0), 1),
            self.across(self.half_block(partial, 3, 1), 2),
            self.across(self.half_block(partial, 1, 0), 1),
            self.across(self.half_block(partial, 2, 1), 2),
        )

    def last_sends(self, partial, first):
        def passed(block, high, arrived):
            total = self.half_block(partial, block, high).astype(jnp.float32)
            return (total + arrived.astype(jnp.float32)).astype(partial.dtype)

        return (
            self.across(passed(2, 0, first[0]), 2),
            self.across(passed(1, 1, first[1]), 1),
        )

    def combined(self, partial, first, last):
        return jnp.concatenate(
            [
                self.half_block(partial, 0, high).astype(jnp.float32)
                + first[2 + high].astype(jnp.float32)
                + last[high].astype(jnp.float32)
                for high in range(2)
            ],
            axis=0,
        )

    def scatter_first(self, partial):
        if self.tensor_size != 4:
            return (partial,)
        return lax.optimization_barrier(self.first_sends(partial))

    def scatter_second(self, partial, first):
        if self.tensor_size != 4:
            (partial,) = first
            bit = self.tensor_size // 2
            while bit:
                middle = partial.shape[0] // 2
                arrived = self.across(partial[middle:], bit).astype(jnp.float32)
                total = partial[:middle].astype(jnp.float32) + arrived
                partial = total.astype(partial.dtype)
                bit //= 2
            return total
        last = lax.optimization_barrier(self.last_sends(partial, first))
        return self.combined(partial, first, last)

    def scatter_last(self, partial, first):
        if self.tensor_size != 4:
            return (self.scatter_second(partial, first),)
        return lax.optimization_barrier(self.last_sends(partial, first))

    def scatter_end(self, partial, first, last):
        return last[0] if self.tensor_size != 4 else self.combined(partial, first, last)

    def scatter_beside(self, partial, terms):
        if self.tensor_size != 4:
            return self.scatter_tokens(partial), self.total_tensor(terms)
        first, arrived = lax.optimization_barrier(
            (self.first_sends(partial), self.across(terms, 1))
        )
        terms = terms + arrived
        last, arrived = lax.optimization_barrier(
            (self.last_sends(partial, first), self.across(terms, 2))
        )
        return self.combined(partial, first, last), terms + arrived

    def gather_weight(self, shard):
        return lax.all_gather(shard, "dp", axis=0, tiled=True)

    def core_columns(self, rows, core):
        width = rows.shape[1] // self.dp_size
        return jnp.concatenate(
            [
                lax.dynamic_slice_in_dim(rows, (2 * chip + core) * width, width, 1)
                for chip in range(self.chips)
            ],
            axis=1,
        )

    def both_cores(self, rows):
        return jnp.stack([rows, self.other_core(rows)])

    def both_columns(self, rows):
        core = lax.axis_index("dp") % 2
        theirs = self.other_core(self.core_columns(rows, core ^ 1))
        return jnp.stack([self.core_columns(rows, core), theirs])

    def scatter_weight(self, partial):
        return lax.psum_scatter(partial, "dp", scatter_dimension=0, tiled=True)

    def scatter_chips(self, partial):
        groups = [list(range(core, self.dp_size, 2)) for core in range(2)]
        return lax.psum_scatter(
            partial, "dp", scatter_dimension=0, tiled=True, axis_index_groups=groups
        )

    def total_tensor(self, value):
        bit = 1
        while bit < self.tensor_size:
            value = value + self.across(value, bit)
            bit *= 2
        return value

    def total_dp(self, value):
        chip = lax.axis_index("dp") // 2
        value = value + self.other_core(value)
        parts = jnp.stack([value] + [self.shifted(value, step) for step in range(1, self.chips)])
        total = None
        for target in range(self.chips):
            part = lax.dynamic_index_in_dim(parts, (chip - target) % self.chips, 0, keepdims=False)
            total = part if total is None else total + part
        return total


def product(left, right, left_axis, right_axis):
    return lax.dot_general(
        left,
        right,
        (((left_axis,), (right_axis,)), ((), ())),
        preferred_element_type=jnp.float32,
    )


def split_columns(rows, widths):
    def kernel(source, *targets):
        start = 0
        for target in targets:
            width = target.shape[1]
            target[...] = source[:, start : start + width].astype(jnp.float32)
            start += width

    return pl.pallas_call(
        kernel,
        name="split_columns",
        out_shape=[jax.ShapeDtypeStruct((rows.shape[0], width), jnp.float32) for width in widths],
    )(rows)


class Attention:
    def __init__(self, rows, head_size, query_heads, key_heads, blocks):
        self.rows = rows
        self.head_size = head_size
        self.query_heads = query_heads
        self.key_heads = key_heads
        self.grouping = query_heads // key_heads
        self.blocks = blocks
        self.block = rows // blocks
        self.scale = head_size ** (-0.5)

    def cost(self, products):
        scores = self.query_heads * self.rows * self.rows
        return pl.CostEstimate(
            flops=products * 2 * scores * 2 * self.head_size,
            transcendentals=scores,
            bytes_accessed=16 * self.query_heads * self.rows * self.head_size,
        )

    def outside(self, place, index):
        return pl.ds(pl.multiple_of((index ^ place) * self.block, self.block), self.block)

    def inside(self, index):
        return slice(index * self.block, (index + 1) * self.block)

    def head(self, index):
        return slice(index * self.head_size, (index + 1) * self.head_size)

    def turn(self, rows):
        return pltpu.roll(rows, self.head_size // 2, axis=1)

    def forward_kernel(
        self, place_ref, raw_query, raw_key, raw_value, cosine, sine, query_gain, key_gain,
        query, key, value, attended, totals,
    ):
        place = place_ref[0]

        def prepared(raw, gain, where):
            normed = raw * inverse_rms(raw) * gain
            turned = normed * cosine[where, :] + self.turn(normed) * sine[where, :]
            return turned.astype(jnp.bfloat16)

        for index in range(self.blocks):
            there, here = self.outside(place, index), self.inside(index)
            key[here, :] = prepared(raw_key[there, :], key_gain[...], there)
            value[here, :] = raw_value[there, :].astype(jnp.bfloat16)
            for member in range(self.grouping):
                query[here, self.head(member)] = prepared(
                    raw_query[there, self.head(member)], query_gain[...], there
                )
        for member in range(self.grouping):
            for index in range(self.blocks):
                span = (index + 1) * self.block
                scores = self.scale * product(
                    query[self.inside(index), self.head(member)], key[:span, :], 1, 1
                )
                row = index * self.block + lax.broadcasted_iota(jnp.int32, scores.shape, 0)
                column = lax.broadcasted_iota(jnp.int32, scores.shape, 1)
                scores = jnp.where(column <= row, scores, masked)
                highest = jnp.max(scores, axis=1, keepdims=True)
                powers = jnp.exp(scores - highest)
                total = jnp.sum(powers, axis=1, keepdims=True)
                shares = (powers * (1.0 / total)).astype(jnp.bfloat16)
                attended[self.outside(place, index), self.head(member)] = product(
                    shares, value[:span, :], 1, 0
                ).astype(jnp.bfloat16)
                log_total = jnp.broadcast_to(
                    highest + jnp.log(total), (self.block, self.head_size)
                )
                totals[0, member : member + 1, self.inside(index)] = log_total.T[:1, :]

    def forward(self, place, raw, cosine, sine, query_gain, key_gain):
        rows, size, group = self.rows, self.head_size, self.grouping
        wide = group * size
        first_key, first_value = self.query_heads, self.query_heads + self.key_heads
        whole = lambda h, p: (0, 0)
        by_head = lambda h, p: (0, h)
        low = jnp.bfloat16
        return pl.pallas_call(
            self.forward_kernel,
            name="attention_forward",
            cost_estimate=self.cost(2),
            grid_spec=pltpu.PrefetchScalarGridSpec(
                num_scalar_prefetch=1,
                grid=(self.key_heads,),
                in_specs=[
                    pl.BlockSpec((rows, wide), by_head),
                    pl.BlockSpec((rows, size), lambda h, p: (0, first_key + h)),
                    pl.BlockSpec((rows, size), lambda h, p: (0, first_value + h)),
                    pl.BlockSpec((rows, size), whole),
                    pl.BlockSpec((rows, size), whole),
                    pl.BlockSpec((1, size), whole),
                    pl.BlockSpec((1, size), whole),
                ],
                out_specs=[
                    pl.BlockSpec((rows, wide), by_head),
                    pl.BlockSpec((rows, size), by_head),
                    pl.BlockSpec((rows, size), by_head),
                    pl.BlockSpec((rows, wide), by_head),
                    pl.BlockSpec((1, group, rows), lambda h, p: (h, 0, 0)),
                ],
            ),
            out_shape=[
                jax.ShapeDtypeStruct((rows, self.query_heads * size), low),
                jax.ShapeDtypeStruct((rows, self.key_heads * size), low),
                jax.ShapeDtypeStruct((rows, self.key_heads * size), low),
                jax.ShapeDtypeStruct((rows, self.query_heads * size), low),
                jax.ShapeDtypeStruct((self.key_heads, group, rows), jnp.float32),
            ],
        )(place, raw, raw, raw, cosine, sine, query_gain[None, :], key_gain[None, :])

    def backward_kernel(
        self, place_ref, raw_query, raw_key, cosine, sine, query_gain, key_gain,
        query, key, value, totals, upstream,
        raw_grad, query_gain_grad, key_gain_grad, key_total, value_total,
    ):
        place = place_ref[0]
        current = pl.program_id(0)
        size, group = self.head_size, self.grouping

        @pl.when(current == 0)
        def _():
            query_gain_grad[...] = jnp.zeros_like(query_gain_grad)
            key_gain_grad[...] = jnp.zeros_like(key_gain_grad)

        def store(where, head, grad):
            column = pl.multiple_of(head * size, size)
            raw_grad[where, pl.ds(column, size)] = grad.astype(jnp.bfloat16)

        def through_norm(raw, grad, gain, where, gain_grad):
            inverse = inverse_rms(raw)
            scaled = raw * inverse
            normed_grad = grad * cosine[where, :] - self.turn(grad) * sine[where, :]
            gain_grad[...] += jnp.sum(normed_grad * scaled, axis=0, keepdims=True)
            return norm_backward(normed_grad, scaled, inverse, gain)

        for member in range(group):
            for index in reversed(range(self.blocks)):
                here, there = self.inside(index), self.outside(place, index)
                span = (index + 1) * self.block
                query_block = query[here, self.head(member)]
                grad_block = upstream[there, self.head(member)]
                scores = self.scale * product(key[:span, :], query_block, 1, 1)
                row = index * self.block + lax.broadcasted_iota(jnp.int32, scores.shape, 1)
                column = lax.broadcasted_iota(jnp.int32, scores.shape, 0)
                scores = jnp.where(column <= row, scores, masked)
                shares = jnp.exp(scores - totals[0, member : member + 1, here])
                share_grad = product(value[:span, :], grad_block, 1, 1)
                inner = jnp.sum(share_grad * shares, axis=0, keepdims=True)
                score_grad = (shares * (share_grad - inner)).astype(jnp.bfloat16)
                value_part = product(shares.astype(jnp.bfloat16), grad_block, 1, 0)
                key_part = product(score_grad, query_block, 1, 0)
                if member == 0 and index == self.blocks - 1:
                    value_total[...] = value_part
                    key_total[...] = key_part
                else:
                    value_total[:span, :] += value_part
                    key_total[:span, :] += key_part
                query_grad = self.scale * product(score_grad, key[:span, :], 0, 0)
                store(
                    there,
                    current * group + member,
                    through_norm(
                        raw_query[there, self.head(member)],
                        query_grad,
                        query_gain[...],
                        there,
                        query_gain_grad,
                    ),
                )
        for index in range(self.blocks):
            here, there = self.inside(index), self.outside(place, index)
            store(
                there,
                self.query_heads + current,
                through_norm(
                    raw_key[there, :],
                    self.scale * key_total[here, :],
                    key_gain[...],
                    there,
                    key_gain_grad,
                ),
            )
            store(there, self.query_heads + self.key_heads + current, value_total[here, :])

    def backward(
        self, place, raw, cosine, sine, query_gain, key_gain, query, key, value, totals, upstream
    ):
        rows, size, group = self.rows, self.head_size, self.grouping
        wide = group * size
        first_key = self.query_heads
        whole = lambda h, p: (0, 0)
        by_head = lambda h, p: (0, h)
        columns = (self.query_heads + 2 * self.key_heads) * size
        return pl.pallas_call(
            self.backward_kernel,
            name="attention_backward",
            cost_estimate=pl.CostEstimate(flops=1, transcendentals=0, bytes_accessed=1),
            grid_spec=pltpu.PrefetchScalarGridSpec(
                num_scalar_prefetch=1,
                grid=(self.key_heads,),
                in_specs=[
                    pl.BlockSpec((rows, wide), by_head),
                    pl.BlockSpec((rows, size), lambda h, p: (0, first_key + h)),
                    pl.BlockSpec((rows, size), whole),
                    pl.BlockSpec((rows, size), whole),
                    pl.BlockSpec((1, size), whole),
                    pl.BlockSpec((1, size), whole),
                    pl.BlockSpec((rows, wide), by_head),
                    pl.BlockSpec((rows, size), by_head),
                    pl.BlockSpec((rows, size), by_head),
                    pl.BlockSpec((1, group, rows), lambda h, p: (h, 0, 0)),
                    pl.BlockSpec((rows, wide), by_head),
                ],
                out_specs=[
                    pl.BlockSpec((rows, columns), whole),
                    pl.BlockSpec((1, size), whole),
                    pl.BlockSpec((1, size), whole),
                ],
                scratch_shapes=[
                    pltpu.VMEM((rows, size), jnp.float32),
                    pltpu.VMEM((rows, size), jnp.float32),
                ],
            ),
            out_shape=[
                jax.ShapeDtypeStruct((rows, columns), jnp.bfloat16),
                jax.ShapeDtypeStruct((1, size), jnp.float32),
                jax.ShapeDtypeStruct((1, size), jnp.float32),
            ],
        )(
            place, raw, raw, cosine, sine, query_gain[None, :], key_gain[None, :],
            query, key, value, totals, upstream,
        )


def shards(
    links,
    tokens,
    positions,
    input_gain,
    middle_gain,
    query_gain,
    key_gain,
    query_weight,
    key_matrix,
    value_matrix,
    output_weight,
    gate_weight,
    up_weight,
    down_weight,
    layer_cotangent,
):
    head_size = query_gain.shape[0]
    query_heads = query_weight.shape[1] // head_size
    key_heads = key_matrix.shape[1] // head_size
    query_width = query_heads * head_size
    key_width = key_heads * head_size
    group_rows = positions.shape[0]
    assert group_rows == SEQUENCE_LENGTH
    attention = Attention(group_rows, head_size, query_heads, key_heads, links.tensor_size)
    place = lax.axis_index("tensor").astype(jnp.int32)[None]
    hidden = gate_weight.shape[1]
    wide_mixing = links.gather_weight(
        jnp.concatenate([query_weight, key_matrix, value_matrix, output_weight], axis=1)
    )
    wide_attention = wide_mixing[:, : query_width + 2 * key_width]
    wide_output = wide_mixing[:, query_width + 2 * key_width :]
    wide_feed = links.gather_weight(jnp.concatenate([gate_weight, up_weight], axis=1))
    wide_down = links.gather_weight(down_weight)

    positions = links.relative_tokens(positions)
    inputs = tokens.astype(jnp.float32)
    inverse_in = inverse_rms(inputs)
    scaled_in = inputs * inverse_in
    normed_rows = links.gather_tokens((scaled_in * input_gain).astype(jnp.bfloat16))
    own_cotangent = layer_cotangent
    cotangent_first = links.gather_first(own_cotangent)
    normed_rows, cotangent_first = lax.optimization_barrier((normed_rows, cotangent_first))
    cotangent = links.gather_second(own_cotangent, cotangent_first)

    cosine, sine = tables(positions, head_size)
    raw_rows = matmul(normed_rows, wide_attention)
    query_rows, key_rows, value_rows, attended_rows, log_totals = attention.forward(
        place, raw_rows, cosine, sine, query_gain, key_gain
    )
    attended_rows, cotangent = lax.optimization_barrier((attended_rows, cotangent))
    branch_partial = contract_last(attended_rows, wide_output).astype(jnp.bfloat16)
    branch_first = links.scatter_first(branch_partial)
    branch = links.scatter_second(branch_partial, branch_first)
    middle = inputs + branch
    inverse_mid = inverse_rms(middle)
    scaled_mid = middle * inverse_mid
    normed_middle = links.gather_tokens((scaled_mid * middle_gain).astype(jnp.bfloat16))
    feed = matmul(normed_middle, wide_feed)
    gating, upward = feed[:, :hidden], feed[:, hidden:]
    gate_sigmoid = jax.nn.sigmoid(gating)
    silu_gate = gating * gate_sigmoid
    active = (silu_gate * upward).astype(jnp.bfloat16)
    down_term = contract_first(cotangent, active).astype(jnp.bfloat16)
    middle_columns = links.both_columns(normed_middle)
    active, down_term, middle_columns = lax.optimization_barrier(
        (active, down_term, middle_columns)
    )
    down_sum = links.scatter_weight(down_term)
    cotangent, down_term = lax.optimization_barrier((cotangent, down_term))
    active_grad = matmul(cotangent, wide_down)
    gate_grad = (
        active_grad * upward * gate_sigmoid * (1.0 + gating * (1.0 - gate_sigmoid))
    ).astype(jnp.bfloat16)
    upward_grad = (active_grad * silu_gate).astype(jnp.bfloat16)
    feed_grad = jnp.concatenate([gate_grad, upward_grad], axis=1)
    middle_partial = contract_last(feed_grad, wide_feed)
    middle_partial = middle_partial.astype(jnp.bfloat16)
    other_grad = links.other_core(feed_grad)
    feed_grad, other_grad, middle_partial = lax.optimization_barrier(
        (feed_grad, other_grad, middle_partial)
    )
    middle_first = links.scatter_first(middle_partial)
    feed_term = weight_term(middle_columns, jnp.stack([feed_grad, other_grad]))
    feed_term, middle_first = lax.optimization_barrier((feed_term, middle_first))
    feed_term, down_sum = lax.optimization_barrier((feed_term, down_sum))
    feed_sum = links.scatter_chips(feed_term)
    middle_normed_grad = links.scatter_second(middle_partial, middle_first)
    feed_partial = contract_last(active, wide_down).astype(jnp.bfloat16)
    middle_normed_grad, feed_partial = lax.optimization_barrier((middle_normed_grad, feed_partial))
    middle_gain_term = jnp.sum(middle_normed_grad * scaled_mid, axis=0)
    middle_grad = own_cotangent.astype(jnp.float32) + norm_backward(
        middle_normed_grad, scaled_mid, inverse_mid, middle_gain
    )
    branch_grad = links.gather_tokens(middle_grad.astype(jnp.bfloat16))
    feed_partial, branch_grad = lax.optimization_barrier((feed_partial, branch_grad))
    feed_first = links.scatter_first(feed_partial)
    attended_grad = matmul(branch_grad, wide_output).astype(jnp.bfloat16)
    raw_grad, query_gain_term, key_gain_term = attention.backward(
        place,
        raw_rows,
        cosine,
        sine,
        query_gain,
        key_gain,
        query_rows,
        key_rows,
        value_rows,
        log_totals,
        attended_grad,
    )
    raw_grad, feed_first, branch_grad = lax.optimization_barrier(
        (raw_grad, feed_first, branch_grad)
    )
    output_term = weight_term(links.both_columns(branch_grad), links.both_cores(attended_rows))
    attention_term = weight_term(links.both_columns(normed_rows), links.both_cores(raw_grad))
    feed_first, attention_term = lax.optimization_barrier((feed_first, attention_term))
    feed_last = links.scatter_last(feed_partial, feed_first)
    raw_grad, attention_term = lax.optimization_barrier((raw_grad, attention_term))
    input_partial = contract_last(raw_grad, wide_attention).astype(jnp.bfloat16)
    mixing_term = jnp.concatenate([attention_term, output_term], axis=1)
    input_gain_term = (
        jnp.sum(input_partial.astype(jnp.float32) * normed_rows.astype(jnp.float32), axis=0)
        / input_gain
    )
    terms = jnp.concatenate(
        [input_gain_term, middle_gain_term, query_gain_term[0], key_gain_term[0]]
    )
    mixing_term, feed_sum, feed_last, input_partial, terms = lax.optimization_barrier(
        (mixing_term, feed_sum, feed_last, input_partial, terms)
    )
    mixing_sum = links.scatter_chips(mixing_term)
    input_normed_grad, terms = links.scatter_beside(input_partial, terms)
    layer_output = middle + links.scatter_end(feed_partial, feed_first, feed_last)
    tokens_grad = middle_grad + norm_backward(input_normed_grad, scaled_in, inverse_in, input_gain)
    terms = links.total_dp(terms)
    width = tokens.shape[1]
    feed_sum = feed_sum.astype(jnp.float32)
    query_sum, key_sum, value_sum, output_sum = split_columns(
        mixing_sum, (query_width, key_width, key_width, query_width)
    )
    return (
        layer_output,
        tokens_grad,
        terms[:width],
        terms[width : 2 * width],
        terms[2 * width : 2 * width + head_size],
        terms[2 * width + head_size :],
        query_sum,
        key_sum,
        value_sum,
        output_sum,
        feed_sum[:, :hidden],
        feed_sum[:, hidden:],
        down_sum.astype(jnp.float32),
    )


def solution(mesh):
    links = Links(mesh.shape["dp"], mesh.shape["tensor"])
    placed = (
        P(("dp", "tensor"), None),
        P("dp"),
        P(),
        P(),
        P(),
        P(),
        P("dp", "tensor"),
        P("dp", "tensor"),
        P("dp", "tensor"),
        P("dp", "tensor"),
        P("dp", "tensor"),
        P("dp", "tensor"),
        P("dp", "tensor"),
        P(("dp", "tensor"), None),
    )
    return jax.shard_map(
        lambda *arrays: shards(links, *arrays),
        mesh=mesh,
        in_specs=placed,
        out_specs=(
            P(("dp", "tensor"), None),
            P(("dp", "tensor"), None),
            P(),
            P(),
            P(),
            P(),
            P("dp", "tensor"),
            P("dp", "tensor"),
            P("dp", "tensor"),
            P("dp", "tensor"),
            P("dp", "tensor"),
            P("dp", "tensor"),
            P("dp", "tensor"),
        ),
        check_vma=False,
    )
```

```python
import math

import jax
import jax.numpy as jnp
from jax import lax
from jax.experimental import pallas as pl
from jax.experimental.pallas import tpu as pltpu
from jax.sharding import PartitionSpec as P

SEQUENCE_LENGTH = 1024


epsilon = 1e-06
masked = -1e30


def matmul(left, right):
    return jnp.dot(left, right, preferred_element_type=jnp.float32)


def contract_first(left, right):
    return lax.dot_general(
        left, right, (((0,), (0,)), ((), ())), preferred_element_type=jnp.float32
    )


def weight_term(left, right):
    return lax.dot_general(
        left, right, (((0, 1), (0, 1)), ((), ())), preferred_element_type=jnp.float32
    ).astype(jnp.bfloat16)


def contract_last(left, right):
    return lax.dot_general(
        left, right, (((1,), (1,)), ((), ())), preferred_element_type=jnp.float32
    )


def tables(positions, width):
    frequency = jnp.exp(
        jnp.arange(width // 2, dtype=jnp.float32) * (-2.0 * math.log(1000000.0) / width)
    )
    angles = positions.astype(jnp.float32)[:, None] * frequency[None, :]
    cosine = jnp.cos(angles)
    sine = jnp.sin(angles)
    return (
        jnp.concatenate([cosine, cosine], axis=-1),
        jnp.concatenate([-sine, sine], axis=-1),
    )


def inverse_rms(value_rows):
    return lax.rsqrt(jnp.mean(value_rows * value_rows, axis=-1, keepdims=True) + epsilon)


def norm_backward(upstream, scaled, inverse, gain):
    inner = upstream * gain
    return inverse * (inner - scaled * jnp.mean(inner * scaled, axis=-1, keepdims=True))


class Links:
    def __init__(self, dp_size, tensor_size):
        self.dp_size = dp_size
        self.tensor_size = tensor_size
        self.chips = dp_size // 2
        self.swap = [(place, place ^ 1) for place in range(dp_size)]

    def shifted(self, value, step):
        return lax.ppermute(
            value,
            "dp",
            [
                (2 * chip + core, 2 * ((chip + step) % self.chips) + core)
                for chip in range(self.chips)
                for core in range(2)
            ],
        )

    def other_core(self, value):
        return lax.ppermute(value, "dp", self.swap)

    def across(self, value, bit):
        return lax.ppermute(
            value, "tensor", [(place, place ^ bit) for place in range(self.tensor_size)]
        )

    def relative_tokens(self, values):
        count = values.shape[0] // self.tensor_size
        place = lax.axis_index("tensor")
        return jnp.concatenate(
            [
                lax.dynamic_slice_in_dim(values, (place ^ other) * count, count, 0)
                for other in range(self.tensor_size)
            ],
            axis=0,
        )

    def gather_first(self, block):
        if self.tensor_size != 4:
            return block, block
        return lax.optimization_barrier((self.across(block, 1), self.across(block, 2)))

    def gather_second(self, block, first):
        if self.tensor_size != 4:
            bit = 1
            while bit < self.tensor_size:
                block = jnp.concatenate([block, self.across(block, bit)], axis=0)
                bit *= 2
            return block
        half = block.shape[0] // 2
        by_x, by_y = first
        corner_low, corner_high = lax.optimization_barrier(
            (self.across(by_y[:half], 1), self.across(by_x[half:], 2))
        )
        return jnp.concatenate([block, by_x, by_y, corner_low, corner_high], axis=0)

    def gather_tokens(self, block):
        return self.gather_second(block, self.gather_first(block))

    def scatter_tokens(self, partial):
        return self.scatter_second(partial, self.scatter_first(partial))

    def half_block(self, partial, block, high):
        half = partial.shape[0] // (2 * self.tensor_size)
        start = 2 * block * half + high * half
        return partial[start : start + half]

    def first_sends(self, partial):
        return (
            self.across(self.half_block(partial, 3, 0), 1),
            self.across(self.half_block(partial, 3, 1), 2),
            self.across(self.half_block(partial, 1, 0), 1),
            self.across(self.half_block(partial, 2, 1), 2),
        )

    def last_sends(self, partial, first):
        def passed(block, high, arrived):
            total = self.half_block(partial, block, high).astype(jnp.float32)
            return (total + arrived.astype(jnp.float32)).astype(partial.dtype)

        return (
            self.across(passed(2, 0, first[0]), 2),
            self.across(passed(1, 1, first[1]), 1),
        )

    def combined(self, partial, first, last):
        return jnp.concatenate(
            [
                self.half_block(partial, 0, high).astype(jnp.float32)
                + first[2 + high].astype(jnp.float32)
                + last[high].astype(jnp.float32)
                for high in range(2)
            ],
            axis=0,
        )

    def scatter_first(self, partial):
        if self.tensor_size != 4:
            return (partial,)
        return lax.optimization_barrier(self.first_sends(partial))

    def scatter_second(self, partial, first):
        if self.tensor_size != 4:
            (partial,) = first
            bit = self.tensor_size // 2
            while bit:
                middle = partial.shape[0] // 2
                arrived = self.across(partial[middle:], bit).astype(jnp.float32)
                total = partial[:middle].astype(jnp.float32) + arrived
                partial = total.astype(partial.dtype)
                bit //= 2
            return total
        last = lax.optimization_barrier(self.last_sends(partial, first))
        return self.combined(partial, first, last)

    def scatter_last(self, partial, first):
        if self.tensor_size != 4:
            return (self.scatter_second(partial, first),)
        return lax.optimization_barrier(self.last_sends(partial, first))

    def scatter_end(self, partial, first, last):
        return last[0] if self.tensor_size != 4 else self.combined(partial, first, last)

    def scatter_beside(self, partial, terms):
        if self.tensor_size != 4:
            return self.scatter_tokens(partial), self.total_tensor(terms)
        first, arrived = lax.optimization_barrier(
            (self.first_sends(partial), self.across(terms, 1))
        )
        terms = terms + arrived
        last, arrived = lax.optimization_barrier(
            (self.last_sends(partial, first), self.across(terms, 2))
        )
        return self.combined(partial, first, last), terms + arrived

    def gather_weight(self, shard):
        return lax.all_gather(shard, "dp", axis=0, tiled=True)

    def core_columns(self, rows, core):
        width = rows.shape[1] // self.dp_size
        return jnp.concatenate(
            [
                lax.dynamic_slice_in_dim(rows, (2 * chip + core) * width, width, 1)
                for chip in range(self.chips)
            ],
            axis=1,
        )

    def both_cores(self, rows):
        return jnp.stack([rows, self.other_core(rows)])

    def both_columns(self, rows):
        core = lax.axis_index("dp") % 2
        theirs = self.other_core(self.core_columns(rows, core ^ 1))
        return jnp.stack([self.core_columns(rows, core), theirs])

    def scatter_weight(self, partial):
        return lax.psum_scatter(partial, "dp", scatter_dimension=0, tiled=True)

    def scatter_chips(self, partial):
        groups = [list(range(core, self.dp_size, 2)) for core in range(2)]
        return lax.psum_scatter(
            partial, "dp", scatter_dimension=0, tiled=True, axis_index_groups=groups
        )

    def total_tensor(self, value):
        bit = 1
        while bit < self.tensor_size:
            value = value + self.across(value, bit)
            bit *= 2
        return value

    def total_dp(self, value):
        chip = lax.axis_index("dp") // 2
        value = value + self.other_core(value)
        parts = jnp.stack([value] + [self.shifted(value, step) for step in range(1, self.chips)])
        total = None
        for target in range(self.chips):
            part = lax.dynamic_index_in_dim(parts, (chip - target) % self.chips, 0, keepdims=False)
            total = part if total is None else total + part
        return total


def product(left, right, left_axis, right_axis):
    return lax.dot_general(
        left,
        right,
        (((left_axis,), (right_axis,)), ((), ())),
        preferred_element_type=jnp.float32,
    )


def split_columns(rows, widths):
    def kernel(source, *targets):
        start = 0
        for target in targets:
            width = target.shape[1]
            target[...] = source[:, start : start + width].astype(jnp.float32)
            start += width

    return pl.pallas_call(
        kernel,
        name="split_columns",
        out_shape=[jax.ShapeDtypeStruct((rows.shape[0], width), jnp.float32) for width in widths],
    )(rows)


def long_product(left, right):
    rows, depth = left.shape
    columns = right.shape[0]
    width = math.gcd(512, columns)

    def kernel(left_ref, right_ref, target):
        target[...] = product(left_ref[...], right_ref[...], 1, 1).astype(target.dtype)

    return pl.pallas_call(
        kernel,
        name="long_product",
        grid=(columns // width,),
        in_specs=[
            pl.BlockSpec((rows, depth), lambda column: (0, 0)),
            pl.BlockSpec((width, depth), lambda column: (column, 0)),
        ],
        out_specs=pl.BlockSpec((rows, width), lambda column: (0, column)),
        out_shape=jax.ShapeDtypeStruct((rows, columns), left.dtype),
        cost_estimate=pl.CostEstimate(flops=1, transcendentals=0, bytes_accessed=1),
    )(left, right)


class Attention:
    def __init__(self, rows, head_size, query_heads, key_heads, blocks):
        self.rows = rows
        self.head_size = head_size
        self.query_heads = query_heads
        self.key_heads = key_heads
        self.grouping = query_heads // key_heads
        self.blocks = blocks
        self.block = rows // blocks
        self.scale = head_size ** (-0.5)

    def cost(self, products):
        scores = self.query_heads * self.rows * self.rows
        return pl.CostEstimate(
            flops=products * 2 * scores * 2 * self.head_size,
            transcendentals=scores,
            bytes_accessed=16 * self.query_heads * self.rows * self.head_size,
        )

    def outside(self, place, index):
        return pl.ds(pl.multiple_of((index ^ place) * self.block, self.block), self.block)

    def inside(self, index):
        return slice(index * self.block, (index + 1) * self.block)

    def head(self, index):
        return slice(index * self.head_size, (index + 1) * self.head_size)

    def turn(self, rows):
        return pltpu.roll(rows, self.head_size // 2, axis=1)

    def forward_kernel(
        self, place_ref, raw_query, raw_key, raw_value, cosine, sine, query_gain, key_gain,
        query, key, value, attended, totals,
    ):
        place = place_ref[0]

        def prepared(raw, gain, where):
            normed = raw * inverse_rms(raw) * gain
            turned = normed * cosine[where, :] + self.turn(normed) * sine[where, :]
            return turned.astype(jnp.bfloat16)

        for index in range(self.blocks):
            there, here = self.outside(place, index), self.inside(index)
            key[here, :] = prepared(raw_key[there, :], key_gain[...], there)
            value[here, :] = raw_value[there, :].astype(jnp.bfloat16)
            for member in range(self.grouping):
                query[here, self.head(member)] = prepared(
                    raw_query[there, self.head(member)], query_gain[...], there
                )
        for member in range(self.grouping):
            for index in range(self.blocks):
                span = (index + 1) * self.block
                scores = self.scale * product(
                    query[self.inside(index), self.head(member)], key[:span, :], 1, 1
                )
                row = index * self.block + lax.broadcasted_iota(jnp.int32, scores.shape, 0)
                column = lax.broadcasted_iota(jnp.int32, scores.shape, 1)
                scores = jnp.where(column <= row, scores, masked)
                highest = jnp.max(scores, axis=1, keepdims=True)
                powers = jnp.exp(scores - highest)
                total = jnp.sum(powers, axis=1, keepdims=True)
                shares = (powers * (1.0 / total)).astype(jnp.bfloat16)
                attended[self.outside(place, index), self.head(member)] = product(
                    shares, value[:span, :], 1, 0
                ).astype(jnp.bfloat16)
                log_total = jnp.broadcast_to(
                    highest + jnp.log(total), (self.block, self.head_size)
                )
                totals[0, member : member + 1, self.inside(index)] = log_total.T[:1, :]

    def forward(self, place, raw, cosine, sine, query_gain, key_gain):
        rows, size, group = self.rows, self.head_size, self.grouping
        wide = group * size
        first_key, first_value = self.query_heads, self.query_heads + self.key_heads
        whole = lambda h, p: (0, 0)
        by_head = lambda h, p: (0, h)
        low = jnp.bfloat16
        return pl.pallas_call(
            self.forward_kernel,
            name="attention_forward",
            cost_estimate=self.cost(2),
            grid_spec=pltpu.PrefetchScalarGridSpec(
                num_scalar_prefetch=1,
                grid=(self.key_heads,),
                in_specs=[
                    pl.BlockSpec((rows, wide), by_head),
                    pl.BlockSpec((rows, size), lambda h, p: (0, first_key + h)),
                    pl.BlockSpec((rows, size), lambda h, p: (0, first_value + h)),
                    pl.BlockSpec((rows, size), whole),
                    pl.BlockSpec((rows, size), whole),
                    pl.BlockSpec((1, size), whole),
                    pl.BlockSpec((1, size), whole),
                ],
                out_specs=[
                    pl.BlockSpec((rows, wide), by_head),
                    pl.BlockSpec((rows, size), by_head),
                    pl.BlockSpec((rows, size), by_head),
                    pl.BlockSpec((rows, wide), by_head),
                    pl.BlockSpec((1, group, rows), lambda h, p: (h, 0, 0)),
                ],
            ),
            out_shape=[
                jax.ShapeDtypeStruct((rows, self.query_heads * size), low),
                jax.ShapeDtypeStruct((rows, self.key_heads * size), low),
                jax.ShapeDtypeStruct((rows, self.key_heads * size), low),
                jax.ShapeDtypeStruct((rows, self.query_heads * size), low),
                jax.ShapeDtypeStruct((self.key_heads, group, rows), jnp.float32),
            ],
        )(place, raw, raw, raw, cosine, sine, query_gain[None, :], key_gain[None, :])

    def backward_kernel(
        self, place_ref, raw_query, raw_key, cosine, sine, query_gain, key_gain,
        query, key, value, totals, upstream,
        raw_grad, query_gain_grad, key_gain_grad, key_total, value_total,
    ):
        place = place_ref[0]
        current = pl.program_id(0)
        size, group = self.head_size, self.grouping

        @pl.when(current == 0)
        def _():
            query_gain_grad[...] = jnp.zeros_like(query_gain_grad)
            key_gain_grad[...] = jnp.zeros_like(key_gain_grad)

        def store(where, head, grad):
            column = pl.multiple_of(head * size, size)
            raw_grad[where, pl.ds(column, size)] = grad.astype(jnp.bfloat16)

        def through_norm(raw, grad, gain, where, gain_grad):
            inverse = inverse_rms(raw)
            scaled = raw * inverse
            normed_grad = grad * cosine[where, :] - self.turn(grad) * sine[where, :]
            gain_grad[...] += jnp.sum(normed_grad * scaled, axis=0, keepdims=True)
            return norm_backward(normed_grad, scaled, inverse, gain)

        for member in range(group):
            for index in reversed(range(self.blocks)):
                here, there = self.inside(index), self.outside(place, index)
                span = (index + 1) * self.block
                query_block = query[here, self.head(member)]
                grad_block = upstream[there, self.head(member)]
                scores = self.scale * product(key[:span, :], query_block, 1, 1)
                row = index * self.block + lax.broadcasted_iota(jnp.int32, scores.shape, 1)
                column = lax.broadcasted_iota(jnp.int32, scores.shape, 0)
                scores = jnp.where(column <= row, scores, masked)
                shares = jnp.exp(scores - totals[0, member : member + 1, here])
                share_grad = product(value[:span, :], grad_block, 1, 1)
                inner = jnp.sum(share_grad * shares, axis=0, keepdims=True)
                score_grad = (shares * (share_grad - inner)).astype(jnp.bfloat16)
                value_part = product(shares.astype(jnp.bfloat16), grad_block, 1, 0)
                key_part = product(score_grad, query_block, 1, 0)
                if member == 0 and index == self.blocks - 1:
                    value_total[...] = value_part
                    key_total[...] = key_part
                else:
                    value_total[:span, :] += value_part
                    key_total[:span, :] += key_part
                query_grad = self.scale * product(score_grad, key[:span, :], 0, 0)
                store(
                    there,
                    current * group + member,
                    through_norm(
                        raw_query[there, self.head(member)],
                        query_grad,
                        query_gain[...],
                        there,
                        query_gain_grad,
                    ),
                )
        for index in range(self.blocks):
            here, there = self.inside(index), self.outside(place, index)
            store(
                there,
                self.query_heads + current,
                through_norm(
                    raw_key[there, :],
                    self.scale * key_total[here, :],
                    key_gain[...],
                    there,
                    key_gain_grad,
                ),
            )
            store(there, self.query_heads + self.key_heads + current, value_total[here, :])

    def backward(
        self, place, raw, cosine, sine, query_gain, key_gain, query, key, value, totals, upstream
    ):
        rows, size, group = self.rows, self.head_size, self.grouping
        wide = group * size
        first_key = self.query_heads
        whole = lambda h, p: (0, 0)
        by_head = lambda h, p: (0, h)
        columns = (self.query_heads + 2 * self.key_heads) * size
        return pl.pallas_call(
            self.backward_kernel,
            name="attention_backward",
            cost_estimate=pl.CostEstimate(flops=1, transcendentals=0, bytes_accessed=1),
            grid_spec=pltpu.PrefetchScalarGridSpec(
                num_scalar_prefetch=1,
                grid=(self.key_heads,),
                in_specs=[
                    pl.BlockSpec((rows, wide), by_head),
                    pl.BlockSpec((rows, size), lambda h, p: (0, first_key + h)),
                    pl.BlockSpec((rows, size), whole),
                    pl.BlockSpec((rows, size), whole),
                    pl.BlockSpec((1, size), whole),
                    pl.BlockSpec((1, size), whole),
                    pl.BlockSpec((rows, wide), by_head),
                    pl.BlockSpec((rows, size), by_head),
                    pl.BlockSpec((rows, size), by_head),
                    pl.BlockSpec((1, group, rows), lambda h, p: (h, 0, 0)),
                    pl.BlockSpec((rows, wide), by_head),
                ],
                out_specs=[
                    pl.BlockSpec((rows, columns), whole),
                    pl.BlockSpec((1, size), whole),
                    pl.BlockSpec((1, size), whole),
                ],
                scratch_shapes=[
                    pltpu.VMEM((rows, size), jnp.float32),
                    pltpu.VMEM((rows, size), jnp.float32),
                ],
            ),
            out_shape=[
                jax.ShapeDtypeStruct((rows, columns), jnp.bfloat16),
                jax.ShapeDtypeStruct((1, size), jnp.float32),
                jax.ShapeDtypeStruct((1, size), jnp.float32),
            ],
        )(
            place, raw, raw, cosine, sine, query_gain[None, :], key_gain[None, :],
            query, key, value, totals, upstream,
        )


def shards(
    links,
    tokens,
    positions,
    input_gain,
    middle_gain,
    query_gain,
    key_gain,
    query_weight,
    key_matrix,
    value_matrix,
    output_weight,
    gate_weight,
    up_weight,
    down_weight,
    layer_cotangent,
):
    head_size = query_gain.shape[0]
    query_heads = query_weight.shape[1] // head_size
    key_heads = key_matrix.shape[1] // head_size
    query_width = query_heads * head_size
    key_width = key_heads * head_size
    group_rows = positions.shape[0]
    assert group_rows == SEQUENCE_LENGTH
    attention = Attention(group_rows, head_size, query_heads, key_heads, links.tensor_size)
    place = lax.axis_index("tensor").astype(jnp.int32)[None]
    hidden = gate_weight.shape[1]
    wide_mixing = links.gather_weight(
        jnp.concatenate([query_weight, key_matrix, value_matrix, output_weight], axis=1)
    )
    wide_attention = wide_mixing[:, : query_width + 2 * key_width]
    wide_output = wide_mixing[:, query_width + 2 * key_width :]
    wide_feed = links.gather_weight(jnp.concatenate([gate_weight, up_weight], axis=1))
    wide_down = links.gather_weight(down_weight)

    positions = links.relative_tokens(positions)
    inputs = tokens.astype(jnp.float32)
    inverse_in = inverse_rms(inputs)
    scaled_in = inputs * inverse_in
    normed_rows = links.gather_tokens((scaled_in * input_gain).astype(jnp.bfloat16))
    own_cotangent = layer_cotangent
    cotangent_first = links.gather_first(own_cotangent)
    normed_rows, cotangent_first = lax.optimization_barrier((normed_rows, cotangent_first))
    cotangent = links.gather_second(own_cotangent, cotangent_first)

    cosine, sine = tables(positions, head_size)
    raw_rows = matmul(normed_rows, wide_attention)
    query_rows, key_rows, value_rows, attended_rows, log_totals = attention.forward(
        place, raw_rows, cosine, sine, query_gain, key_gain
    )
    attended_rows, cotangent = lax.optimization_barrier((attended_rows, cotangent))
    branch_partial = contract_last(attended_rows, wide_output).astype(jnp.bfloat16)
    branch_first = links.scatter_first(branch_partial)
    branch = links.scatter_second(branch_partial, branch_first)
    middle = inputs + branch
    inverse_mid = inverse_rms(middle)
    scaled_mid = middle * inverse_mid
    normed_middle = links.gather_tokens((scaled_mid * middle_gain).astype(jnp.bfloat16))
    feed = matmul(normed_middle, wide_feed)
    gating, upward = feed[:, :hidden], feed[:, hidden:]
    gate_sigmoid = jax.nn.sigmoid(gating)
    silu_gate = gating * gate_sigmoid
    active = (silu_gate * upward).astype(jnp.bfloat16)
    down_term = contract_first(cotangent, active).astype(jnp.bfloat16)
    middle_columns = links.both_columns(normed_middle)
    active, down_term, middle_columns = lax.optimization_barrier(
        (active, down_term, middle_columns)
    )
    down_sum = links.scatter_weight(down_term)
    cotangent, down_term = lax.optimization_barrier((cotangent, down_term))
    active_grad = matmul(cotangent, wide_down)
    gate_grad = (
        active_grad * upward * gate_sigmoid * (1.0 + gating * (1.0 - gate_sigmoid))
    ).astype(jnp.bfloat16)
    upward_grad = (active_grad * silu_gate).astype(jnp.bfloat16)
    feed_grad = jnp.concatenate([gate_grad, upward_grad], axis=1)
    middle_partial = long_product(feed_grad, wide_feed)
    other_grad = links.other_core(feed_grad)
    feed_grad, other_grad, middle_partial = lax.optimization_barrier(
        (feed_grad, other_grad, middle_partial)
    )
    middle_first = links.scatter_first(middle_partial)
    feed_term = weight_term(middle_columns, jnp.stack([feed_grad, other_grad]))
    feed_term, middle_first = lax.optimization_barrier((feed_term, middle_first))
    feed_term, down_sum = lax.optimization_barrier((feed_term, down_sum))
    feed_sum = links.scatter_chips(feed_term)
    middle_normed_grad = links.scatter_second(middle_partial, middle_first)
    feed_partial = long_product(active, wide_down)
    middle_normed_grad, feed_partial = lax.optimization_barrier((middle_normed_grad, feed_partial))
    middle_gain_term = jnp.sum(middle_normed_grad * scaled_mid, axis=0)
    middle_grad = own_cotangent.astype(jnp.float32) + norm_backward(
        middle_normed_grad, scaled_mid, inverse_mid, middle_gain
    )
    branch_grad = links.gather_tokens(middle_grad.astype(jnp.bfloat16))
    feed_partial, branch_grad = lax.optimization_barrier((feed_partial, branch_grad))
    feed_first = links.scatter_first(feed_partial)
    attended_grad = matmul(branch_grad, wide_output).astype(jnp.bfloat16)
    raw_grad, query_gain_term, key_gain_term = attention.backward(
        place,
        raw_rows,
        cosine,
        sine,
        query_gain,
        key_gain,
        query_rows,
        key_rows,
        value_rows,
        log_totals,
        attended_grad,
    )
    raw_grad, feed_first, branch_grad = lax.optimization_barrier(
        (raw_grad, feed_first, branch_grad)
    )
    output_term = weight_term(links.both_columns(branch_grad), links.both_cores(attended_rows))
    attention_term = weight_term(links.both_columns(normed_rows), links.both_cores(raw_grad))
    feed_first, attention_term = lax.optimization_barrier((feed_first, attention_term))
    feed_last = links.scatter_last(feed_partial, feed_first)
    raw_grad, attention_term = lax.optimization_barrier((raw_grad, attention_term))
    input_partial = contract_last(raw_grad, wide_attention).astype(jnp.bfloat16)
    mixing_term = jnp.concatenate([attention_term, output_term], axis=1)
    input_gain_term = (
        jnp.sum(input_partial.astype(jnp.float32) * normed_rows.astype(jnp.float32), axis=0)
        / input_gain
    )
    terms = jnp.concatenate(
        [input_gain_term, middle_gain_term, query_gain_term[0], key_gain_term[0]]
    )
    mixing_term, feed_sum, feed_last, input_partial, terms = lax.optimization_barrier(
        (mixing_term, feed_sum, feed_last, input_partial, terms)
    )
    mixing_sum = links.scatter_chips(mixing_term)
    input_normed_grad, terms = links.scatter_beside(input_partial, terms)
    layer_output = middle + links.scatter_end(feed_partial, feed_first, feed_last)
    tokens_grad = middle_grad + norm_backward(input_normed_grad, scaled_in, inverse_in, input_gain)
    terms = links.total_dp(terms)
    width = tokens.shape[1]
    feed_sum = feed_sum.astype(jnp.float32)
    query_sum, key_sum, value_sum, output_sum = split_columns(
        mixing_sum, (query_width, key_width, key_width, query_width)
    )
    return (
        layer_output,
        tokens_grad,
        terms[:width],
        terms[width : 2 * width],
        terms[2 * width : 2 * width + head_size],
        terms[2 * width + head_size :],
        query_sum,
        key_sum,
        value_sum,
        output_sum,
        feed_sum[:, :hidden],
        feed_sum[:, hidden:],
        down_sum.astype(jnp.float32),
    )


def solution(mesh):
    links = Links(mesh.shape["dp"], mesh.shape["tensor"])
    placed = (
        P(("dp", "tensor"), None),
        P("dp"),
        P(),
        P(),
        P(),
        P(),
        P("dp", "tensor"),
        P("dp", "tensor"),
        P("dp", "tensor"),
        P("dp", "tensor"),
        P("dp", "tensor"),
        P("dp", "tensor"),
        P("dp", "tensor"),
        P(("dp", "tensor"), None),
    )
    return jax.shard_map(
        lambda *arrays: shards(links, *arrays),
        mesh=mesh,
        in_specs=placed,
        out_specs=(
            P(("dp", "tensor"), None),
            P(("dp", "tensor"), None),
            P(),
            P(),
            P(),
            P(),
            P("dp", "tensor"),
            P("dp", "tensor"),
            P("dp", "tensor"),
            P("dp", "tensor"),
            P("dp", "tensor"),
            P("dp", "tensor"),
            P("dp", "tensor"),
        ),
        check_vma=False,
    )
```
